128 devices in a mesh: lon: 8 (over x_hi, y), lat: 8 (over z, core), batch: 2 (over x_lo).
Axes of the slice: x: 4 (x_hi: 2, x_lo: 2; x = x_hi * 2 + x_lo), y: 4, z: 4, core: 2. Of those that a mesh axis runs over, the one named last changes fastest.
Arguments:
- state: bfloat16 [2, 21, 256, 4096], P('batch', None, 'lat', 'lon'), may hold values from -6 to 6
- forcing: bfloat16 [2, 96, 256, 4096], P('batch', None, 'lat', 'lon'), may hold values from -6 to 6
- land_mask: int32 [256, 4096], P('lat', 'lon'), may hold values 0 or 1
- partner: int32 [4096], P('lon'), may hold values from 0 to 4095, as said below
- cotangent: bfloat16 [2, 512, 128, 2048], P('batch', None, 'lat', 'lon'), may hold values from -6 to 6
- weight_state: bfloat16 [512, 336], replicated, may hold values from -0.125 to 0.125
- weight_force: bfloat16 [512, 1536], replicated, may hold values from -0.125 to 0.125
Outputs:
- grad_state: bfloat16 [2, 21, 256, 4096], P('batch', None, 'lat', 'lon')
- grad_forcing: bfloat16 [2, 96, 256, 4096], P('batch', None, 'lat', 'lon')
- grad_wstate: float32 [512, 336], P(('lat', 'batch'))
- grad_wforce: float32 [512, 1536], P(('lat', 'batch'))
The draws below stay inside these ranges and needn't reach their ends.
Inputs may be any that keep to these rules, and one draw needn't show every extreme that they name: partner is an involution that maps the columns of the k-th block of 512 columns onto the columns of the block k-th from the other end, in an order drawn for each pair of blocks.
All inputs are finite; a program needn't handle non-finite values. No bound on the sum of `land_mask` on one device may be relied on, other than what follows from the above.
Results may differ from the reference program's by a relative error of at most 0.0011.
Values may be sent and summed in bfloat16 or wider, within the bound.
A program may use at most 256 MiB of HBM per device.

```python
import math
import jax
import jax.numpy as jnp

SC = 21
FC = 96
WIDTH = 512
CLO = 512
SAMPLES = 2
NLAT = 256
NLON = 4096


def draw_partner(key, part):
    block_count = NLON // CLO
    pieces = [None] * block_count
    for block in range(block_count // 2):
        order = jax.random.permutation(jax.random.fold_in(key, 7919 + block), CLO).astype(jnp.int32)
        inverse = jnp.argsort(order, stable=True).astype(jnp.int32)
        mirror = block_count - 1 - block
        pieces[block] = mirror * CLO + order
        pieces[mirror] = block * CLO + inverse
    return jnp.concatenate(pieces, axis=0).astype(jnp.int32)


def set_ends(drawn, rng, least, high):
    longest = drawn.shape.index(max(drawn.shape))
    spots = []
    for shift in (0, 1):
        where = [jax.random.randint(jax.random.fold_in(rng, axis), (), 0, length) for axis, length in enumerate(drawn.shape)]
        where[longest] = (where[longest] + shift) % drawn.shape[longest]
        spots.append(tuple(where))
    return drawn.at[spots[0]].set(least).at[spots[1]].set(high)


def raised(entries, key, source, target, blocks, factor):
    def block_of(axis_at):
        return (jnp.arange(entries.shape[axis_at]) // (entries.shape[axis_at] // blocks)).reshape((-1,) + (1,) * (entries.ndim - 1 - axis_at))

    one_side = jax.random.permutation(key, blocks)[block_of(target)]
    second = (block_of(target) + blocks // 2) % blocks
    return jnp.where((block_of(source) == one_side) | (block_of(source) == second), factor * entries, entries)


def level_of(key, extent, cuts, smallest, high):
    def one(dim, blocks):
        draws = jax.random.uniform(jax.random.fold_in(jax.random.fold_in(key, 6), dim), (blocks,), jnp.float32, smallest / len(cuts), high / len(cuts))
        return jnp.repeat(jnp.exp(draws), extent[dim] // blocks).reshape((-1,) + (1,) * (len(extent) - dim - 1))

    gain = one(*cuts[0])
    for cut in cuts[1:]:
        gain = gain * one(*cut)
    return gain


def normal_values(key, extent, width, bound, cuts=(), kind=jnp.bfloat16):
    gain = level_of(key, extent, cuts, -0.22, 0.18) if cuts else 1.0
    drawn = jax.random.normal(key, extent, jnp.float32) * width * gain
    return jnp.minimum(jnp.maximum(drawn, -bound), bound).astype(kind)


def heavy_noise(key, shape, width, limit, split, heavy, dtype=jnp.bfloat16):
    values = width * jax.random.normal(key, shape, jnp.float32)
    if split:
        values = values * level_of(key, shape, split, -0.22, 0.18)
    return jnp.clip(raised(values, jax.random.fold_in(key, 3), *heavy), -limit, limit).astype(dtype)


def setup_inputs(seed: int = 0) -> dict:
    keys = jax.random.split(jax.random.key(seed), 8)
    state = normal_values(keys[0], (SAMPLES, SC, NLAT, NLON), 1.0, 6.0, ((0, 2), (2, 8), (3, 8)))
    forcing = normal_values(keys[1], (SAMPLES, FC, NLAT, NLON), 1.0, 6.0, ((0, 2), (2, 8), (3, 8)))
    land_mask = set_ends((jax.random.randint(keys[2], (NLAT, NLON), 0, 5) < 4).astype(jnp.int32), jax.random.fold_in(keys[2], 1), 0, 1)
    partner = draw_partner(jax.random.fold_in(keys[7], 71), 0)
    cotangent = heavy_noise(keys[4], (SAMPLES, WIDTH, NLAT // 2, NLON // 2), 1.0, 6.0, ((0, 2), (2, 8), (3, 8)), (2, 1, 8, 2.0))
    weight_state = normal_values(keys[5], (WIDTH, SC * 16), ((SC + FC) * 16) ** -0.5, 0.125)
    weight_force = normal_values(keys[6], (WIDTH, FC * 16), ((SC + FC) * 16) ** -0.5, 0.125)
    return dict(state=state, forcing=forcing, land_mask=land_mask, partner=partner, cotangent=cotangent, weight_state=weight_state, weight_force=weight_force)


def reference(state, forcing, land_mask, partner, cotangent, weight_state, weight_force):
    channels = SC + FC
    weights = jnp.concatenate([weight_state, weight_force], axis=1).astype(jnp.float32)
    weights = weights.reshape(WIDTH, channels, 4, 4)
    mask_float = land_mask.astype(jnp.float32)
    kernel_sum = jnp.zeros((WIDTH, channels, 4, 4), jnp.float32)
    state_list = []
    force_list = []
    for sample in range(SAMPLES):
        masked = jnp.concatenate([state[sample], forcing[sample]], axis=0).astype(jnp.float32) * mask_float
        fold_row = masked[:, NLAT - 1, :][:, partner]
        row_ext = jnp.concatenate([jnp.zeros((channels, 1, NLON), jnp.float32), masked, fold_row[:, None, :]], axis=1)
        padded = jnp.concatenate([row_ext[:, :, -1:], row_ext, row_ext[:, :, :1]], axis=2)
        cot_field = cotangent[sample].astype(jnp.float32)
        pad_grad = jnp.zeros((channels, NLAT + 2, NLON + 2), jnp.float32)
        for row_off in range(4):
            for col_off in range(4):
                window = padded[:, row_off:row_off + NLAT:2, col_off:col_off + NLON:2]
                kernel_sum = kernel_sum.at[:, :, row_off, col_off].add(jnp.einsum('wab,cab->wc', cot_field, window))
                spread = jnp.einsum('wc,wab->cab', weights[:, :, row_off, col_off], cot_field)
                pad_grad = pad_grad.at[:, row_off:row_off + NLAT:2, col_off:col_off + NLON:2].add(spread)
        col_fold = pad_grad[:, :, 1:NLON + 1]
        col_fold = col_fold.at[:, :, NLON - 1].add(pad_grad[:, :, 0])
        col_fold = col_fold.at[:, :, 0].add(pad_grad[:, :, NLON + 1])
        cell_grad = col_fold[:, 1:NLAT + 1, :]
        cell_grad = cell_grad.at[:, NLAT - 1, partner].add(col_fold[:, NLAT + 1, :])
        result = (cell_grad * mask_float).astype(jnp.bfloat16)
        state_list.append(result[:SC])
        force_list.append(result[SC:])
    scale = 1.0 / math.sqrt(SAMPLES * (NLAT // 2) * (NLON // 2))
    kernel_grad = (kernel_sum * scale).reshape(WIDTH, channels * 16)
    return (jnp.stack(state_list, axis=0), jnp.stack(force_list, axis=0), kernel_grad[:, :SC * 16], kernel_grad[:, SC * 16:])
```

```python
import functools
import math

import jax
import jax.numpy as jnp
from jax import lax
from jax.experimental import pallas as pl
from jax.experimental.pallas import tpu as pltpu
from jax.sharding import PartitionSpec as P

SC = 21
CP = 128
F0 = 24
F32 = jnp.float32
BF16 = jnp.bfloat16
JORD = (1, 2, 0, 3)
ROWS = ((1, 0, 0), (2, 1, 1), (0, 1, 0), (3, 0, 1))


def iota(shape, dim):
    return lax.broadcasted_iota(jnp.int32, shape, dim)


def dot(a, b):
    return lax.dot_general(a, b, (((1,), (0,)), ((), ())), preferred_element_type=F32)


def dot_nt(a, b):
    return lax.dot_general(a, b, (((1,), (1,)), ((), ())), preferred_element_type=F32)


def put(buf, at, value):
    for t in range(value.shape[1] // 128):
        buf[t, at, :] = value[:, t * 128:(t + 1) * 128]


def get(buf, at):
    return jnp.concatenate([buf[t, at, :] for t in range(buf.shape[0])], axis=1)


def main_kernel(
    state, force, mask, local_col, cot, wst, wf,
    g_out, xs_out, xf_out,
    raw, sbuf, planes, craw, cf32, cot_a, cot_b, wcat, gbuf, wstage, wspad, perm, permt, fold_sel,
    rxs, rxn, rmir, rcs, rcn, sx, rxw, rxe, sc, rcw, rce, sfold, rfold,
    in_sem, out_sem, send, recv,
):
    lon_n = lax.axis_size("lon")
    lat_n = lax.axis_size("lat")
    lon = lax.axis_index("lon")
    lat = lax.axis_index("lat")
    at_top = lat == lat_n - 1
    at_bottom = lat == 0
    north = {"lat": lax.rem(lat + 1, lat_n)}
    south = {"lat": lax.rem(lat + lat_n - 1, lat_n)}
    east = {"lon": lax.rem(lon + 1, lon_n)}
    west = {"lon": lax.rem(lon + lon_n - 1, lon_n)}
    mirror = {"lon": lon_n - 1 - lon}

    cuts = [(state, 0, 0, SC * 32)]
    for k in range(6):
        cuts.append((force, k * 512, F0 * 32 + k * 512, 512))
    loads = []
    for n, (src, at, to, rows) in enumerate(cuts):
        loads.append(pltpu.make_async_copy(src.at[pl.ds(at, rows)], raw.at[pl.ds(to, rows)], in_sem.at[n]))
    loads.append(pltpu.make_async_copy(cot, craw, in_sem.at[7]))
    loads.append(pltpu.make_async_copy(wst, wspad.at[pl.ds(0, 336)], in_sem.at[8]))
    loads.append(pltpu.make_async_copy(wf, wstage, in_sem.at[9]))
    for copy in loads:
        copy.start()

    barrier = pltpu.get_barrier_semaphore()
    for peer in (north, south, east, west, mirror):
        pl.semaphore_signal(barrier, inc=1, device_id=peer, device_id_type=pl.DeviceIdType.MESH)
    pl.semaphore_wait(barrier, 5)

    def remote(n, src, dst, peer):
        return pltpu.make_async_remote_copy(
            src_ref=src, dst_ref=dst, send_sem=send.at[n], recv_sem=recv.at[n],
            device_id=peer, device_id_type=pl.DeviceIdType.MESH,
        )

    row5, col5 = iota((512, 512), 0), iota((512, 512), 1)
    deint = jnp.where(lax.rem(row5, 2) * 256 + lax.div(row5, 2) == col5, 1.0, 0.0).astype(BF16)
    perm[...] = deint
    permt[...] = jnp.where(lax.rem(col5, 2) * 256 + lax.div(col5, 2) == row5, 1.0, 0.0).astype(BF16)

    put(sbuf, pl.ds(SC * 32, 3 * 32), jnp.zeros((96, 512), F32))
    put(sbuf, pl.ds(120 * 32, 8 * 32), jnp.zeros((256, 512), F32))
    mask_bf = mask[...].astype(F32).astype(BF16)
    for n, (_, _, to, rows) in enumerate(cuts):
        loads[n].wait()
        x = raw[pl.ds(to, rows), :].reshape(rows // 32, 32, 512) * mask_bf[None]
        put(sbuf, pl.ds(to, rows), dot(x.reshape(rows, 512), perm[...]))

    lane128 = iota((CP, 128), 1)
    lane256 = iota((CP, 256), 1)

    def four(even, odd):
        left = jnp.where(lane256 == 0, 0.0, pltpu.roll(odd, 1, 1))
        right = jnp.where(lane256 == 255, 0.0, pltpu.roll(even, 255, 1))
        return even, odd, left, right

    def put_row(parity, slot, even, odd):
        at = pl.multiple_of(slot * 256, 256)
        for j, part in enumerate(four(even, odd)):
            planes[pl.ds((parity * 4 + j) * CP, CP), pl.ds(at, 256)] = part.astype(BF16)

    def edge_of(acc, r, even, odd):
        acc = jnp.where(lane128 == r + 1, even[:, 0:1], acc)
        return jnp.where(lane128 == 65 + r, odd[:, 255:256], acc)

    def split_rows(a, acc):
        for parity in range(2):
            r = 2 * a + parity
            x = get(sbuf, pl.ds(r, CP, stride=32))
            even, odd = x[:, :256], x[:, 256:]
            put_row(parity, a + parity, even, odd)
            acc = edge_of(acc, r, even, odd)
        return acc

    edges = lax.fori_loop(0, 16, split_rows, jnp.zeros((CP, 128), F32))

    x_north = remote(0, planes.at[pl.ds(512, 512), pl.ds(16 * 256, 256)], rxs, north)
    x_south = remote(1, planes.at[pl.ds(0, 512), pl.ds(0, 256)], rxn, south)
    x_mirror = remote(2, planes.at[pl.ds(512, 256), pl.ds(16 * 256, 256)], rmir, mirror)
    x_north.start()
    x_south.start()

    @pl.when(at_top)
    def _():
        x_mirror.start()

    loads[7].wait()

    def widen(k, _):
        at = pl.multiple_of(k * 512, 512)
        put(cf32, pl.ds(at, 512), craw[pl.ds(at, 512), :].astype(F32))
        return 0

    lax.fori_loop(0, 16, widen, 0)
    clane = iota((512, 128), 1)

    def split_tokens(a, acc):
        x = get(cf32, pl.ds(a, 512, stride=16))
        xb = x.astype(BF16)
        cot_a[:, pl.ds(pl.multiple_of(a * 256, 256), 256)] = xb
        cot_b[pl.ds(pl.multiple_of((a + 1) * 512, 512), 512), :] = xb
        acc = jnp.where(clane == a + 1, x[:, 0:1], acc)
        return jnp.where(clane == 65 + a, x[:, 255:256], acc)

    cedges = lax.fori_loop(0, 16, split_tokens, jnp.zeros((512, 128), F32))
    sc[...] = cedges.astype(BF16)
    c_north = remote(3, cot_b.at[pl.ds(16 * 512, 512)], rcs, north)
    c_south = remote(4, cot_b.at[pl.ds(512, 512)], rcn, south)
    c_north.start()
    c_south.start()

    def tile(n, pair):
        _, parity, off = ROWS[n]
        rows = planes[pl.ds((parity * 4 + pair * 2) * CP, 2 * CP), pl.ds(off * 256, 4096)]
        return dot_nt(cot_a[...], rows)

    gbuf[0] = tile(0, 0)
    gbuf[1] = tile(1, 0)

    natural = jnp.where(row5 == local_col[...], 1.0, 0.0).astype(BF16)
    half = dot(natural, perm[...]).astype(BF16)
    fold_sel[...] = dot(permt[...], half).astype(BF16)

    x_north.wait()
    x_south.wait()
    zero16 = jnp.zeros((), BF16)
    planes[pl.ds(512, 512), pl.ds(0, 256)] = jnp.where(at_bottom, zero16, rxs[...])
    planes[pl.ds(0, 512), pl.ds(16 * 256, 256)] = rxn[...]

    @pl.when(at_top)
    def _():
        x_mirror.wait()
        top = jnp.concatenate([rmir[pl.ds(0, CP), :], rmir[pl.ds(CP, CP), :]], axis=1)
        folded = dot(top, fold_sel[...])
        put_row(0, 16, folded[:, :256], folded[:, 256:])

    acc = edges
    low_e = planes[pl.ds(512, CP), pl.ds(0, 128)].astype(F32)
    low_o = planes[pl.ds(512 + CP, CP), pl.ds(128, 128)].astype(F32)
    high_e = planes[pl.ds(0, CP), pl.ds(16 * 256, 128)].astype(F32)
    high_o = planes[pl.ds(CP, CP), pl.ds(16 * 256 + 128, 128)].astype(F32)
    acc = jnp.where(lane128 == 0, low_e[:, 0:1], acc)
    acc = jnp.where(lane128 == 64, low_o[:, 127:128], acc)
    acc = jnp.where(lane128 == 33, high_e[:, 0:1], acc)
    acc = jnp.where(lane128 == 97, high_o[:, 127:128], acc)
    sx[...] = acc.astype(BF16)
    x_east = remote(5, sx, rxw, east)
    x_west = remote(6, sx, rxe, west)
    x_east.start()
    x_west.start()

    c_north.wait()
    c_south.wait()
    cot_b[pl.ds(0, 512), :] = jnp.where(at_bottom, zero16, rcs[...])
    cot_b[pl.ds(17 * 512, 512), :] = jnp.where(at_top, zero16, rcn[...])
    low = cot_b[pl.ds(0, 512), :].astype(F32)
    high = cot_b[pl.ds(17 * 512, 512), :].astype(F32)
    acc = sc[...].astype(F32)
    acc = jnp.where(clane == 0, low[:, 0:1], acc)
    acc = jnp.where(clane == 64, low[:, 255:256], acc)
    acc = jnp.where(clane == 17, high[:, 0:1], acc)
    acc = jnp.where(clane == 81, high[:, 255:256], acc)
    sc[...] = acc.astype(BF16)
    c_east = remote(7, sc, rcw, east)
    c_west = remote(8, sc, rce, west)
    c_east.start()
    c_west.start()

    gbuf[2] = tile(2, 0)
    gbuf[3] = tile(3, 0)
    x_east.wait()
    x_west.wait()
    side = jnp.concatenate(
        [jnp.where(lane128 >= 64, rxw[...], zero16), jnp.where(lane128 < 64, rxe[...], zero16)], axis=0
    )
    lrow, lcol = iota((128, 128), 0), iota((128, 128), 1)
    for n in range(4):
        i = ROWS[n][0]
        first = (lrow >= 1) & (lrow <= 16) & (lcol == 62 + 2 * lrow + i)
        last = (lrow >= 65) & (lrow <= 80) & (lcol == 2 * lrow - 130 + i)
        spread = jnp.where(first | last, 1.0, 0.0).astype(BF16)
        moved = dot(sc[...], spread).astype(BF16)
        gbuf[4 + n] = tile(n, 1) + dot_nt(moved, side)
    g_copy = pltpu.make_async_copy(gbuf, g_out, out_sem.at[8])
    g_copy.start()

    loads[8].wait()
    loads[9].wait()
    wspad[pl.ds(336, 48), :] = jnp.zeros((48, 512), BF16)
    pick = jnp.where(lax.rem(lrow, 8) * 16 + lax.div(lrow, 8) == lcol, 1.0, 0.0).astype(BF16)
    for o in range(16):
        put(sbuf, pl.ds(o * CP + 120, 8), jnp.zeros((8, 512), F32))
    for kb in range(15):
        if kb < 3:
            got = dot(pick, wspad[pl.ds(kb * 128, 128), :])
        else:
            got = dot_nt(pick, wstage[:, pl.ds((kb - 3) * 128, 128)])
        for o in range(16):
            put(sbuf, pl.ds(o * CP + kb * 8, 8), got[o * 8:o * 8 + 8, :])
    for parity in range(2):
        for j in range(4):
            for k, i in enumerate(((3, 1), (2, 0))[parity]):
                wcat[pl.ds((parity * 4 + j) * CP, CP), pl.ds(k * 512, 512)] = get(
                    sbuf, pl.ds((i * 4 + JORD[j]) * CP, CP)
                ).astype(BF16)

    c_east.wait()
    c_west.wait()
    z_west, z_east = [], []
    for parity in range(2):
        for j, src, out in ((3, rcw, z_west), (2, rce, z_east)):
            w_rows = wcat[pl.ds((parity * 4 + j) * CP, CP), :]
            first = dot(w_rows[:, :512], src[...])
            second = dot(w_rows[:, 512:], src[...])
            out.append(first + pltpu.roll(second, 127, 1))

    def token_row(s, parity):
        tokens = cot_b[pl.ds(pl.multiple_of(s * 512, 512), 1024), :]
        u = dot(wcat[pl.ds(parity * 512, 512), :], tokens)
        u1, u2, u0, u3 = (u[k * CP:(k + 1) * CP] for k in range(4))
        zw = pltpu.roll(z_west[parity], 64 - s, 1)
        ze = pltpu.roll(z_east[parity], 127 - s, 1)
        r3 = pltpu.roll(u3, 1, 1)
        r0 = pltpu.roll(u0, 255, 1)
        r3 = jnp.concatenate([jnp.where(lane128 == 0, zw, r3[:, :128]), r3[:, 128:]], axis=1)
        r0 = jnp.concatenate([r0[:, :128], jnp.where(lane128 == 127, ze, r0[:, 128:])], axis=1)
        return jnp.concatenate([u1 + r3, u2 + r0], axis=1)

    sfold[...] = token_row(16, 0).astype(BF16)
    g_mirror = remote(9, sfold, rfold, mirror)

    @pl.when(at_top)
    def _():
        g_mirror.start()

    put(sbuf, pl.ds(31, CP, stride=32), token_row(16, 1))
    put(sbuf, pl.ds(0, CP, stride=32), token_row(0, 0))

    def rows_of(s, _):
        put(sbuf, pl.ds(2 * s, CP, stride=32), token_row(s, 0))
        put(sbuf, pl.ds(2 * s - 1, CP, stride=32), token_row(s, 1))
        return 0

    lax.fori_loop(1, 16, rows_of, 0)

    @pl.when(at_top)
    def _():
        g_mirror.wait()
        at = pl.ds(31, CP, stride=32)
        put(sbuf, at, get(sbuf, at) + dot(rfold[...], fold_sel[...]))

    stores = []
    outs = [(xs_out, 0, 0, SC * 32)]
    for k in range(6):
        outs.append((xf_out, k * 512, F0 * 32 + k * 512, 512))
    for n, (dst, at, to, rows) in enumerate(outs):
        cells = dot(get(sbuf, pl.ds(to, rows)).astype(BF16), permt[...]).astype(BF16)
        cells = cells.reshape(rows // 32, 32, 512) * mask_bf[None]
        raw[pl.ds(to, rows), :] = cells.reshape(rows, 512)
        copy = pltpu.make_async_copy(raw.at[pl.ds(to, rows)], dst.at[pl.ds(at, rows)], out_sem.at[n])
        copy.start()
        stores.append(copy)
    for copy in stores:
        copy.wait()
    g_copy.wait()


def on_device(state, forcing, land_mask, partner, cotangent, weight_state, weight_force):
    sc, fc = state.shape[1], forcing.shape[1]
    rows, cols = state.shape[2:]
    width = cotangent.shape[1]
    lon_n, lat_n, batch_n = (lax.axis_size(a) for a in ("lon", "lat", "batch"))
    local_col = (partner - (lon_n - 1 - lax.axis_index("lon")) * cols)[None, :]
    any_spec = pl.BlockSpec(memory_space=pl.ANY)
    vmem = pl.BlockSpec(memory_space=pltpu.VMEM)
    g, xs, xf = pl.pallas_call(
        main_kernel,
        out_shape=(
            jax.ShapeDtypeStruct((8, width, 256), F32),
            jax.ShapeDtypeStruct((sc * rows, cols), BF16),
            jax.ShapeDtypeStruct((fc * rows, cols), BF16),
        ),
        in_specs=[any_spec, any_spec, vmem, vmem, any_spec, any_spec, any_spec],
        out_specs=(any_spec, any_spec, any_spec),
        scratch_shapes=[
            pltpu.VMEM((4096, 512), BF16),
            pltpu.VMEM((4, 4096, 128), F32),
            pltpu.VMEM((8 * CP, 17 * 256), BF16),
            pltpu.VMEM((8192, 256), BF16),
            pltpu.VMEM((2, 8192, 128), F32),
            pltpu.VMEM((512, 4096), BF16),
            pltpu.VMEM((18 * 512, 256), BF16),
            pltpu.VMEM((1024, 1024), BF16),
            pltpu.VMEM((8, 512, 256), F32),
            pltpu.VMEM((512, 1536), BF16),
            pltpu.VMEM((384, 512), BF16),
            pltpu.VMEM((512, 512), BF16),
            pltpu.VMEM((512, 512), BF16),
            pltpu.VMEM((512, 512), BF16),
            pltpu.VMEM((512, 256), BF16),
            pltpu.VMEM((512, 256), BF16),
            pltpu.VMEM((256, 256), BF16),
            pltpu.VMEM((512, 256), BF16),
            pltpu.VMEM((512, 256), BF16),
            pltpu.VMEM((CP, 128), BF16),
            pltpu.VMEM((CP, 128), BF16),
            pltpu.VMEM((CP, 128), BF16),
            pltpu.VMEM((512, 128), BF16),
            pltpu.VMEM((512, 128), BF16),
            pltpu.VMEM((512, 128), BF16),
            pltpu.VMEM((CP, 512), BF16),
            pltpu.VMEM((CP, 512), BF16),
            pltpu.SemaphoreType.DMA((10,)),
            pltpu.SemaphoreType.DMA((9,)),
            pltpu.SemaphoreType.DMA((10,)),
            pltpu.SemaphoreType.DMA((10,)),
        ],
        compiler_params=pltpu.CompilerParams(
            collective_id=0, has_side_effects=True, vmem_limit_bytes=62 * 1024 * 1024
        ),
        name="encoder_backward",
    )(
        state.reshape(sc * rows, cols), forcing.reshape(fc * rows, cols), land_mask, local_col,
        cotangent.reshape(width * cotangent.shape[2], cotangent.shape[3]), weight_state.T, weight_force,
    )
    scale = 1.0 / math.sqrt(batch_n * (rows // 2) * lat_n * (cols // 2) * lon_n)
    share = lax.psum_scatter(g, ("lat", "batch"), scatter_dimension=1, tiled=True)
    share = lax.psum(share, "lon") * scale
    own = share.shape[1]
    share = share.reshape(2, 4, own, 2, CP)
    offsets = []
    for i in range(4):
        n = [r[0] for r in ROWS].index(i)
        for j in range(4):
            k = JORD.index(j)
            offsets.append(share[k // 2, n, :, k % 2, :])
    kernel = jnp.stack(offsets, axis=-1)
    return (
        xs.reshape(state.shape),
        xf.reshape(forcing.shape),
        kernel[:, :sc].reshape(own, sc * 16),
        kernel[:, F0:F0 + fc].reshape(own, fc * 16),
    )


def solution(mesh):
    in_specs = (
        P("batch", None, "lat", "lon"),
        P("batch", None, "lat", "lon"),
        P("lat", "lon"),
        P("lon"),
        P("batch", None, "lat", "lon"),
        P(),
        P(),
    )
    out_specs = (
        P("batch", None, "lat", "lon"),
        P("batch", None, "lat", "lon"),
        P(("lat", "batch"), None),
        P(("lat", "batch"), None),
    )
    return jax.shard_map(on_device, mesh=mesh, in_specs=in_specs, out_specs=out_specs, check_vma=False)
```

```python
import functools
import math

import jax
import jax.numpy as jnp
from jax import lax
from jax.experimental import pallas as pl
from jax.experimental.pallas import tpu as pltpu
from jax.sharding import PartitionSpec as P

SC = 21
CP = 128
F0 = 24
F32 = jnp.float32
BF16 = jnp.bfloat16
JORD = (1, 2, 0, 3)
ROWS = ((1, 0, 0), (2, 1, 1), (0, 1, 0), (3, 0, 1))


def iota(shape, dim):
    return lax.broadcasted_iota(jnp.int32, shape, dim)


def dot(a, b):
    return lax.dot_general(a, b, (((1,), (0,)), ((), ())), preferred_element_type=F32)


def dot_nt(a, b):
    return lax.dot_general(a, b, (((1,), (1,)), ((), ())), preferred_element_type=F32)


def put(buf, at, value):
    for t in range(value.shape[1] // 128):
        buf[t, at, :] = value[:, t * 128:(t + 1) * 128]


def get(buf, at):
    return jnp.concatenate([buf[t, at, :] for t in range(buf.shape[0])], axis=1)


def main_kernel(
    state, force, mask, local_col, cot, wst, wf,
    ks_out, kf_out, xs_out, xf_out,
    raw, sbuf, planes, craw, cf32, cot_a, cot_b, wcat, gbuf, wstage, wspad, perm, permt, fold_sel,
    rxs, rxn, rmir, rcs, rcn, sx, rxw, rxe, sc, rcw, rce, sfold, rfold,
    rcore, ra_z, ra_x, ra_y, s2_z, s2_x, s2_y, rb_z, rb_x, rb_y, s3_z, s3_x, s3_y, rc_z, rc_x, rc_y, s4, gathered, tbuf,
    in_sem, out_sem, send, recv, core_s, core_r, a_s, a_r, b_s, b_r, c_s, c_r, g_s, g_r,
):
    lon_n = lax.axis_size("lon")
    lat_n = lax.axis_size("lat")
    lon = lax.axis_index("lon")
    lat = lax.axis_index("lat")
    at_top = lat == lat_n - 1
    at_bottom = lat == 0
    north = {"lat": lax.rem(lat + 1, lat_n)}
    south = {"lat": lax.rem(lat + lat_n - 1, lat_n)}
    east = {"lon": lax.rem(lon + 1, lon_n)}
    west = {"lon": lax.rem(lon + lon_n - 1, lon_n)}
    mirror = {"lon": lon_n - 1 - lon}
    at_y, at_z, core = lax.rem(lon, 4), lax.div(lat, 2), lax.rem(lat, 2)
    x_lo, x_hi = lax.axis_index("batch"), lax.div(lon, 4)
    spot = {"x": 2 * x_hi + x_lo, "y": at_y, "z": at_z}
    other_core = {"lat": 2 * at_z + 1 - core}

    def peer_on(axis, place):
        if axis == "z":
            return {"lat": 2 * place + core}
        if axis == "y":
            return {"lon": 4 * x_hi + place}
        return {"lon": 4 * lax.div(place, 2) + at_y, "batch": lax.rem(place, 2)}

    def lon_peer(d):
        return {"lon": lax.rem(lon + d, lon_n)}

    peers = [north, south, mirror, other_core] + [lon_peer(d) for d in range(1, 8)]
    for axis in "xyz":
        peers += [peer_on(axis, lax.rem(spot[axis] + d, 4)) for d in range(1, 4)]

    cuts = [(state, 0, 0, SC * 32)]
    for k in range(6):
        cuts.append((force, k * 512, F0 * 32 + k * 512, 512))
    loads = []
    for n, (src, at, to, rows) in enumerate(cuts):
        loads.append(pltpu.make_async_copy(src.at[pl.ds(at, rows)], raw.at[pl.ds(to, rows)], in_sem.at[n]))
    loads.append(pltpu.make_async_copy(cot, craw, in_sem.at[7]))
    loads.append(pltpu.make_async_copy(wst, wspad.at[pl.ds(0, 336)], in_sem.at[8]))
    loads.append(pltpu.make_async_copy(wf, wstage, in_sem.at[9]))
    for copy in loads:
        copy.start()

    barrier = pltpu.get_barrier_semaphore()
    for peer in peers:
        pl.semaphore_signal(barrier, inc=1, device_id=peer, device_id_type=pl.DeviceIdType.MESH)
    pl.semaphore_wait(barrier, len(peers))

    def remote(n, src, dst, peer):
        return pltpu.make_async_remote_copy(
            src_ref=src, dst_ref=dst, send_sem=send.at[n], recv_sem=recv.at[n],
            device_id=peer, device_id_type=pl.DeviceIdType.MESH,
        )

    row5, col5 = iota((512, 512), 0), iota((512, 512), 1)
    deint = jnp.where(lax.rem(row5, 2) * 256 + lax.div(row5, 2) == col5, 1.0, 0.0).astype(BF16)
    perm[...] = deint
    permt[...] = jnp.where(lax.rem(col5, 2) * 256 + lax.div(col5, 2) == row5, 1.0, 0.0).astype(BF16)

    put(sbuf, pl.ds(SC * 32, 3 * 32), jnp.zeros((96, 512), F32))
    put(sbuf, pl.ds(120 * 32, 8 * 32), jnp.zeros((256, 512), F32))
    mask_bf = mask[...].astype(F32).astype(BF16)
    for n, (_, _, to, rows) in enumerate(cuts):
        loads[n].wait()
        x = raw[pl.ds(to, rows), :].reshape(rows // 32, 32, 512) * mask_bf[None]
        put(sbuf, pl.ds(to, rows), dot(x.reshape(rows, 512), perm[...]))

    lane128 = iota((CP, 128), 1)
    lane256 = iota((CP, 256), 1)

    def four(even, odd):
        left = jnp.where(lane256 == 0, 0.0, pltpu.roll(odd, 1, 1))
        right = jnp.where(lane256 == 255, 0.0, pltpu.roll(even, 255, 1))
        return even, odd, left, right

    def put_row(parity, slot, even, odd):
        at = pl.multiple_of(slot * 256, 256)
        for j, part in enumerate(four(even, odd)):
            planes[pl.ds((parity * 4 + j) * CP, CP), pl.ds(at, 256)] = part.astype(BF16)

    def edge_of(acc, r, even, odd):
        acc = jnp.where(lane128 == r + 1, even[:, 0:1], acc)
        return jnp.where(lane128 == 65 + r, odd[:, 255:256], acc)

    def split_rows(a, acc):
        for parity in range(2):
            r = 2 * a + parity
            x = get(sbuf, pl.ds(r, CP, stride=32))
            even, odd = x[:, :256], x[:, 256:]
            put_row(parity, a + parity, even, odd)
            acc = edge_of(acc, r, even, odd)
        return acc

    edges = lax.fori_loop(0, 16, split_rows, jnp.zeros((CP, 128), F32))

    x_north = remote(0, planes.at[pl.ds(512, 512), pl.ds(16 * 256, 256)], rxs, north)
    x_south = remote(1, planes.at[pl.ds(0, 512), pl.ds(0, 256)], rxn, south)
    x_mirror = remote(2, planes.at[pl.ds(512, 256), pl.ds(16 * 256, 256)], rmir, mirror)
    x_north.start()
    x_south.start()

    @pl.when(at_top)
    def _():
        x_mirror.start()

    loads[7].wait()

    def widen(k, _):
        at = pl.multiple_of(k * 512, 512)
        put(cf32, pl.ds(at, 512), craw[pl.ds(at, 512), :].astype(F32))
        return 0

    lax.fori_loop(0, 16, widen, 0)
    clane = iota((512, 128), 1)

    def split_tokens(a, acc):
        x = get(cf32, pl.ds(a, 512, stride=16))
        xb = x.astype(BF16)
        cot_a[:, pl.ds(pl.multiple_of(a * 256, 256), 256)] = xb
        cot_b[pl.ds(pl.multiple_of((a + 1) * 512, 512), 512), :] = xb
        acc = jnp.where(clane == a + 1, x[:, 0:1], acc)
        return jnp.where(clane == 65 + a, x[:, 255:256], acc)

    cedges = lax.fori_loop(0, 16, split_tokens, jnp.zeros((512, 128), F32))
    sc[...] = cedges.astype(BF16)
    c_north = remote(3, cot_b.at[pl.ds(16 * 512, 512)], rcs, north)
    c_south = remote(4, cot_b.at[pl.ds(512, 512)], rcn, south)
    c_north.start()
    c_south.start()

    orders = ("zxy", "xyz", "yzx")
    recv_a, sum_2 = (ra_z, ra_x, ra_y), (s2_z, s2_x, s2_y)
    recv_b, sum_3 = (rb_z, rb_x, rb_y), (s3_z, s3_x, s3_y)
    recv_c = (rc_z, rc_x, rc_y)

    def part(axis, place):
        every = slice(None)
        if axis == "z":
            return (pl.ds(place, 1), every, every, every, every)
        if axis == "y":
            return (every, every, pl.ds(place, 1), every, every)
        lanes = pl.ds(pl.multiple_of(lax.div(place, 2) * 128, 128), 128)
        return (every, pl.ds(lax.rem(place, 2), 1), every, every, lanes)

    def exchange(axis, src, dst, ss, rs):
        copies = []
        for d in range(1, 4):
            place = lax.rem(spot[axis] + d, 4)
            copies.append(pltpu.make_async_remote_copy(
                src_ref=src(part(axis, place)), dst_ref=dst(d - 1), send_sem=ss(d - 1), recv_sem=rs(d - 1),
                device_id=peer_on(axis, place), device_id_type=pl.DeviceIdType.MESH,
            ))
        return copies

    def core_copy(p):
        return pltpu.make_async_remote_copy(
            src_ref=gbuf.at[p, :, 1 - core], dst_ref=rcore.at[p], send_sem=core_s.at[p], recv_sem=core_r.at[p],
            device_id=other_core, device_id_type=pl.DeviceIdType.MESH,
        )

    def a_copies(p):
        k, slot = p % 3, p // 3
        return exchange(
            orders[k][0], lambda at_part: rcore.at[(p,) + at_part], lambda d: recv_a[k].at[slot, d],
            lambda d: a_s.at[p, d], lambda d: a_r.at[p, d],
        )

    def b_copies(k):
        return exchange(
            orders[k][1], lambda at_part: sum_2[k].at[(slice(None),) + at_part], lambda d: recv_b[k].at[d],
            lambda d: b_s.at[k, d], lambda d: b_r.at[k, d],
        )

    def c_copies(k):
        return exchange(
            orders[k][2], lambda at_part: sum_3[k].at[(slice(None),) + at_part], lambda d: recv_c[k].at[d],
            lambda d: c_s.at[k, d], lambda d: c_r.at[k, d],
        )

    def g_copies():
        return [
            pltpu.make_async_remote_copy(
                src_ref=s4, dst_ref=gathered.at[lon], send_sem=g_s.at[d - 1], recv_sem=g_r.at[d - 1],
                device_id=lon_peer(d), device_id_type=pl.DeviceIdType.MESH,
            )
            for d in range(1, 8)
        ]

    def core_start(p, value):
        gbuf[p] = value.reshape(4, 2, 2, 4, 8, 256)
        core_copy(p).start()

    def a_start(p):
        core_copy(p).wait()
        rcore[p] = rcore[p] + gbuf[p, :, core]
        for copy in a_copies(p):
            copy.start()

    def b_start():
        for p in range(8):
            k, slot = p % 3, p // 3
            for copy in a_copies(p):
                copy.wait()
            own = rcore[(p,) + part(orders[k][0], spot[orders[k][0]])]
            got = recv_a[k][slot]
            sum_2[k][slot] = own + got[0] + got[1] + got[2]
        for k in range(3):
            for copy in b_copies(k):
                copy.start()

    def c_start():
        for k in range(3):
            for copy in b_copies(k):
                copy.wait()
            own = sum_2[k][(slice(None),) + part(orders[k][1], spot[orders[k][1]])]
            got = recv_b[k][...]
            sum_3[k][...] = own + got[0] + got[1] + got[2]
            for copy in c_copies(k):
                copy.start()

    def g_start():
        for k in range(3):
            for copy in c_copies(k):
                copy.wait()
            own = sum_3[k][(slice(None),) + part(orders[k][2], spot[orders[k][2]])]
            got = recv_c[k][...]
            total = own + got[0] + got[1] + got[2]
            for slot in range(total.shape[0]):
                s4[slot * 3 + k] = total[slot, 0, 0, 0]
        for copy in g_copies():
            copy.start()

    def tile(n, pair):
        _, parity, off = ROWS[n]
        rows = planes[pl.ds((parity * 4 + pair * 2) * CP, 2 * CP), pl.ds(off * 256, 4096)]
        return dot_nt(cot_a[...], rows)

    core_start(0, tile(0, 0))
    core_start(1, tile(1, 0))
    a_start(0)

    natural = jnp.where(row5 == local_col[...], 1.0, 0.0).astype(BF16)
    half = dot(natural, perm[...]).astype(BF16)
    fold_sel[...] = dot(permt[...], half).astype(BF16)

    x_north.wait()
    x_south.wait()
    zero16 = jnp.zeros((), BF16)
    planes[pl.ds(512, 512), pl.ds(0, 256)] = jnp.where(at_bottom, zero16, rxs[...])
    planes[pl.ds(0, 512), pl.ds(16 * 256, 256)] = rxn[...]

    @pl.when(at_top)
    def _():
        x_mirror.wait()
        top = jnp.concatenate([rmir[pl.ds(0, CP), :], rmir[pl.ds(CP, CP), :]], axis=1)
        folded = dot(top, fold_sel[...])
        put_row(0, 16, folded[:, :256], folded[:, 256:])

    acc = edges
    low_e = planes[pl.ds(512, CP), pl.ds(0, 128)].astype(F32)
    low_o = planes[pl.ds(512 + CP, CP), pl.ds(128, 128)].astype(F32)
    high_e = planes[pl.ds(0, CP), pl.ds(16 * 256, 128)].astype(F32)
    high_o = planes[pl.ds(CP, CP), pl.ds(16 * 256 + 128, 128)].astype(F32)
    acc = jnp.where(lane128 == 0, low_e[:, 0:1], acc)
    acc = jnp.where(lane128 == 64, low_o[:, 127:128], acc)
    acc = jnp.where(lane128 == 33, high_e[:, 0:1], acc)
    acc = jnp.where(lane128 == 97, high_o[:, 127:128], acc)
    sx[...] = acc.astype(BF16)
    x_east = remote(5, sx, rxw, east)
    x_west = remote(6, sx, rxe, west)
    x_east.start()
    x_west.start()

    c_north.wait()
    c_south.wait()
    cot_b[pl.ds(0, 512), :] = jnp.where(at_bottom, zero16, rcs[...])
    cot_b[pl.ds(17 * 512, 512), :] = jnp.where(at_top, zero16, rcn[...])
    low = cot_b[pl.ds(0, 512), :].astype(F32)
    high = cot_b[pl.ds(17 * 512, 512), :].astype(F32)
    acc = sc[...].astype(F32)
    acc = jnp.where(clane == 0, low[:, 0:1], acc)
    acc = jnp.where(clane == 64, low[:, 255:256], acc)
    acc = jnp.where(clane == 17, high[:, 0:1], acc)
    acc = jnp.where(clane == 81, high[:, 255:256], acc)
    sc[...] = acc.astype(BF16)
    c_east = remote(7, sc, rcw, east)
    c_west = remote(8, sc, rce, west)
    c_east.start()
    c_west.start()

    core_start(2, tile(2, 0))
    a_start(1)
    core_start(3, tile(3, 0))
    a_start(2)
    x_east.wait()
    x_west.wait()
    side = jnp.concatenate(
        [jnp.where(lane128 >= 64, rxw[...], zero16), jnp.where(lane128 < 64, rxe[...], zero16)], axis=0
    )
    lrow, lcol = iota((128, 128), 0), iota((128, 128), 1)
    for n in range(4):
        i = ROWS[n][0]
        first = (lrow >= 1) & (lrow <= 16) & (lcol == 62 + 2 * lrow + i)
        last = (lrow >= 65) & (lrow <= 80) & (lcol == 2 * lrow - 130 + i)
        spread = jnp.where(first | last, 1.0, 0.0).astype(BF16)
        moved = dot(sc[...], spread).astype(BF16)
        core_start(4 + n, tile(n, 1) + dot_nt(moved, side))
        a_start(3 + n)

    loads[8].wait()
    loads[9].wait()
    wspad[pl.ds(336, 48), :] = jnp.zeros((48, 512), BF16)
    pick = jnp.where(lax.rem(lrow, 8) * 16 + lax.div(lrow, 8) == lcol, 1.0, 0.0).astype(BF16)
    for o in range(16):
        put(sbuf, pl.ds(o * CP + 120, 8), jnp.zeros((8, 512), F32))
    for kb in range(15):
        if kb < 3:
            got = dot(pick, wspad[pl.ds(kb * 128, 128), :])
        else:
            got = dot_nt(pick, wstage[:, pl.ds((kb - 3) * 128, 128)])
        for o in range(16):
            put(sbuf, pl.ds(o * CP + kb * 8, 8), got[o * 8:o * 8 + 8, :])
    for parity in range(2):
        for j in range(4):
            for k, i in enumerate(((3, 1), (2, 0))[parity]):
                wcat[pl.ds((parity * 4 + j) * CP, CP), pl.ds(k * 512, 512)] = get(
                    sbuf, pl.ds((i * 4 + JORD[j]) * CP, CP)
                ).astype(BF16)

    a_start(7)

    c_east.wait()
    c_west.wait()
    z_west, z_east = [], []
    for parity in range(2):
        for j, src, out in ((3, rcw, z_west), (2, rce, z_east)):
            w_rows = wcat[pl.ds((parity * 4 + j) * CP, CP), :]
            first = dot(w_rows[:, :512], src[...])
            second = dot(w_rows[:, 512:], src[...])
            out.append(first + pltpu.roll(second, 127, 1))

    def token_row(s, parity):
        tokens = cot_b[pl.ds(pl.multiple_of(s * 512, 512), 1024), :]
        u = dot(wcat[pl.ds(parity * 512, 512), :], tokens)
        u1, u2, u0, u3 = (u[k * CP:(k + 1) * CP] for k in range(4))
        zw = pltpu.roll(z_west[parity], 64 - s, 1)
        ze = pltpu.roll(z_east[parity], 127 - s, 1)
        r3 = pltpu.roll(u3, 1, 1)
        r0 = pltpu.roll(u0, 255, 1)
        r3 = jnp.concatenate([jnp.where(lane128 == 0, zw, r3[:, :128]), r3[:, 128:]], axis=1)
        r0 = jnp.concatenate([r0[:, :128], jnp.where(lane128 == 127, ze, r0[:, 128:])], axis=1)
        return jnp.concatenate([u1 + r3, u2 + r0], axis=1)

    sfold[...] = token_row(16, 0).astype(BF16)
    g_mirror = remote(9, sfold, rfold, mirror)

    @pl.when(at_top)
    def _():
        g_mirror.start()

    put(sbuf, pl.ds(31, CP, stride=32), token_row(16, 1))
    put(sbuf, pl.ds(0, CP, stride=32), token_row(0, 0))

    def rows_of(s, _):
        put(sbuf, pl.ds(2 * s, CP, stride=32), token_row(s, 0))
        put(sbuf, pl.ds(2 * s - 1, CP, stride=32), token_row(s, 1))
        pl.when(s == 4)(b_start)
        pl.when(s == 8)(c_start)
        pl.when(s == 12)(g_start)
        return 0

    lax.fori_loop(1, 16, rows_of, 0)

    @pl.when(at_top)
    def _():
        g_mirror.wait()
        at = pl.ds(31, CP, stride=32)
        put(sbuf, at, get(sbuf, at) + dot(rfold[...], fold_sel[...]))

    stores = []
    outs = [(xs_out, 0, 0, SC * 32)]
    for k in range(6):
        outs.append((xf_out, k * 512, F0 * 32 + k * 512, 512))
    for n, (dst, at, to, rows) in enumerate(outs):
        cells = dot(get(sbuf, pl.ds(to, rows)).astype(BF16), permt[...]).astype(BF16)
        cells = cells.reshape(rows // 32, 32, 512) * mask_bf[None]
        raw[pl.ds(to, rows), :] = cells.reshape(rows, 512)
        copy = pltpu.make_async_copy(raw.at[pl.ds(to, rows)], dst.at[pl.ds(at, rows)], out_sem.at[n])
        copy.start()
        stores.append(copy)

    for copy in g_copies():
        copy.wait()
    gathered[lon] = s4[...]
    scale = 1.0 / math.sqrt(lax.axis_size("batch") * 16 * lat_n * 256 * lon_n)
    for p in range(8):
        for which in range(2):
            o = ROWS[p % 4][0] * 4 + JORD[p // 4 * 2 + which]
            rows = [gathered[4 * which + y, p] for y in range(4)] + [jnp.zeros((96, 128), F32)]
            tbuf[pl.ds(o, 128, stride=16), :] = jnp.transpose(jnp.concatenate(rows, axis=0) * scale)
    for k in range(3):
        block = jnp.transpose(tbuf[pl.ds(k * 128, 128), :])[:32]
        if k < 2:
            ks_out[:, pl.ds(k * 128, 128)] = block
        else:
            ks_out[:, pl.ds(256, 80)] = block[:, :80]
    for k in range(12):
        kf_out[:, pl.ds(k * 128, 128)] = jnp.transpose(tbuf[pl.ds((k + 3) * 128, 128), :])[:32]
    for copy in stores:
        copy.wait()


def on_device(state, forcing, land_mask, partner, cotangent, weight_state, weight_force):
    sc, fc = state.shape[1], forcing.shape[1]
    rows, cols = state.shape[2:]
    width = cotangent.shape[1]
    lon_n, lat_n, batch_n = (lax.axis_size(a) for a in ("lon", "lat", "batch"))
    local_col = (partner - (lon_n - 1 - lax.axis_index("lon")) * cols)[None, :]
    any_spec = pl.BlockSpec(memory_space=pl.ANY)
    vmem = pl.BlockSpec(memory_space=pltpu.VMEM)
    ks, kf, xs, xf = pl.pallas_call(
        main_kernel,
        out_shape=(
            jax.ShapeDtypeStruct((width // (lat_n * batch_n), sc * 16), F32),
            jax.ShapeDtypeStruct((width // (lat_n * batch_n), fc * 16), F32),
            jax.ShapeDtypeStruct((sc * rows, cols), BF16),
            jax.ShapeDtypeStruct((fc * rows, cols), BF16),
        ),
        in_specs=[any_spec, any_spec, vmem, vmem, any_spec, any_spec, any_spec],
        out_specs=(vmem, vmem, any_spec, any_spec),
        scratch_shapes=[
            pltpu.VMEM((4096, 512), BF16),
            pltpu.VMEM((4, 4096, 128), F32),
            pltpu.VMEM((8 * CP, 17 * 256), BF16),
            pltpu.VMEM((8192, 256), BF16),
            pltpu.VMEM((2, 8192, 128), F32),
            pltpu.VMEM((512, 4096), BF16),
            pltpu.VMEM((18 * 512, 256), BF16),
            pltpu.VMEM((1024, 1024), BF16),
            pltpu.VMEM((8, 4, 2, 2, 4, 8, 256), F32),
            pltpu.VMEM((512, 1536), BF16),
            pltpu.VMEM((384, 512), BF16),
            pltpu.VMEM((512, 512), BF16),
            pltpu.VMEM((512, 512), BF16),
            pltpu.VMEM((512, 512), BF16),
            pltpu.VMEM((512, 256), BF16),
            pltpu.VMEM((512, 256), BF16),
            pltpu.VMEM((256, 256), BF16),
            pltpu.VMEM((512, 256), BF16),
            pltpu.VMEM((512, 256), BF16),
            pltpu.VMEM((CP, 128), BF16),
            pltpu.VMEM((CP, 128), BF16),
            pltpu.VMEM((CP, 128), BF16),
            pltpu.VMEM((512, 128), BF16),
            pltpu.VMEM((512, 128), BF16),
            pltpu.VMEM((512, 128), BF16),
            pltpu.VMEM((CP, 512), BF16),
            pltpu.VMEM((CP, 512), BF16),
            pltpu.VMEM((8, 4, 2, 4, 8, 256), F32),
            pltpu.VMEM((3, 3, 1, 2, 4, 8, 256), F32),
            pltpu.VMEM((3, 3, 4, 1, 4, 8, 128), F32),
            pltpu.VMEM((2, 3, 4, 2, 1, 8, 256), F32),
            pltpu.VMEM((3, 1, 2, 4, 8, 256), F32),
            pltpu.VMEM((3, 4, 1, 4, 8, 128), F32),
            pltpu.VMEM((2, 4, 2, 1, 8, 256), F32),
            pltpu.VMEM((3, 3, 1, 1, 4, 8, 128), F32),
            pltpu.VMEM((3, 3, 4, 1, 1, 8, 128), F32),
            pltpu.VMEM((3, 2, 1, 2, 1, 8, 256), F32),
            pltpu.VMEM((3, 1, 1, 4, 8, 128), F32),
            pltpu.VMEM((3, 4, 1, 1, 8, 128), F32),
            pltpu.VMEM((2, 1, 2, 1, 8, 256), F32),
            pltpu.VMEM((3, 3, 1, 1, 1, 8, 128), F32),
            pltpu.VMEM((3, 3, 1, 1, 1, 8, 128), F32),
            pltpu.VMEM((3, 2, 1, 1, 1, 8, 128), F32),
            pltpu.VMEM((8, 8, 128), F32),
            pltpu.VMEM((8, 8, 8, 128), F32),
            pltpu.VMEM((2048, 128), F32),
            pltpu.SemaphoreType.DMA((10,)),
            pltpu.SemaphoreType.DMA((8,)),
            pltpu.SemaphoreType.DMA((10,)),
            pltpu.SemaphoreType.DMA((10,)),
            pltpu.SemaphoreType.DMA((8,)),
            pltpu.SemaphoreType.DMA((8,)),
            pltpu.SemaphoreType.DMA((8, 3)),
            pltpu.SemaphoreType.DMA((8, 3)),
            pltpu.SemaphoreType.DMA((3, 3)),
            pltpu.SemaphoreType.DMA((3, 3)),
            pltpu.SemaphoreType.DMA((3, 3)),
            pltpu.SemaphoreType.DMA((3, 3)),
            pltpu.SemaphoreType.DMA((7,)),
            pltpu.SemaphoreType.DMA((7,)),
        ],
        compiler_params=pltpu.CompilerParams(
            collective_id=0, has_side_effects=True, vmem_limit_bytes=62 * 1024 * 1024
        ),
        name="encoder_backward",
    )(
        state.reshape(sc * rows, cols), forcing.reshape(fc * rows, cols), land_mask, local_col,
        cotangent.reshape(width * cotangent.shape[2], cotangent.shape[3]), weight_state.T, weight_force,
    )
    return (
        xs.reshape(state.shape),
        xf.reshape(forcing.shape),
        ks,
        kf,
    )


def solution(mesh):
    in_specs = (
        P("batch", None, "lat", "lon"),
        P("batch", None, "lat", "lon"),
        P("lat", "lon"),
        P("lon"),
        P("batch", None, "lat", "lon"),
        P(),
        P(),
    )
    out_specs = (
        P("batch", None, "lat", "lon"),
        P("batch", None, "lat", "lon"),
        P(("lat", "batch"), None),
        P(("lat", "batch"), None),
    )
    return jax.shard_map(on_device, mesh=mesh, in_specs=in_specs, out_specs=out_specs, check_vma=False)
```

```python
import functools
import math

import jax
import jax.numpy as jnp
from jax import lax
from jax.experimental import pallas as pl
from jax.experimental.pallas import tpu as pltpu
from jax.sharding import PartitionSpec as P

SC = 21
FC = 96
CP = 128
F32 = jnp.float32
BF16 = jnp.bfloat16
JORD = (1, 2, 0, 3)
ROWS = ((1, 0, 0), (2, 1, 1), (0, 1, 0), (3, 0, 1))


def iota(shape, dim):
    return lax.broadcasted_iota(jnp.int32, shape, dim)


def dot(a, b):
    return lax.dot_general(a, b, (((1,), (0,)), ((), ())), preferred_element_type=F32)


def dot_nt(a, b):
    return lax.dot_general(a, b, (((1,), (1,)), ((), ())), preferred_element_type=F32)


def flag(where):
    return jnp.where(where, 1.0, 0.0).astype(BF16)


def main_kernel(
    state, force, mask, partner, cot, wst, wf,
    share_out, rows_out,
    raw, planes, craw, cot_a, cot_b, wcat, wscr, gbuf, wstage, wspad, perm, permt, perm2, permt2, fold_sel, top_row,
    rxs, rxn, rmir, rcs, rcn, sx, rxw, rxe, sc, rcw, rce, sfold, rfold,
    rcore, ra_z, ra_x, ra_y, s2_z, s2_x, s2_y, rb_z, rb_x, rb_y, s3_z, s3_x, s3_y, rc_z, rc_x, rc_y, s4, gathered,
    in_sem, out_sem, send, recv, core_s, core_r, a_s, a_r, b_s, b_r, c_s, c_r, g_s, g_r,
):
    lon_n = lax.axis_size("lon")
    lat_n = lax.axis_size("lat")
    lon = lax.axis_index("lon")
    lat = lax.axis_index("lat")
    at_top = lat == lat_n - 1
    at_bottom = lat == 0
    north = {"lat": lax.rem(lat + 1, lat_n)}
    south = {"lat": lax.rem(lat + lat_n - 1, lat_n)}
    east = {"lon": lax.rem(lon + 1, lon_n)}
    west = {"lon": lax.rem(lon + lon_n - 1, lon_n)}
    mirror = {"lon": lon_n - 1 - lon}
    at_y, at_z, core = lax.rem(lon, 4), lax.div(lat, 2), lax.rem(lat, 2)
    x_lo, x_hi = lax.axis_index("batch"), lax.div(lon, 4)
    spot = {"x": 2 * x_hi + x_lo, "y": at_y, "z": at_z}
    other_core = {"lat": 2 * at_z + 1 - core}

    def peer_on(axis, place):
        if axis == "z":
            return {"lat": 2 * place + core}
        if axis == "y":
            return {"lon": 4 * x_hi + place}
        return {"lon": 4 * lax.div(place, 2) + at_y, "batch": lax.rem(place, 2)}

    def lon_peer(d):
        return {"lon": lax.rem(lon + d, lon_n)}

    peers = [north, south, mirror, other_core] + [lon_peer(d) for d in range(1, 8)]
    for axis in "xyz":
        peers += [peer_on(axis, lax.rem(spot[axis] + d, 4)) for d in range(1, 4)]

    loads = []
    for k in range(6):
        loads.append(pltpu.make_async_copy(force.at[pl.ds(k * 512, 512)], raw.at[pl.ds(k * 512, 512)], in_sem.at[k]))
    loads.append(pltpu.make_async_copy(state, raw.at[pl.ds(FC * 32, SC * 32)], in_sem.at[6]))
    loads.append(pltpu.make_async_copy(cot, craw, in_sem.at[7]))
    loads.append(pltpu.make_async_copy(wst, wspad.at[pl.ds(0, 336)], in_sem.at[8]))
    loads.append(pltpu.make_async_copy(wf, wstage, in_sem.at[9]))
    for copy in loads:
        copy.start()

    barrier = pltpu.get_barrier_semaphore()
    for peer in peers:
        pl.semaphore_signal(barrier, inc=1, device_id=peer, device_id_type=pl.DeviceIdType.MESH)
    def remote(n, src, dst, peer):
        return pltpu.make_async_remote_copy(
            src_ref=src, dst_ref=dst, send_sem=send.at[n], recv_sem=recv.at[n],
            device_id=peer, device_id_type=pl.DeviceIdType.MESH,
        )

    down, across = iota((512, 1), 0), iota((1, 512), 1)

    def column(lane, late):
        half = lax.shift_right_logical(lane, 8)
        return (2 * lane + (-half if late else half)) & 511

    perm[...] = flag(down == column(across, False))
    permt[...] = flag(column(down, False) == across)
    perm2[...] = flag(down == column(across, True))
    permt2[...] = flag(column(down, True) == across)

    raw[pl.ds((FC + SC) * 32, (CP - FC - SC) * 32), :] = jnp.zeros(((CP - FC - SC) * 32, 512), BF16)
    mask_bf = mask[...].astype(F32).astype(BF16)
    zero16 = jnp.zeros((), BF16)
    lane128 = iota((CP, 128), 1)

    def put_row(parity, slot, channels, both):
        n = both.shape[0]
        lane256 = iota((n, 256), 1)
        even, odd = both[:, :256], both[:, 256:]
        left = jnp.where(lane256 == 0, zero16, pltpu.roll(odd, 1, 1))
        right = jnp.where(lane256 == 255, zero16, pltpu.roll(even, 255, 1))
        for j, part in enumerate((even, odd, left, right)):
            planes[pl.ds((parity * 4 + j) * CP + channels, n), pl.ds(slot * 256, 256)] = part

    lane16 = iota((16, 128), 1)
    for k in range(8):
        if k < 7:
            loads[k].wait()
        x = raw[pl.ds(k * 512, 512), :].reshape(16, 32, 512) * mask_bf[None]
        y = dot(x.reshape(512, 512), perm[...]).astype(BF16)
        y = jnp.swapaxes(y.reshape(16, 32, 512), 0, 1)
        edge = jnp.zeros((16, 128), BF16)
        for r in range(32):
            put_row(r % 2, r // 2 + r % 2, k * 16, y[r])
            edge = jnp.where(lane16 == r + 1, y[r][:, 0:1], edge)
            edge = jnp.where(lane16 == 65 + r, y[r][:, 511:512], edge)
        sx[pl.ds(k * 16, 16), :] = edge

    pl.semaphore_wait(barrier, len(peers))
    x_north = remote(0, planes.at[pl.ds(512, 512), pl.ds(16 * 256, 256)], rxs, north)
    x_south = remote(1, planes.at[pl.ds(0, 512), pl.ds(0, 256)], rxn, south)
    x_mirror = remote(2, planes.at[pl.ds(512, 256), pl.ds(16 * 256, 256)], rmir, mirror)
    x_north.start()
    x_south.start()

    @pl.when(at_top)
    def _():
        x_mirror.start()

    loads[7].wait()
    clane = iota((512, 128), 1)
    lane32 = iota((32, 128), 1)

    def late(x):
        return jnp.where(iota(x.shape, 1) == 0, zero16, pltpu.roll(x, 1, 1))

    def split_tokens(k, _):
        x = craw[pl.ds(pl.multiple_of(k * 512, 512), 512), :].reshape(32, 16, 256)
        y = jnp.swapaxes(x, 0, 1)
        w = pl.multiple_of(k * 32, 32)
        edge = jnp.zeros((32, 128), BF16)
        for a in range(16):
            cot_a[pl.ds(w, 32), pl.ds(a * 256, 256)] = y[a]
            cot_b[pl.ds((a + 1) * 1024 + w, 32), :] = y[a]
            cot_b[pl.ds((a + 1) * 1024 + 512 + w, 32), :] = late(y[a])
            edge = jnp.where(lane32 == a + 1, y[a][:, 0:1], edge)
            edge = jnp.where(lane32 == 65 + a, y[a][:, 255:256], edge)
        sc[pl.ds(w, 32), :] = edge
        return 0

    lax.fori_loop(0, 16, split_tokens, 0)
    c_north = remote(3, cot_b.at[pl.ds(16 * 1024, 512)], rcs, north)
    c_south = remote(4, cot_b.at[pl.ds(1024, 512)], rcn, south)
    c_north.start()
    c_south.start()

    def tile(n, pair):
        _, parity, off = ROWS[n]
        rows = planes[pl.ds((parity * 4 + pair * 2) * CP, 2 * CP), pl.ds(off * 256, 4096)]
        return dot_nt(cot_a[...], rows)

    orders = ("zxy", "xyz", "yzx")
    recv_a, sum_2 = (ra_z, ra_x, ra_y), (s2_z, s2_x, s2_y)
    recv_b, sum_3 = (rb_z, rb_x, rb_y), (s3_z, s3_x, s3_y)
    recv_c = (rc_z, rc_x, rc_y)

    def part(axis, place):
        every = slice(None)
        if axis == "z":
            return (pl.ds(place, 1), every, every, every, every)
        if axis == "y":
            return (every, every, pl.ds(place, 1), every, every)
        lanes = pl.ds(pl.multiple_of(lax.div(place, 2) * 128, 128), 128)
        return (every, pl.ds(lax.rem(place, 2), 1), every, every, lanes)

    def exchange(axis, src, dst, ss, rs):
        copies = []
        for d in range(1, 4):
            place = lax.rem(spot[axis] + d, 4)
            copies.append(pltpu.make_async_remote_copy(
                src_ref=src(part(axis, place)), dst_ref=dst(d - 1), send_sem=ss(d - 1), recv_sem=rs(d - 1),
                device_id=peer_on(axis, place), device_id_type=pl.DeviceIdType.MESH,
            ))
        return copies

    def core_copy(p):
        return pltpu.make_async_remote_copy(
            src_ref=gbuf.at[p, :, 1 - core], dst_ref=rcore.at[p], send_sem=core_s.at[p], recv_sem=core_r.at[p],
            device_id=other_core, device_id_type=pl.DeviceIdType.MESH,
        )

    def a_copies(p):
        k, slot = p % 3, p // 3
        return exchange(
            orders[k][0], lambda at_part: rcore.at[(p,) + at_part], lambda d: recv_a[k].at[slot, d],
            lambda d: a_s.at[p, d], lambda d: a_r.at[p, d],
        )

    def b_copies(k):
        return exchange(
            orders[k][1], lambda at_part: sum_2[k].at[(slice(None),) + at_part], lambda d: recv_b[k].at[d],
            lambda d: b_s.at[k, d], lambda d: b_r.at[k, d],
        )

    def c_copies(k):
        return exchange(
            orders[k][2], lambda at_part: sum_3[k].at[(slice(None),) + at_part], lambda d: recv_c[k].at[d],
            lambda d: c_s.at[k, d], lambda d: c_r.at[k, d],
        )

    def g_copies():
        return [
            pltpu.make_async_remote_copy(
                src_ref=s4, dst_ref=gathered.at[lon], send_sem=g_s.at[d - 1], recv_sem=g_r.at[d - 1],
                device_id=lon_peer(d), device_id_type=pl.DeviceIdType.MESH,
            )
            for d in range(1, 8)
        ]

    def core_start(p, value):
        gbuf[p] = value.reshape(4, 2, 2, 4, 8, 256)
        core_copy(p).start()

    def a_start(p):
        core_copy(p).wait()
        rcore[p] = rcore[p] + gbuf[p, :, core]
        for copy in a_copies(p):
            copy.start()

    def b_start():
        for p in range(8):
            k, slot = p % 3, p // 3
            for copy in a_copies(p):
                copy.wait()
            own = rcore[(p,) + part(orders[k][0], spot[orders[k][0]])]
            got = recv_a[k][slot]
            sum_2[k][slot] = own + got[0] + got[1] + got[2]
        for k in range(3):
            for copy in b_copies(k):
                copy.start()

    def c_start():
        for k in range(3):
            for copy in b_copies(k):
                copy.wait()
            own = sum_2[k][(slice(None),) + part(orders[k][1], spot[orders[k][1]])]
            got = recv_b[k][...]
            sum_3[k][...] = own + got[0] + got[1] + got[2]
            for copy in c_copies(k):
                copy.start()

    def g_start():
        for k in range(3):
            for copy in c_copies(k):
                copy.wait()
            own = sum_3[k][(slice(None),) + part(orders[k][2], spot[orders[k][2]])]
            got = recv_c[k][...]
            total = own + got[0] + got[1] + got[2]
            for slot in range(total.shape[0]):
                s4[slot * 3 + k] = total[slot, 0, 0, 0]
        for copy in g_copies():
            copy.start()

    def tile(n, pair):
        _, parity, off = ROWS[n]
        rows = planes[pl.ds((parity * 4 + pair * 2) * CP, 2 * CP), pl.ds(off * 256, 4096)]
        return dot_nt(cot_a[...], rows)

    core_start(0, tile(0, 0))
    core_start(1, tile(1, 0))
    a_start(0)

    fold_sel[...] = flag(down == partner[...] - (lon_n - 1 - lon) * 512)

    def folded(x, before, after):
        x = dot(x, before[...]).astype(BF16)
        x = dot(x, fold_sel[...]).astype(BF16)
        return dot(x, after[...])

    x_north.wait()
    x_south.wait()
    planes[pl.ds(512, 512), pl.ds(0, 256)] = jnp.where(at_bottom, zero16, rxs[...])
    planes[pl.ds(0, 512), pl.ds(16 * 256, 256)] = rxn[...]

    @pl.when(at_top)
    def _():
        x_mirror.wait()
        top = jnp.concatenate([rmir[pl.ds(0, CP), :], rmir[pl.ds(CP, CP), :]], axis=1)
        put_row(0, 16, 0, folded(top, permt, perm).astype(BF16))

    acc = sx[...]
    acc = jnp.where(lane128 == 0, planes[pl.ds(512, CP), pl.ds(0, 128)][:, 0:1], acc)
    acc = jnp.where(lane128 == 64, planes[pl.ds(512 + CP, CP), pl.ds(128, 128)][:, 127:128], acc)
    acc = jnp.where(lane128 == 33, planes[pl.ds(0, CP), pl.ds(16 * 256, 128)][:, 0:1], acc)
    acc = jnp.where(lane128 == 97, planes[pl.ds(CP, CP), pl.ds(16 * 256 + 128, 128)][:, 127:128], acc)
    sx[...] = acc
    x_east = remote(5, sx, rxw, east)
    x_west = remote(6, sx, rxe, west)
    x_east.start()
    x_west.start()

    c_north.wait()
    c_south.wait()
    low = jnp.where(at_bottom, zero16, rcs[...])
    high = jnp.where(at_top, zero16, rcn[...])
    for slot, x in ((0, low), (17, high)):
        cot_b[pl.ds(slot * 1024, 512), :] = x
        cot_b[pl.ds(slot * 1024 + 512, 512), :] = late(x)
    acc = sc[...]
    acc = jnp.where(clane == 0, low[:, 0:1], acc)
    acc = jnp.where(clane == 64, low[:, 255:256], acc)
    acc = jnp.where(clane == 17, high[:, 0:1], acc)
    acc = jnp.where(clane == 81, high[:, 255:256], acc)
    sc[...] = acc
    c_east = remote(7, sc, rcw, east)
    c_west = remote(8, sc, rce, west)
    c_east.start()
    c_west.start()

    core_start(2, tile(2, 0))
    a_start(1)
    core_start(3, tile(3, 0))
    a_start(2)
    x_east.wait()
    x_west.wait()
    side = jnp.concatenate(
        [jnp.where(lane128 >= 64, rxw[...], zero16), jnp.where(lane128 < 64, rxe[...], zero16)], axis=0
    )
    lrow, lcol = iota((128, 128), 0), iota((128, 128), 1)
    for n in range(4):
        i = ROWS[n][0]
        first = (lrow >= 1) & (lrow <= 16) & (lcol == 62 + 2 * lrow + i)
        last = (lrow >= 65) & (lrow <= 80) & (lcol == 2 * lrow - 130 + i)
        spread = jnp.where(first | last, 1.0, 0.0).astype(BF16)
        moved = dot(sc[...], spread).astype(BF16)
        core_start(4 + n, tile(n, 1) + dot_nt(moved, side))
        a_start(3 + n)

    loads[8].wait()
    loads[9].wait()
    wspad[pl.ds(336, 48), :] = jnp.zeros((48, 512), BF16)
    pick = flag((lrow & 7) * 16 + lax.shift_right_logical(lrow, 3) == lcol)
    for o in range(16):
        wscr[pl.ds(o * CP + 120, 8), :] = jnp.zeros((8, 512), F32)
    for kb in range(15):
        if kb < 12:
            got = dot_nt(pick, wstage[:, pl.ds(kb * 128, 128)])
        else:
            got = dot(pick, wspad[pl.ds((kb - 12) * 128, 128), :])
        for o in range(16):
            wscr[pl.ds(o * CP + kb * 8, 8), :] = got[o * 8:o * 8 + 8, :]
    for parity in range(2):
        for q in range(2):
            for n, i in enumerate(((3, 1), (2, 0))[parity]):
                for m, j in enumerate(((1, 3), (0, 2))[q]):
                    wcat[pl.ds((parity * 2 + q) * CP, CP), pl.ds((n * 2 + m) * 512, 512)] = wscr[
                        pl.ds((i * 4 + j) * CP, CP), :
                    ].astype(BF16)
    a_start(7)

    c_east.wait()
    c_west.wait()
    for slot in range(18):
        at = (pl.ds(slot * 1024 + 512, 512), pl.ds(0, 128))
        cot_b[at] = jnp.where(clane == 0, rcw[...][:, 64 + slot:65 + slot], cot_b[at])
    last = []
    for parity in range(2):
        w_rows = wcat[pl.ds((parity * 2 + 1) * CP, CP), :]
        total = dot(w_rows[:, :512], rce[...]) + pltpu.roll(dot(w_rows[:, 512:1024], sc[...]), 64, 1)
        total = total + pltpu.roll(dot(w_rows[:, 1024:1536], rce[...]), 127, 1)
        last.append(total + pltpu.roll(dot(w_rows[:, 1536:], sc[...]), 63, 1))

    def token_row(s, parities):
        tokens = cot_b[pl.ds(pl.multiple_of(s * 1024, 1024), 2048), :]
        u = dot(wcat[pl.ds(0, 256 * parities), :], tokens)
        rows = []
        for parity in range(parities):
            even, odd = u[parity * 256:parity * 256 + 128], u[parity * 256 + 128:parity * 256 + 256]
            first = jnp.where(lane128 == 0, pltpu.roll(last[parity], lax.rem(128 - s, 128), 1), odd[:, :128])
            rows.append(jnp.concatenate([even, first, odd[:, 128:]], axis=1))
        return rows

    fold, top = token_row(16, 2)
    sfold[...] = fold.astype(BF16)
    top_row[...] = top
    g_mirror = remote(9, sfold, rfold, mirror)

    @pl.when(at_top)
    def _():
        g_mirror.start()

    raw[pl.ds(0, CP), :] = token_row(0, 1)[0].astype(BF16)

    def out_copy(n, first, count):
        return pltpu.make_async_copy(raw.at[pl.ds(first * CP, count * CP)], rows_out.at[pl.ds(first * CP, count * CP)], out_sem.at[n])

    def rows_of(s, _):
        even, odd = token_row(s, 2)
        raw[pl.ds(pl.multiple_of(2 * s * CP, CP), CP), :] = even.astype(BF16)
        raw[pl.ds(pl.multiple_of((2 * s - 1) * CP, CP), CP), :] = odd.astype(BF16)
        pl.when(s == 4)(b_start)
        pl.when(s == 8)(c_start)
        pl.when(s == 9)(lambda: out_copy(0, 0, 19).start())
        pl.when(s == 12)(g_start)
        return 0

    lax.fori_loop(1, 16, rows_of, 0)
    out_copy(1, 19, 12).start()

    @pl.when(at_top)
    def _():
        g_mirror.wait()
        top_row[...] = top_row[...] + folded(rfold[...], permt2, perm2)

    raw[pl.ds(31 * CP, CP), :] = top_row[...].astype(BF16)
    out_copy(2, 31, 1).start()
    for copy in g_copies():
        copy.wait()
    gathered[lon] = s4[...]
    out_share = pltpu.make_async_copy(gathered, share_out, out_sem.at[3])
    out_share.start()
    for n, first, count in ((0, 0, 19), (1, 19, 12), (2, 31, 1)):
        out_copy(n, first, count).wait()
    out_share.wait()


def last_kernel(scale, share, rows, mask, ks_out, kf_out, xs_out, xf_out, permt2):
    k = pl.program_id(0)

    @pl.when(k == 0)
    def _():
        lane, across = iota((512, 1), 0), iota((1, 512), 1)
        permt2[...] = flag(((2 * lane - lax.shift_right_logical(lane, 8)) & 511) == across)
        turned = [None] * 16
        for p in range(8):
            for which in range(2):
                o = ROWS[p % 4][0] * 4 + JORD[p // 4 * 2 + which]
                own = [share[4 * which + y, p] for y in range(4)] + [jnp.zeros((96, 128), F32)]
                turned[o] = jnp.transpose(jnp.concatenate(own, axis=0)) * scale
        for n in range(15):
            block = jnp.stack([x[n * 8:n * 8 + 8] for x in turned], axis=0)
            block = jnp.transpose(jnp.swapaxes(block, 0, 1).reshape(128, 128))[:32]
            if n < 12:
                kf_out[:, pl.ds(n * 128, 128)] = block
            elif n < 14:
                ks_out[:, pl.ds((n - 12) * 128, 128)] = block
            else:
                ks_out[:, pl.ds(256, 80)] = block[:, :80]

    x = jnp.swapaxes(rows[...], 0, 1).reshape(512, 512)
    cells = dot(x, permt2[...]).astype(BF16).reshape(16, 32, 512)
    cells = (cells * mask[...].astype(F32).astype(BF16)[None]).reshape(512, 512)

    @pl.when(k < 6)
    def _():
        xf_out[...] = cells

    @pl.when(k >= 6)
    def _():
        xs_out[...] = cells


def on_device(state, forcing, land_mask, partner, cotangent, weight_state, weight_force):
    sc, fc = state.shape[1], forcing.shape[1]
    rows, cols = state.shape[2:]
    width = cotangent.shape[1]
    lon_n, lat_n, batch_n = (lax.axis_size(a) for a in ("lon", "lat", "batch"))
    any_spec = pl.BlockSpec(memory_space=pl.ANY)
    vmem = pl.BlockSpec(memory_space=pltpu.VMEM)
    share, cells = pl.pallas_call(
        main_kernel,
        out_shape=(
            jax.ShapeDtypeStruct((8, 8, 8, 128), F32),
            jax.ShapeDtypeStruct((rows * CP, cols), BF16),
        ),
        in_specs=[any_spec, any_spec, vmem, vmem, any_spec, any_spec, any_spec],
        out_specs=(any_spec, any_spec),
        scratch_shapes=[
            pltpu.VMEM((4096, 512), BF16),
            pltpu.VMEM((8 * CP, 17 * 256), BF16),
            pltpu.VMEM((8192, 256), BF16),
            pltpu.VMEM((512, 4096), BF16),
            pltpu.VMEM((18 * 1024, 256), BF16),
            pltpu.VMEM((512, 2048), BF16),
            pltpu.VMEM((2048, 512), F32),
            pltpu.VMEM((8, 4, 2, 2, 4, 8, 256), F32),
            pltpu.VMEM((512, 1536), BF16),
            pltpu.VMEM((384, 512), BF16),
            pltpu.VMEM((512, 512), BF16),
            pltpu.VMEM((512, 512), BF16),
            pltpu.VMEM((512, 512), BF16),
            pltpu.VMEM((512, 512), BF16),
            pltpu.VMEM((512, 512), BF16),
            pltpu.VMEM((CP, 512), F32),
            pltpu.VMEM((512, 256), BF16),
            pltpu.VMEM((512, 256), BF16),
            pltpu.VMEM((256, 256), BF16),
            pltpu.VMEM((512, 256), BF16),
            pltpu.VMEM((512, 256), BF16),
            pltpu.VMEM((CP, 128), BF16),
            pltpu.VMEM((CP, 128), BF16),
            pltpu.VMEM((CP, 128), BF16),
            pltpu.VMEM((512, 128), BF16),
            pltpu.VMEM((512, 128), BF16),
            pltpu.VMEM((512, 128), BF16),
            pltpu.VMEM((CP, 512), BF16),
            pltpu.VMEM((CP, 512), BF16),
            pltpu.VMEM((8, 4, 2, 4, 8, 256), F32),
            pltpu.VMEM((3, 3, 1, 2, 4, 8, 256), F32),
            pltpu.VMEM((3, 3, 4, 1, 4, 8, 128), F32),
            pltpu.VMEM((2, 3, 4, 2, 1, 8, 256), F32),
            pltpu.VMEM((3, 1, 2, 4, 8, 256), F32),
            pltpu.VMEM((3, 4, 1, 4, 8, 128), F32),
            pltpu.VMEM((2, 4, 2, 1, 8, 256), F32),
            pltpu.VMEM((3, 3, 1, 1, 4, 8, 128), F32),
            pltpu.VMEM((3, 3, 4, 1, 1, 8, 128), F32),
            pltpu.VMEM((3, 2, 1, 2, 1, 8, 256), F32),
            pltpu.VMEM((3, 1, 1, 4, 8, 128), F32),
            pltpu.VMEM((3, 4, 1, 1, 8, 128), F32),
            pltpu.VMEM((2, 1, 2, 1, 8, 256), F32),
            pltpu.VMEM((3, 3, 1, 1, 1, 8, 128), F32),
            pltpu.VMEM((3, 3, 1, 1, 1, 8, 128), F32),
            pltpu.VMEM((3, 2, 1, 1, 1, 8, 128), F32),
            pltpu.VMEM((8, 8, 128), F32),
            pltpu.VMEM((8, 8, 8, 128), F32),
            pltpu.SemaphoreType.DMA((10,)),
            pltpu.SemaphoreType.DMA((8,)),
            pltpu.SemaphoreType.DMA((10,)),
            pltpu.SemaphoreType.DMA((10,)),
            pltpu.SemaphoreType.DMA((8,)),
            pltpu.SemaphoreType.DMA((8,)),
            pltpu.SemaphoreType.DMA((8, 3)),
            pltpu.SemaphoreType.DMA((8, 3)),
            pltpu.SemaphoreType.DMA((3, 3)),
            pltpu.SemaphoreType.DMA((3, 3)),
            pltpu.SemaphoreType.DMA((3, 3)),
            pltpu.SemaphoreType.DMA((3, 3)),
            pltpu.SemaphoreType.DMA((7,)),
            pltpu.SemaphoreType.DMA((7,)),
        ],
        compiler_params=pltpu.CompilerParams(
            collective_id=0, has_side_effects=True, vmem_limit_bytes=62 * 1024 * 1024
        ),
        name="encoder_backward",
    )(
        state.reshape(sc * rows, cols), forcing.reshape(fc * rows, cols), land_mask, partner[None, :],
        cotangent.reshape(width * cotangent.shape[2], cotangent.shape[3]), weight_state.T, weight_force,
    )
    scale = 1.0 / math.sqrt(batch_n * (rows // 2) * lat_n * (cols // 2) * lon_n)
    own = width // (lat_n * batch_n)
    ks, kf, xs, xf = pl.pallas_call(
        functools.partial(last_kernel, scale),
        grid=(8,),
        out_shape=(
            jax.ShapeDtypeStruct((own, sc * 16), F32),
            jax.ShapeDtypeStruct((own, fc * 16), F32),
            jax.ShapeDtypeStruct((sc * rows, cols), BF16),
            jax.ShapeDtypeStruct((fc * rows, cols), BF16),
        ),
        in_specs=[
            pl.BlockSpec((8, 8, 8, 128), lambda k: (0, 0, 0, 0)),
            pl.BlockSpec((rows, 16, cols), lambda k: (0, k, 0)),
            pl.BlockSpec((rows, cols), lambda k: (0, 0)),
        ],
        out_specs=(
            pl.BlockSpec((own, sc * 16), lambda k: (0, 0)),
            pl.BlockSpec((own, fc * 16), lambda k: (0, 0)),
            pl.BlockSpec((16 * rows, cols), lambda k: (jnp.maximum(k - 6, 0), 0)),
            pl.BlockSpec((16 * rows, cols), lambda k: (jnp.minimum(k, 5), 0)),
        ),
        scratch_shapes=[pltpu.VMEM((512, 512), BF16)],
        name="encoder_finish",
    )(share, cells.reshape(rows, CP, cols), land_mask)
    return (
        xs.reshape(state.shape),
        xf.reshape(forcing.shape),
        ks,
        kf,
    )


def solution(mesh):
    in_specs = (
        P("batch", None, "lat", "lon"),
        P("batch", None, "lat", "lon"),
        P("lat", "lon"),
        P("lon"),
        P("batch", None, "lat", "lon"),
        P(),
        P(),
    )
    out_specs = (
        P("batch", None, "lat", "lon"),
        P("batch", None, "lat", "lon"),
        P(("lat", "batch"), None),
        P(("lat", "batch"), None),
    )
    return jax.shard_map(on_device, mesh=mesh, in_specs=in_specs, out_specs=out_specs, check_vma=False)
```

```python
import functools
import math

import jax
import jax.numpy as jnp
from jax import lax
from jax.experimental import pallas as pl
from jax.experimental.pallas import tpu as pltpu
from jax.sharding import PartitionSpec as P

SC = 21
FC = 96
CP = 128
F32 = jnp.float32
BF16 = jnp.bfloat16
JORD = (1, 2, 0, 3)
ROWS = ((1, 0, 0), (2, 1, 1), (0, 1, 0), (3, 0, 1))


def iota(shape, dim):
    return lax.broadcasted_iota(jnp.int32, shape, dim)


def dot(a, b):
    return lax.dot_general(a, b, (((1,), (0,)), ((), ())), preferred_element_type=F32)


def dot_nt(a, b):
    return lax.dot_general(a, b, (((1,), (1,)), ((), ())), preferred_element_type=F32)


def flag(where):
    return jnp.where(where, 1.0, 0.0).astype(BF16)


def main_kernel(
    state, force, mask, partner, cot, wst, wf,
    share_out, rows_out,
    raw, planes, craw, cot_a, cot_b, wcat, wscr, gbuf, wstage, wspad, perm, permt, perm2, permt2, fold_sel, top_row,
    rxs, rxn, rmir, rcs, rcn, sx, rxw, rxe, sc, rcw, rce, sfold, rfold,
    rcore, ra_z, ra_x, ra_y, s2_z, s2_x, s2_y, rb_z, rb_x, rb_y, s3_z, s3_x, s3_y, rc_z, rc_x, rc_y, s4, gathered,
    in_sem, out_sem, send, recv, core_s, core_r, a_s, a_r, b_s, b_r, c_s, c_r, g_s, g_r,
):
    lon_n = lax.axis_size("lon")
    lat_n = lax.axis_size("lat")
    lon = lax.axis_index("lon")
    lat = lax.axis_index("lat")
    at_top = lat == lat_n - 1
    at_bottom = lat == 0
    north = {"lat": lax.rem(lat + 1, lat_n)}
    south = {"lat": lax.rem(lat + lat_n - 1, lat_n)}
    east = {"lon": lax.rem(lon + 1, lon_n)}
    west = {"lon": lax.rem(lon + lon_n - 1, lon_n)}
    mirror = {"lon": lon_n - 1 - lon}
    at_y, at_z, core = lax.rem(lon, 4), lax.div(lat, 2), lax.rem(lat, 2)
    x_lo, x_hi = lax.axis_index("batch"), lax.div(lon, 4)
    spot = {"x": 2 * x_hi + x_lo, "y": at_y, "z": at_z}
    other_core = {"lat": 2 * at_z + 1 - core}

    def peer_on(axis, place):
        if axis == "z":
            return {"lat": 2 * place + core}
        if axis == "y":
            return {"lon": 4 * x_hi + place}
        return {"lon": 4 * lax.div(place, 2) + at_y, "batch": lax.rem(place, 2)}

    def lon_peer(d):
        return {"lon": lax.rem(lon + d, lon_n)}

    peers = [north, south, mirror, other_core] + [lon_peer(d) for d in range(1, 8)]
    for axis in "xyz":
        peers += [peer_on(axis, lax.rem(spot[axis] + d, 4)) for d in range(1, 4)]

    loads = []
    for k in range(6):
        loads.append(pltpu.make_async_copy(force.at[pl.ds(k * 512, 512)], raw.at[pl.ds(k * 512, 512)], in_sem.at[k]))
    loads.append(pltpu.make_async_copy(state, raw.at[pl.ds(FC * 32, SC * 32)], in_sem.at[6]))
    loads.append(pltpu.make_async_copy(cot, craw, in_sem.at[7]))
    loads.append(pltpu.make_async_copy(wst, wspad.at[pl.ds(0, 336)], in_sem.at[8]))
    loads.append(pltpu.make_async_copy(wf, wstage, in_sem.at[9]))
    for copy in loads[:7]:
        copy.start()

    barrier = pltpu.get_barrier_semaphore()
    for peer in peers:
        pl.semaphore_signal(barrier, inc=1, device_id=peer, device_id_type=pl.DeviceIdType.MESH)
    def remote(n, src, dst, peer):
        return pltpu.make_async_remote_copy(
            src_ref=src, dst_ref=dst, send_sem=send.at[n], recv_sem=recv.at[n],
            device_id=peer, device_id_type=pl.DeviceIdType.MESH,
        )

    down, across = iota((512, 1), 0), iota((1, 512), 1)

    def column(lane, late):
        half = lax.shift_right_logical(lane, 8)
        return (2 * lane + (-half if late else half)) & 511

    perm[...] = flag(down == column(across, False))
    permt[...] = flag(column(down, False) == across)
    perm2[...] = flag(down == column(across, True))
    permt2[...] = flag(column(down, True) == across)

    raw[pl.ds((FC + SC) * 32, (CP - FC - SC) * 32), :] = jnp.zeros(((CP - FC - SC) * 32, 512), BF16)
    mask_bf = mask[...].astype(F32).astype(BF16)
    zero16 = jnp.zeros((), BF16)
    lane128 = iota((CP, 128), 1)

    def put_row(parity, slot, channels, both):
        n = both.shape[0]
        lane256 = iota((n, 256), 1)
        even, odd = both[:, :256], both[:, 256:]
        left = jnp.where(lane256 == 0, zero16, pltpu.roll(odd, 1, 1))
        right = jnp.where(lane256 == 255, zero16, pltpu.roll(even, 255, 1))
        for j, part in enumerate((even, odd, left, right)):
            planes[pl.ds((parity * 4 + j) * CP + channels, n), pl.ds(slot * 256, 256)] = part

    lane16 = iota((16, 128), 1)
    for k in range(8):
        if k < 7:
            loads[k].wait()
        if k == 3:
            for copy in loads[7:]:
                copy.start()
        x = raw[pl.ds(k * 512, 512), :].reshape(16, 32, 512) * mask_bf[None]
        y = dot(x.reshape(512, 512), perm[...]).astype(BF16)
        y = jnp.swapaxes(y.reshape(16, 32, 512), 0, 1)
        edge = jnp.zeros((16, 128), BF16)
        for r in range(32):
            put_row(r % 2, r // 2 + r % 2, k * 16, y[r])
            edge = jnp.where(lane16 == r + 1, y[r][:, 0:1], edge)
            edge = jnp.where(lane16 == 65 + r, y[r][:, 511:512], edge)
        sx[pl.ds(k * 16, 16), :] = edge

    pl.semaphore_wait(barrier, len(peers))
    x_north = remote(0, planes.at[pl.ds(512, 512), pl.ds(16 * 256, 256)], rxs, north)
    x_south = remote(1, planes.at[pl.ds(0, 512), pl.ds(0, 256)], rxn, south)
    x_mirror = remote(2, planes.at[pl.ds(512, 256), pl.ds(16 * 256, 256)], rmir, mirror)
    x_north.start()
    x_south.start()

    @pl.when(at_top)
    def _():
        x_mirror.start()

    loads[7].wait()
    clane = iota((512, 128), 1)
    lane32 = iota((32, 128), 1)

    def late(x):
        return jnp.where(iota(x.shape, 1) == 0, zero16, pltpu.roll(x, 1, 1))

    def split_tokens(k, _):
        x = craw[pl.ds(pl.multiple_of(k * 512, 512), 512), :].reshape(32, 16, 256)
        y = jnp.swapaxes(x, 0, 1)
        w = pl.multiple_of(k * 32, 32)
        edge = jnp.zeros((32, 128), BF16)
        for a in range(16):
            cot_a[pl.ds(w, 32), pl.ds(a * 256, 256)] = y[a]
            cot_b[pl.ds((a + 1) * 1024 + w, 32), :] = y[a]
            cot_b[pl.ds((a + 1) * 1024 + 512 + w, 32), :] = late(y[a])
            edge = jnp.where(lane32 == a + 1, y[a][:, 0:1], edge)
            edge = jnp.where(lane32 == 65 + a, y[a][:, 255:256], edge)
        sc[pl.ds(w, 32), :] = edge
        return 0

    lax.fori_loop(0, 16, split_tokens, 0)
    c_north = remote(3, cot_b.at[pl.ds(16 * 1024, 512)], rcs, north)
    c_south = remote(4, cot_b.at[pl.ds(1024, 512)], rcn, south)
    c_north.start()
    c_south.start()

    def tile(n, pair):
        _, parity, off = ROWS[n]
        rows = planes[pl.ds((parity * 4 + pair * 2) * CP, 2 * CP), pl.ds(off * 256, 4096)]
        return dot_nt(cot_a[...], rows)

    orders = ("zxy", "xyz", "yzx")
    recv_a, sum_2 = (ra_z, ra_x, ra_y), (s2_z, s2_x, s2_y)
    recv_b, sum_3 = (rb_z, rb_x, rb_y), (s3_z, s3_x, s3_y)
    recv_c = (rc_z, rc_x, rc_y)

    def part(axis, place):
        every = slice(None)
        if axis == "z":
            return (pl.ds(place, 1), every, every, every, every)
        if axis == "y":
            return (every, every, pl.ds(place, 1), every, every)
        lanes = pl.ds(pl.multiple_of(lax.div(place, 2) * 128, 128), 128)
        return (every, pl.ds(lax.rem(place, 2), 1), every, every, lanes)

    def exchange(axis, src, dst, ss, rs):
        copies = []
        for d in range(1, 4):
            place = lax.rem(spot[axis] + d, 4)
            copies.append(pltpu.make_async_remote_copy(
                src_ref=src(part(axis, place)), dst_ref=dst(d - 1), send_sem=ss(d - 1), recv_sem=rs(d - 1),
                device_id=peer_on(axis, place), device_id_type=pl.DeviceIdType.MESH,
            ))
        return copies

    def core_copy(p):
        return pltpu.make_async_remote_copy(
            src_ref=gbuf.at[p, :, 1 - core], dst_ref=rcore.at[p], send_sem=core_s.at[p], recv_sem=core_r.at[p],
            device_id=other_core, device_id_type=pl.DeviceIdType.MESH,
        )

    def a_copies(p):
        k, slot = p % 3, p // 3
        return exchange(
            orders[k][0], lambda at_part: rcore.at[(p,) + at_part], lambda d: recv_a[k].at[slot, d],
            lambda d: a_s.at[p, d], lambda d: a_r.at[p, d],
        )

    def b_copies(k):
        return exchange(
            orders[k][1], lambda at_part: sum_2[k].at[(slice(None),) + at_part], lambda d: recv_b[k].at[d],
            lambda d: b_s.at[k, d], lambda d: b_r.at[k, d],
        )

    def c_copies(k):
        return exchange(
            orders[k][2], lambda at_part: sum_3[k].at[(slice(None),) + at_part], lambda d: recv_c[k].at[d],
            lambda d: c_s.at[k, d], lambda d: c_r.at[k, d],
        )

    def g_copies():
        return [
            pltpu.make_async_remote_copy(
                src_ref=s4, dst_ref=gathered.at[lon], send_sem=g_s.at[d - 1], recv_sem=g_r.at[d - 1],
                device_id=lon_peer(d), device_id_type=pl.DeviceIdType.MESH,
            )
            for d in range(1, 8)
        ]

    def core_start(p, value):
        gbuf[p] = value.reshape(4, 2, 2, 4, 8, 256)
        core_copy(p).start()

    def a_start(p):
        core_copy(p).wait()
        rcore[p] = rcore[p] + gbuf[p, :, core]
        for copy in a_copies(p):
            copy.start()

    def b_start(k):
        for p in range(k, 8, 3):
            slot = p // 3
            for copy in a_copies(p):
                copy.wait()
            own = rcore[(p,) + part(orders[k][0], spot[orders[k][0]])]
            got = recv_a[k][slot]
            sum_2[k][slot] = own + got[0] + got[1] + got[2]
        for copy in b_copies(k):
            copy.start()

    def c_start(k):
        for copy in b_copies(k):
            copy.wait()
        own = sum_2[k][(slice(None),) + part(orders[k][1], spot[orders[k][1]])]
        got = recv_b[k][...]
        sum_3[k][...] = own + got[0] + got[1] + got[2]
        for copy in c_copies(k):
            copy.start()

    def g_start():
        for k in range(3):
            for copy in c_copies(k):
                copy.wait()
            own = sum_3[k][(slice(None),) + part(orders[k][2], spot[orders[k][2]])]
            got = recv_c[k][...]
            total = own + got[0] + got[1] + got[2]
            for slot in range(total.shape[0]):
                s4[slot * 3 + k] = total[slot, 0, 0, 0]
        for copy in g_copies():
            copy.start()

    fold_sel[...] = flag(down == partner[...] - (lon_n - 1 - lon) * 512)

    def folded(x, before, after):
        x = dot(x, before[...]).astype(BF16)
        x = dot(x, fold_sel[...]).astype(BF16)
        return dot(x, after[...])

    x_north.wait()
    x_south.wait()
    planes[pl.ds(512, 512), pl.ds(0, 256)] = jnp.where(at_bottom, zero16, rxs[...])
    planes[pl.ds(0, 512), pl.ds(16 * 256, 256)] = rxn[...]

    @pl.when(at_top)
    def _():
        x_mirror.wait()
        top = jnp.concatenate([rmir[pl.ds(0, CP), :], rmir[pl.ds(CP, CP), :]], axis=1)
        put_row(0, 16, 0, folded(top, permt, perm).astype(BF16))

    acc = sx[...]
    acc = jnp.where(lane128 == 0, planes[pl.ds(512, CP), pl.ds(0, 128)][:, 0:1], acc)
    acc = jnp.where(lane128 == 64, planes[pl.ds(512 + CP, CP), pl.ds(128, 128)][:, 127:128], acc)
    acc = jnp.where(lane128 == 33, planes[pl.ds(0, CP), pl.ds(16 * 256, 128)][:, 0:1], acc)
    acc = jnp.where(lane128 == 97, planes[pl.ds(CP, CP), pl.ds(16 * 256 + 128, 128)][:, 127:128], acc)
    sx[...] = acc
    x_east = remote(5, sx, rxw, east)
    x_west = remote(6, sx, rxe, west)
    x_east.start()
    x_west.start()

    core_start(0, tile(0, 0))
    core_start(1, tile(1, 0))

    c_north.wait()
    c_south.wait()
    low = jnp.where(at_bottom, zero16, rcs[...])
    high = jnp.where(at_top, zero16, rcn[...])
    for slot, x in ((0, low), (17, high)):
        cot_b[pl.ds(slot * 1024, 512), :] = x
        cot_b[pl.ds(slot * 1024 + 512, 512), :] = late(x)
    acc = sc[...]
    acc = jnp.where(clane == 0, low[:, 0:1], acc)
    acc = jnp.where(clane == 64, low[:, 255:256], acc)
    acc = jnp.where(clane == 17, high[:, 0:1], acc)
    acc = jnp.where(clane == 81, high[:, 255:256], acc)
    sc[...] = acc
    c_east = remote(7, sc, rcw, east)
    c_west = remote(8, sc, rce, west)
    c_east.start()
    c_west.start()

    core_start(2, tile(2, 0))
    core_start(3, tile(3, 0))
    a_start(0)
    x_east.wait()
    x_west.wait()
    side = jnp.concatenate(
        [jnp.where(lane128 >= 64, rxw[...], zero16), jnp.where(lane128 < 64, rxe[...], zero16)], axis=0
    )
    lrow, lcol = iota((128, 128), 0), iota((128, 128), 1)
    for n in range(4):
        i = ROWS[n][0]
        first = (lrow >= 1) & (lrow <= 16) & (lcol == 62 + 2 * lrow + i)
        last = (lrow >= 65) & (lrow <= 80) & (lcol == 2 * lrow - 130 + i)
        spread = jnp.where(first | last, 1.0, 0.0).astype(BF16)
        moved = dot(sc[...], spread).astype(BF16)
        core_start(4 + n, tile(n, 1) + dot_nt(moved, side))
        a_start(1 + n)

    a_start(5)

    loads[8].wait()
    loads[9].wait()
    wspad[pl.ds(336, 48), :] = jnp.zeros((48, 512), BF16)
    pick = flag((lrow & 7) * 16 + lax.shift_right_logical(lrow, 3) == lcol)
    for o in range(16):
        wscr[pl.ds(o * CP + 120, 8), :] = jnp.zeros((8, 512), F32)
    for kb in range(15):
        if kb < 12:
            got = dot_nt(pick, wstage[:, pl.ds(kb * 128, 128)])
        else:
            got = dot(pick, wspad[pl.ds((kb - 12) * 128, 128), :])
        for o in range(16):
            wscr[pl.ds(o * CP + kb * 8, 8), :] = got[o * 8:o * 8 + 8, :]
    for parity in range(2):
        for q in range(2):
            for n, i in enumerate(((3, 1), (2, 0))[parity]):
                for m, j in enumerate(((1, 3), (0, 2))[q]):
                    wcat[pl.ds((parity * 2 + q) * CP, CP), pl.ds((n * 2 + m) * 512, 512)] = wscr[
                        pl.ds((i * 4 + j) * CP, CP), :
                    ].astype(BF16)
    a_start(6)

    c_east.wait()
    c_west.wait()
    for slot in range(18):
        at = (pl.ds(slot * 1024 + 512, 512), pl.ds(0, 128))
        cot_b[at] = jnp.where(clane == 0, rcw[...][:, 64 + slot:65 + slot], cot_b[at])
    last = []
    for parity in range(2):
        w_rows = wcat[pl.ds((parity * 2 + 1) * CP, CP), :]
        total = dot(w_rows[:, :512], rce[...]) + pltpu.roll(dot(w_rows[:, 512:1024], sc[...]), 64, 1)
        total = total + pltpu.roll(dot(w_rows[:, 1024:1536], rce[...]), 127, 1)
        last.append(total + pltpu.roll(dot(w_rows[:, 1536:], sc[...]), 63, 1))

    def token_row(s, parities):
        tokens = cot_b[pl.ds(pl.multiple_of(s * 1024, 1024), 2048), :]
        u = dot(wcat[pl.ds(0, 256 * parities), :], tokens)
        rows = []
        for parity in range(parities):
            even, odd = u[parity * 256:parity * 256 + 128], u[parity * 256 + 128:parity * 256 + 256]
            first = jnp.where(lane128 == 0, pltpu.roll(last[parity], lax.rem(128 - s, 128), 1), odd[:, :128])
            rows.append(jnp.concatenate([even, first, odd[:, 128:]], axis=1))
        return rows

    a_start(7)

    fold, top = token_row(16, 2)
    sfold[...] = fold.astype(BF16)
    top_row[...] = top
    g_mirror = remote(9, sfold, rfold, mirror)

    @pl.when(at_top)
    def _():
        g_mirror.start()

    raw[pl.ds(0, CP), :] = token_row(0, 1)[0].astype(BF16)

    def out_copy(n, first, count):
        return pltpu.make_async_copy(raw.at[pl.ds(first * CP, count * CP)], rows_out.at[pl.ds(first * CP, count * CP)], out_sem.at[n])

    def rows_of(s, _):
        even, odd = token_row(s, 2)
        raw[pl.ds(pl.multiple_of(2 * s * CP, CP), CP), :] = even.astype(BF16)
        raw[pl.ds(pl.multiple_of((2 * s - 1) * CP, CP), CP), :] = odd.astype(BF16)
        for n, k in enumerate((2, 0, 1)):
            pl.when(s == 3 + n)(functools.partial(b_start, k))
            pl.when(s == 8 + n)(functools.partial(c_start, k))
        pl.when(s == 10)(lambda: out_copy(0, 0, 19).start())
        pl.when(s == 14)(g_start)
        return 0

    lax.fori_loop(1, 16, rows_of, 0)
    out_copy(1, 19, 12).start()

    @pl.when(at_top)
    def _():
        g_mirror.wait()
        top_row[...] = top_row[...] + folded(rfold[...], permt2, perm2)

    raw[pl.ds(31 * CP, CP), :] = top_row[...].astype(BF16)
    out_copy(2, 31, 1).start()
    for copy in g_copies():
        copy.wait()
    gathered[lon] = s4[...]
    out_share = pltpu.make_async_copy(gathered, share_out, out_sem.at[3])
    out_share.start()
    for n, first, count in ((0, 0, 19), (1, 19, 12), (2, 31, 1)):
        out_copy(n, first, count).wait()
    out_share.wait()


def last_kernel(scale, share, rows, mask, ks_out, kf_out, xs_out, xf_out, permt2, got, cells, own, ks, kf, in_sem, out_sem):
    loads = [pltpu.make_async_copy(share, own, in_sem.at[8])]
    for k in range(8):
        block = pl.ds(k * 16, 16)
        loads.append(pltpu.make_async_copy(rows.at[:, block], got.at[:, block], in_sem.at[k]))
    for copy in loads:
        copy.start()
    lane, across = iota((512, 1), 0), iota((1, 512), 1)
    permt2[...] = flag(((2 * lane - lax.shift_right_logical(lane, 8)) & 511) == across)
    mask_bf = mask[...].astype(F32).astype(BF16)

    loads[0].wait()
    turned = [None] * 16
    for p in range(8):
        for which in range(2):
            o = ROWS[p % 4][0] * 4 + JORD[p // 4 * 2 + which]
            mine = [own[4 * which + y, p] for y in range(4)] + [jnp.zeros((96, 128), F32)]
            turned[o] = jnp.transpose(jnp.concatenate(mine, axis=0)) * scale
    for n in range(15):
        block = jnp.stack([x[n * 8:n * 8 + 8] for x in turned], axis=0)
        block = jnp.transpose(jnp.swapaxes(block, 0, 1).reshape(128, 128))[:32]
        if n < 12:
            kf[:, pl.ds(n * 128, 128)] = block
        elif n < 14:
            ks[:, pl.ds((n - 12) * 128, 128)] = block
        else:
            ks[:, pl.ds(256, 80)] = block[:, :80]
    stores = [pltpu.make_async_copy(kf, kf_out, out_sem.at[8]), pltpu.make_async_copy(ks, ks_out, out_sem.at[9])]
    for copy in stores:
        copy.start()

    for k in range(8):
        loads[k + 1].wait()
        x = jnp.swapaxes(got[:, pl.ds(k * 16, 16), :], 0, 1).reshape(512, 512)
        y = dot(x, permt2[...]).astype(BF16).reshape(16, 32, 512) * mask_bf[None]
        cells[pl.ds(k * 512, 512), :] = y.reshape(512, 512)
        if k < 6:
            dst, at, count = xf_out, k * 512, 512
        else:
            dst, at, count = xs_out, (k - 6) * 512, 512 if k == 6 else SC * 32 - 512
        copy = pltpu.make_async_copy(cells.at[pl.ds(k * 512, count)], dst.at[pl.ds(at, count)], out_sem.at[k])
        copy.start()
        stores.append(copy)
    for copy in stores:
        copy.wait()


def on_device(state, forcing, land_mask, partner, cotangent, weight_state, weight_force):
    sc, fc = state.shape[1], forcing.shape[1]
    rows, cols = state.shape[2:]
    width = cotangent.shape[1]
    lon_n, lat_n, batch_n = (lax.axis_size(a) for a in ("lon", "lat", "batch"))
    any_spec = pl.BlockSpec(memory_space=pl.ANY)
    vmem = pl.BlockSpec(memory_space=pltpu.VMEM)
    share, cells = pl.pallas_call(
        main_kernel,
        out_shape=(
            jax.ShapeDtypeStruct((8, 8, 8, 128), F32),
            jax.ShapeDtypeStruct((rows * CP, cols), BF16),
        ),
        in_specs=[any_spec, any_spec, vmem, vmem, any_spec, any_spec, any_spec],
        out_specs=(any_spec, any_spec),
        scratch_shapes=[
            pltpu.VMEM((4096, 512), BF16),
            pltpu.VMEM((8 * CP, 17 * 256), BF16),
            pltpu.VMEM((8192, 256), BF16),
            pltpu.VMEM((512, 4096), BF16),
            pltpu.VMEM((18 * 1024, 256), BF16),
            pltpu.VMEM((512, 2048), BF16),
            pltpu.VMEM((2048, 512), F32),
            pltpu.VMEM((8, 4, 2, 2, 4, 8, 256), F32),
            pltpu.VMEM((512, 1536), BF16),
            pltpu.VMEM((384, 512), BF16),
            pltpu.VMEM((512, 512), BF16),
            pltpu.VMEM((512, 512), BF16),
            pltpu.VMEM((512, 512), BF16),
            pltpu.VMEM((512, 512), BF16),
            pltpu.VMEM((512, 512), BF16),
            pltpu.VMEM((CP, 512), F32),
            pltpu.VMEM((512, 256), BF16),
            pltpu.VMEM((512, 256), BF16),
            pltpu.VMEM((256, 256), BF16),
            pltpu.VMEM((512, 256), BF16),
            pltpu.VMEM((512, 256), BF16),
            pltpu.VMEM((CP, 128), BF16),
            pltpu.VMEM((CP, 128), BF16),
            pltpu.VMEM((CP, 128), BF16),
            pltpu.VMEM((512, 128), BF16),
            pltpu.VMEM((512, 128), BF16),
            pltpu.VMEM((512, 128), BF16),
            pltpu.VMEM((CP, 512), BF16),
            pltpu.VMEM((CP, 512), BF16),
            pltpu.VMEM((8, 4, 2, 4, 8, 256), F32),
            pltpu.VMEM((3, 3, 1, 2, 4, 8, 256), F32),
            pltpu.VMEM((3, 3, 4, 1, 4, 8, 128), F32),
            pltpu.VMEM((2, 3, 4, 2, 1, 8, 256), F32),
            pltpu.VMEM((3, 1, 2, 4, 8, 256), F32),
            pltpu.VMEM((3, 4, 1, 4, 8, 128), F32),
            pltpu.VMEM((2, 4, 2, 1, 8, 256), F32),
            pltpu.VMEM((3, 3, 1, 1, 4, 8, 128), F32),
            pltpu.VMEM((3, 3, 4, 1, 1, 8, 128), F32),
            pltpu.VMEM((3, 2, 1, 2, 1, 8, 256), F32),
            pltpu.VMEM((3, 1, 1, 4, 8, 128), F32),
            pltpu.VMEM((3, 4, 1, 1, 8, 128), F32),
            pltpu.VMEM((2, 1, 2, 1, 8, 256), F32),
            pltpu.VMEM((3, 3, 1, 1, 1, 8, 128), F32),
            pltpu.VMEM((3, 3, 1, 1, 1, 8, 128), F32),
            pltpu.VMEM((3, 2, 1, 1, 1, 8, 128), F32),
            pltpu.VMEM((8, 8, 128), F32),
            pltpu.VMEM((8, 8, 8, 128), F32),
            pltpu.SemaphoreType.DMA((10,)),
            pltpu.SemaphoreType.DMA((8,)),
            pltpu.SemaphoreType.DMA((10,)),
            pltpu.SemaphoreType.DMA((10,)),
            pltpu.SemaphoreType.DMA((8,)),
            pltpu.SemaphoreType.DMA((8,)),
            pltpu.SemaphoreType.DMA((8, 3)),
            pltpu.SemaphoreType.DMA((8, 3)),
            pltpu.SemaphoreType.DMA((3, 3)),
            pltpu.SemaphoreType.DMA((3, 3)),
            pltpu.SemaphoreType.DMA((3, 3)),
            pltpu.SemaphoreType.DMA((3, 3)),
            pltpu.SemaphoreType.DMA((7,)),
            pltpu.SemaphoreType.DMA((7,)),
        ],
        compiler_params=pltpu.CompilerParams(
            collective_id=0, has_side_effects=True, vmem_limit_bytes=62 * 1024 * 1024
        ),
        name="encoder_backward",
    )(
        state.reshape(sc * rows, cols), forcing.reshape(fc * rows, cols), land_mask, partner[None, :],
        cotangent.reshape(width * cotangent.shape[2], cotangent.shape[3]), weight_state.T, weight_force,
    )
    scale = 1.0 / math.sqrt(batch_n * (rows // 2) * lat_n * (cols // 2) * lon_n)
    own = width // (lat_n * batch_n)
    ks, kf, xs, xf = pl.pallas_call(
        functools.partial(last_kernel, scale),
        out_shape=(
            jax.ShapeDtypeStruct((own, sc * 16), F32),
            jax.ShapeDtypeStruct((own, fc * 16), F32),
            jax.ShapeDtypeStruct((sc * rows, cols), BF16),
            jax.ShapeDtypeStruct((fc * rows, cols), BF16),
        ),
        in_specs=[any_spec, any_spec, vmem],
        out_specs=(any_spec,) * 4,
        scratch_shapes=[
            pltpu.VMEM((512, 512), BF16),
            pltpu.VMEM((rows, CP, cols), BF16),
            pltpu.VMEM((rows * CP, cols), BF16),
            pltpu.VMEM((8, 8, 8, 128), F32),
            pltpu.VMEM((own, sc * 16), F32),
            pltpu.VMEM((own, fc * 16), F32),
            pltpu.SemaphoreType.DMA((9,)),
            pltpu.SemaphoreType.DMA((10,)),
        ],
        compiler_params=pltpu.CompilerParams(vmem_limit_bytes=62 * 1024 * 1024),
        name="encoder_finish",
    )(share, cells.reshape(rows, CP, cols), land_mask)
    return (
        xs.reshape(state.shape),
        xf.reshape(forcing.shape),
        ks,
        kf,
    )


def solution(mesh):
    in_specs = (
        P("batch", None, "lat", "lon"),
        P("batch", None, "lat", "lon"),
        P("lat", "lon"),
        P("lon"),
        P("batch", None, "lat", "lon"),
        P(),
        P(),
    )
    out_specs = (
        P("batch", None, "lat", "lon"),
        P("batch", None, "lat", "lon"),
        P(("lat", "batch"), None),
        P(("lat", "batch"), None),
    )
    return jax.shard_map(on_device, mesh=mesh, in_specs=in_specs, out_specs=out_specs, check_vma=False)
```

```python
import functools
import math

import jax
import jax.numpy as jnp
from jax import lax
from jax.experimental import pallas as pl
from jax.experimental.pallas import tpu as pltpu
from jax.sharding import PartitionSpec as P

SC = 21
FC = 96
CP = 128
F32 = jnp.float32
BF16 = jnp.bfloat16
JORD = (1, 2, 0, 3)
ROWS = ((1, 0, 0), (2, 1, 1), (0, 1, 0), (3, 0, 1))


def iota(shape, dim):
    return lax.broadcasted_iota(jnp.int32, shape, dim)


def dot(a, b):
    return lax.dot_general(a, b, (((1,), (0,)), ((), ())), preferred_element_type=F32)


def dot_nt(a, b):
    return lax.dot_general(a, b, (((1,), (1,)), ((), ())), preferred_element_type=F32)


def flag(where):
    return jnp.where(where, 1.0, 0.0).astype(BF16)


def main_kernel(
    state, force, mask, partner, cot, wst, wf,
    share_out, rows_out,
    raw, planes, craw, cot_a, cot_b, wcat, wscr, gbuf, wstage, wspad, perm, permt, perm2, permt2, fold_sel, top_row,
    rxs, rxn, rmir, rcs, rcn, sx, rxw, rxe, sc, rcw, rce, sfold, rfold,
    rcore, ra_z, ra_x, ra_y, s2_z, s2_x, s2_y, rb_z, rb_x, rb_y, s3_z, s3_x, s3_y, rc_z, rc_x, rc_y, s4, gathered,
    in_sem, out_sem, send, recv, core_s, core_r, a_s, a_r, b_s, b_r, c_s, c_r, g_s, g_r,
):
    lon_n = lax.axis_size("lon")
    lat_n = lax.axis_size("lat")
    lon = lax.axis_index("lon")
    lat = lax.axis_index("lat")
    at_top = lat == lat_n - 1
    at_bottom = lat == 0
    north = {"lat": lax.rem(lat + 1, lat_n)}
    south = {"lat": lax.rem(lat + lat_n - 1, lat_n)}
    east = {"lon": lax.rem(lon + 1, lon_n)}
    west = {"lon": lax.rem(lon + lon_n - 1, lon_n)}
    mirror = {"lon": lon_n - 1 - lon}
    at_y, at_z, core = lax.rem(lon, 4), lax.div(lat, 2), lax.rem(lat, 2)
    x_lo, x_hi = lax.axis_index("batch"), lax.div(lon, 4)
    spot = {"x": 2 * x_hi + x_lo, "y": at_y, "z": at_z}
    other_core = {"lat": 2 * at_z + 1 - core}

    def peer_on(axis, place):
        if axis == "z":
            return {"lat": 2 * place + core}
        if axis == "y":
            return {"lon": 4 * x_hi + place}
        return {"lon": 4 * lax.div(place, 2) + at_y, "batch": lax.rem(place, 2)}

    def lon_peer(d):
        return {"lon": lax.rem(lon + d, lon_n)}

    peers = [north, south, mirror, other_core] + [lon_peer(d) for d in range(1, 8)]
    for axis in "xyz":
        peers += [peer_on(axis, lax.rem(spot[axis] + d, 4)) for d in range(1, 4)]

    loads = []
    for k in range(6):
        loads.append(pltpu.make_async_copy(force.at[pl.ds(k * 512, 512)], raw.at[pl.ds(k * 512, 512)], in_sem.at[k]))
    loads.append(pltpu.make_async_copy(state, raw.at[pl.ds(FC * 32, SC * 32)], in_sem.at[6]))
    loads.append(pltpu.make_async_copy(cot, craw, in_sem.at[7]))
    loads.append(pltpu.make_async_copy(wst, wspad.at[pl.ds(0, 336)], in_sem.at[8]))
    loads.append(pltpu.make_async_copy(wf, wstage, in_sem.at[9]))
    for copy in loads[:7]:
        copy.start()

    barrier = pltpu.get_barrier_semaphore()
    for peer in peers:
        pl.semaphore_signal(barrier, inc=1, device_id=peer, device_id_type=pl.DeviceIdType.MESH)
    def remote(n, src, dst, peer):
        return pltpu.make_async_remote_copy(
            src_ref=src, dst_ref=dst, send_sem=send.at[n], recv_sem=recv.at[n],
            device_id=peer, device_id_type=pl.DeviceIdType.MESH,
        )

    down, across = iota((512, 1), 0), iota((1, 512), 1)

    def column(lane, late):
        half = lax.shift_right_logical(lane, 8)
        return (2 * lane + (-half if late else half)) & 511

    perm[...] = flag(down == column(across, False))
    permt[...] = flag(column(down, False) == across)
    perm2[...] = flag(down == column(across, True))
    permt2[...] = flag(column(down, True) == across)

    raw[pl.ds((FC + SC) * 32, (CP - FC - SC) * 32), :] = jnp.zeros(((CP - FC - SC) * 32, 512), BF16)
    mask_bf = mask[...].astype(F32).astype(BF16)
    zero16 = jnp.zeros((), BF16)
    lane128 = iota((CP, 128), 1)

    def put_row(parity, slot, channels, both):
        n = both.shape[0]
        lane256 = iota((n, 256), 1)
        even, odd = both[:, :256], both[:, 256:]
        left = jnp.where(lane256 == 0, zero16, pltpu.roll(odd, 1, 1))
        right = jnp.where(lane256 == 255, zero16, pltpu.roll(even, 255, 1))
        for j, part in enumerate((even, odd, left, right)):
            planes[pl.ds((parity * 4 + j) * CP + channels, n), pl.ds(slot * 256, 256)] = part

    lane16 = iota((16, 128), 1)
    for k in range(8):
        if k < 7:
            loads[k].wait()
        if k == 3:
            for copy in loads[7:]:
                copy.start()
        x = raw[pl.ds(k * 512, 512), :].reshape(16, 32, 512) * mask_bf[None]
        y = dot(x.reshape(512, 512), perm[...]).astype(BF16)
        y = jnp.swapaxes(y.reshape(16, 32, 512), 0, 1)
        edge = jnp.zeros((16, 128), BF16)
        for r in range(32):
            put_row(r % 2, r // 2 + r % 2, k * 16, y[r])
            edge = jnp.where(lane16 == r + 1, y[r][:, 0:1], edge)
            edge = jnp.where(lane16 == 65 + r, y[r][:, 511:512], edge)
        sx[pl.ds(k * 16, 16), :] = edge

    pl.semaphore_wait(barrier, len(peers))
    x_north = remote(0, planes.at[pl.ds(512, 512), pl.ds(16 * 256, 256)], rxs, north)
    x_south = remote(1, planes.at[pl.ds(0, 512), pl.ds(0, 256)], rxn, south)
    x_mirror = remote(2, planes.at[pl.ds(512, 256), pl.ds(16 * 256, 256)], rmir, mirror)
    x_north.start()
    x_south.start()

    @pl.when(at_top)
    def _():
        x_mirror.start()

    loads[7].wait()
    clane = iota((512, 128), 1)
    lane32 = iota((32, 128), 1)

    def late(x):
        return jnp.where(iota(x.shape, 1) == 0, zero16, pltpu.roll(x, 1, 1))

    def split_tokens(k, _):
        x = craw[pl.ds(pl.multiple_of(k * 512, 512), 512), :].reshape(32, 16, 256)
        y = jnp.swapaxes(x, 0, 1)
        w = pl.multiple_of(k * 32, 32)
        edge = jnp.zeros((32, 128), BF16)
        for a in range(16):
            cot_a[pl.ds(w, 32), pl.ds(a * 256, 256)] = y[a]
            cot_b[pl.ds((a + 1) * 1024 + w, 32), :] = y[a]
            cot_b[pl.ds((a + 1) * 1024 + 512 + w, 32), :] = late(y[a])
            edge = jnp.where(lane32 == a + 1, y[a][:, 0:1], edge)
            edge = jnp.where(lane32 == 65 + a, y[a][:, 255:256], edge)
        sc[pl.ds(w, 32), :] = edge
        return 0

    lax.fori_loop(0, 16, split_tokens, 0)
    c_north = remote(3, cot_b.at[pl.ds(16 * 1024, 512)], rcs, north)
    c_south = remote(4, cot_b.at[pl.ds(1024, 512)], rcn, south)
    c_north.start()
    c_south.start()

    def tile(n, pair):
        _, parity, off = ROWS[n]
        rows = planes[pl.ds((parity * 4 + pair * 2) * CP, 2 * CP), pl.ds(off * 256, 4096)]
        return dot_nt(cot_a[...], rows)

    orders = ("zxy", "xyz", "yzx")
    recv_a, sum_2 = (ra_z, ra_x, ra_y), (s2_z, s2_x, s2_y)
    recv_b, sum_3 = (rb_z, rb_x, rb_y), (s3_z, s3_x, s3_y)
    recv_c = (rc_z, rc_x, rc_y)

    def part(axis, place):
        every = slice(None)
        if axis == "z":
            return (pl.ds(place, 1), every, every, every, every)
        if axis == "y":
            return (every, every, pl.ds(place, 1), every, every)
        lanes = pl.ds(pl.multiple_of(lax.div(place, 2) * 128, 128), 128)
        return (every, pl.ds(lax.rem(place, 2), 1), every, every, lanes)

    def exchange(axis, src, dst, ss, rs):
        copies = []
        for d in range(1, 4):
            place = lax.rem(spot[axis] + d, 4)
            copies.append(pltpu.make_async_remote_copy(
                src_ref=src(part(axis, place)), dst_ref=dst(d - 1), send_sem=ss(d - 1), recv_sem=rs(d - 1),
                device_id=peer_on(axis, place), device_id_type=pl.DeviceIdType.MESH,
            ))
        return copies

    def core_copy(p):
        return pltpu.make_async_remote_copy(
            src_ref=gbuf.at[p, :, 1 - core], dst_ref=rcore.at[p], send_sem=core_s.at[p], recv_sem=core_r.at[p],
            device_id=other_core, device_id_type=pl.DeviceIdType.MESH,
        )

    def a_copies(p):
        k, slot = p % 3, p // 3
        return exchange(
            orders[k][0], lambda at_part: rcore.at[(p,) + at_part], lambda d: recv_a[k].at[slot, d],
            lambda d: a_s.at[p, d], lambda d: a_r.at[p, d],
        )

    def b_copies(k):
        return exchange(
            orders[k][1], lambda at_part: sum_2[k].at[(slice(None),) + at_part], lambda d: recv_b[k].at[d],
            lambda d: b_s.at[k, d], lambda d: b_r.at[k, d],
        )

    def c_copies(k):
        return exchange(
            orders[k][2], lambda at_part: sum_3[k].at[(slice(None),) + at_part], lambda d: recv_c[k].at[d],
            lambda d: c_s.at[k, d], lambda d: c_r.at[k, d],
        )

    def g_copies():
        return [
            pltpu.make_async_remote_copy(
                src_ref=s4, dst_ref=gathered.at[lon], send_sem=g_s.at[d - 1], recv_sem=g_r.at[d - 1],
                device_id=lon_peer(d), device_id_type=pl.DeviceIdType.MESH,
            )
            for d in range(1, 8)
        ]

    def core_start(p, values):
        for n, value in enumerate(values):
            gbuf[p + n] = value.reshape(4, 2, 2, 4, 8, 256)
        for n in range(len(values)):
            core_copy(p + n).start()

    def a_start(p):
        core_copy(p).wait()
        rcore[p] = rcore[p] + gbuf[p, :, core]
        for copy in a_copies(p):
            copy.start()

    def b_start(k):
        for p in range(k, 8, 3):
            slot = p // 3
            for copy in a_copies(p):
                copy.wait()
            own = rcore[(p,) + part(orders[k][0], spot[orders[k][0]])]
            got = recv_a[k][slot]
            sum_2[k][slot] = own + got[0] + got[1] + got[2]
        for copy in b_copies(k):
            copy.start()

    def c_start(k):
        for copy in b_copies(k):
            copy.wait()
        own = sum_2[k][(slice(None),) + part(orders[k][1], spot[orders[k][1]])]
        got = recv_b[k][...]
        sum_3[k][...] = own + got[0] + got[1] + got[2]
        for copy in c_copies(k):
            copy.start()

    def g_start():
        for k in range(3):
            for copy in c_copies(k):
                copy.wait()
            own = sum_3[k][(slice(None),) + part(orders[k][2], spot[orders[k][2]])]
            got = recv_c[k][...]
            total = own + got[0] + got[1] + got[2]
            for slot in range(total.shape[0]):
                s4[slot * 3 + k] = total[slot, 0, 0, 0]
        for copy in g_copies():
            copy.start()

    fold_sel[...] = flag(down == partner[...] - (lon_n - 1 - lon) * 512)

    def folded(x, before, after):
        x = dot(x, before[...]).astype(BF16)
        x = dot(x, fold_sel[...]).astype(BF16)
        return dot(x, after[...])

    x_north.wait()
    x_south.wait()
    planes[pl.ds(512, 512), pl.ds(0, 256)] = jnp.where(at_bottom, zero16, rxs[...])
    planes[pl.ds(0, 512), pl.ds(16 * 256, 256)] = rxn[...]

    @pl.when(at_top)
    def _():
        x_mirror.wait()
        top = jnp.concatenate([rmir[pl.ds(0, CP), :], rmir[pl.ds(CP, CP), :]], axis=1)
        put_row(0, 16, 0, folded(top, permt, perm).astype(BF16))

    acc = sx[...]
    acc = jnp.where(lane128 == 0, planes[pl.ds(512, CP), pl.ds(0, 128)][:, 0:1], acc)
    acc = jnp.where(lane128 == 64, planes[pl.ds(512 + CP, CP), pl.ds(128, 128)][:, 127:128], acc)
    acc = jnp.where(lane128 == 33, planes[pl.ds(0, CP), pl.ds(16 * 256, 128)][:, 0:1], acc)
    acc = jnp.where(lane128 == 97, planes[pl.ds(CP, CP), pl.ds(16 * 256 + 128, 128)][:, 127:128], acc)
    sx[...] = acc
    x_east = remote(5, sx, rxw, east)
    x_west = remote(6, sx, rxe, west)
    x_east.start()
    x_west.start()

    core_start(0, [tile(0, 0), tile(1, 0)])

    c_north.wait()
    c_south.wait()
    low = jnp.where(at_bottom, zero16, rcs[...])
    high = jnp.where(at_top, zero16, rcn[...])
    for slot, x in ((0, low), (17, high)):
        cot_b[pl.ds(slot * 1024, 512), :] = x
        cot_b[pl.ds(slot * 1024 + 512, 512), :] = late(x)
    acc = sc[...]
    acc = jnp.where(clane == 0, low[:, 0:1], acc)
    acc = jnp.where(clane == 64, low[:, 255:256], acc)
    acc = jnp.where(clane == 17, high[:, 0:1], acc)
    acc = jnp.where(clane == 81, high[:, 255:256], acc)
    sc[...] = acc
    c_east = remote(7, sc, rcw, east)
    c_west = remote(8, sc, rce, west)
    c_east.start()
    c_west.start()

    core_start(2, [tile(2, 0), tile(3, 0)])
    a_start(0)
    a_start(1)
    x_east.wait()
    x_west.wait()
    side = jnp.concatenate(
        [jnp.where(lane128 >= 64, rxw[...], zero16), jnp.where(lane128 < 64, rxe[...], zero16)], axis=0
    )
    lrow, lcol = iota((128, 128), 0), iota((128, 128), 1)

    def side_tile(n):
        i = ROWS[n][0]
        first = (lrow >= 1) & (lrow <= 16) & (lcol == 62 + 2 * lrow + i)
        last = (lrow >= 65) & (lrow <= 80) & (lcol == 2 * lrow - 130 + i)
        moved = dot(sc[...], flag(first | last)).astype(BF16)
        return tile(n, 1) + dot_nt(moved, side)

    core_start(4, [side_tile(0), side_tile(1)])
    a_start(2)
    a_start(3)
    core_start(6, [side_tile(2), side_tile(3)])
    a_start(4)
    a_start(5)

    loads[8].wait()
    loads[9].wait()
    wspad[pl.ds(336, 48), :] = jnp.zeros((48, 512), BF16)
    pick = flag((lrow & 7) * 16 + lax.shift_right_logical(lrow, 3) == lcol)
    for o in range(16):
        wscr[pl.ds(o * CP + 120, 8), :] = jnp.zeros((8, 512), F32)
    for kb in range(15):
        if kb < 12:
            got = dot_nt(pick, wstage[:, pl.ds(kb * 128, 128)])
        else:
            got = dot(pick, wspad[pl.ds((kb - 12) * 128, 128), :])
        for o in range(16):
            wscr[pl.ds(o * CP + kb * 8, 8), :] = got[o * 8:o * 8 + 8, :]
    for parity in range(2):
        for q in range(2):
            for n, i in enumerate(((3, 1), (2, 0))[parity]):
                for m, j in enumerate(((1, 3), (0, 2))[q]):
                    wcat[pl.ds((parity * 2 + q) * CP, CP), pl.ds((n * 2 + m) * 512, 512)] = wscr[
                        pl.ds((i * 4 + j) * CP, CP), :
                    ].astype(BF16)
    a_start(6)
    a_start(7)

    c_east.wait()
    c_west.wait()
    for slot in range(18):
        at = (pl.ds(slot * 1024 + 512, 512), pl.ds(0, 128))
        cot_b[at] = jnp.where(clane == 0, rcw[...][:, 64 + slot:65 + slot], cot_b[at])
    last = []
    for parity in range(2):
        w_rows = wcat[pl.ds((parity * 2 + 1) * CP, CP), :]
        total = dot(w_rows[:, :512], rce[...]) + pltpu.roll(dot(w_rows[:, 512:1024], sc[...]), 64, 1)
        total = total + pltpu.roll(dot(w_rows[:, 1024:1536], rce[...]), 127, 1)
        last.append(total + pltpu.roll(dot(w_rows[:, 1536:], sc[...]), 63, 1))

    def token_row(s, parities):
        tokens = cot_b[pl.ds(pl.multiple_of(s * 1024, 1024), 2048), :]
        u = dot(wcat[pl.ds(0, 256 * parities), :], tokens)
        rows = []
        for parity in range(parities):
            even, odd = u[parity * 256:parity * 256 + 128], u[parity * 256 + 128:parity * 256 + 256]
            first = jnp.where(lane128 == 0, pltpu.roll(last[parity], lax.rem(128 - s, 128), 1), odd[:, :128])
            rows.append(jnp.concatenate([even, first, odd[:, 128:]], axis=1))
        return rows

    fold, top = token_row(16, 2)
    sfold[...] = fold.astype(BF16)
    top_row[...] = top
    g_mirror = remote(9, sfold, rfold, mirror)

    @pl.when(at_top)
    def _():
        g_mirror.start()

    raw[pl.ds(0, CP), :] = token_row(0, 1)[0].astype(BF16)

    def out_copy(n, first, count):
        return pltpu.make_async_copy(raw.at[pl.ds(first * CP, count * CP)], rows_out.at[pl.ds(first * CP, count * CP)], out_sem.at[n])

    def rows_of(s, _):
        even, odd = token_row(s, 2)
        raw[pl.ds(pl.multiple_of(2 * s * CP, CP), CP), :] = even.astype(BF16)
        raw[pl.ds(pl.multiple_of((2 * s - 1) * CP, CP), CP), :] = odd.astype(BF16)
        for n, k in enumerate((2, 0, 1)):
            pl.when(s == 3 + n)(functools.partial(b_start, k))
            pl.when(s == 8 + n)(functools.partial(c_start, k))
        pl.when(s == 10)(lambda: out_copy(0, 0, 19).start())
        pl.when(s == 14)(g_start)
        return 0

    lax.fori_loop(1, 16, rows_of, 0)
    out_copy(1, 19, 12).start()

    @pl.when(at_top)
    def _():
        g_mirror.wait()
        top_row[...] = top_row[...] + folded(rfold[...], permt2, perm2)

    raw[pl.ds(31 * CP, CP), :] = top_row[...].astype(BF16)
    out_copy(2, 31, 1).start()
    for copy in g_copies():
        copy.wait()
    gathered[lon] = s4[...]
    out_share = pltpu.make_async_copy(gathered, share_out, out_sem.at[3])
    out_share.start()
    for n, first, count in ((0, 0, 19), (1, 19, 12), (2, 31, 1)):
        out_copy(n, first, count).wait()
    out_share.wait()


def last_kernel(scale, share, rows, mask, ks_out, kf_out, xs_out, xf_out, permt2, got, cells, own, ks, kf, in_sem, out_sem):
    loads = [pltpu.make_async_copy(share, own, in_sem.at[8])]
    for k in range(8):
        block = pl.ds(k * 16, 16)
        loads.append(pltpu.make_async_copy(rows.at[:, block], got.at[:, block], in_sem.at[k]))
    for copy in loads:
        copy.start()
    lane, across = iota((512, 1), 0), iota((1, 512), 1)
    permt2[...] = flag(((2 * lane - lax.shift_right_logical(lane, 8)) & 511) == across)
    mask_bf = mask[...].astype(F32).astype(BF16)

    loads[0].wait()
    turned = [None] * 16
    for p in range(8):
        for which in range(2):
            o = ROWS[p % 4][0] * 4 + JORD[p // 4 * 2 + which]
            mine = [own[4 * which + y, p] for y in range(4)] + [jnp.zeros((96, 128), F32)]
            turned[o] = jnp.transpose(jnp.concatenate(mine, axis=0)) * scale
    for n in range(15):
        block = jnp.stack([x[n * 8:n * 8 + 8] for x in turned], axis=0)
        block = jnp.transpose(jnp.swapaxes(block, 0, 1).reshape(128, 128))[:32]
        if n < 12:
            kf[:, pl.ds(n * 128, 128)] = block
        elif n < 14:
            ks[:, pl.ds((n - 12) * 128, 128)] = block
        else:
            ks[:, pl.ds(256, 80)] = block[:, :80]
    stores = [pltpu.make_async_copy(kf, kf_out, out_sem.at[8]), pltpu.make_async_copy(ks, ks_out, out_sem.at[9])]
    for copy in stores:
        copy.start()

    for k in range(8):
        loads[k + 1].wait()
        x = jnp.swapaxes(got[:, pl.ds(k * 16, 16), :], 0, 1).reshape(512, 512)
        y = dot(x, permt2[...]).astype(BF16).reshape(16, 32, 512) * mask_bf[None]
        cells[pl.ds(k * 512, 512), :] = y.reshape(512, 512)
        if k < 6:
            dst, at, count = xf_out, k * 512, 512
        else:
            dst, at, count = xs_out, (k - 6) * 512, 512 if k == 6 else SC * 32 - 512
        copy = pltpu.make_async_copy(cells.at[pl.ds(k * 512, count)], dst.at[pl.ds(at, count)], out_sem.at[k])
        copy.start()
        stores.append(copy)
    for copy in stores:
        copy.wait()


def on_device(state, forcing, land_mask, partner, cotangent, weight_state, weight_force):
    sc, fc = state.shape[1], forcing.shape[1]
    rows, cols = state.shape[2:]
    width = cotangent.shape[1]
    lon_n, lat_n, batch_n = (lax.axis_size(a) for a in ("lon", "lat", "batch"))
    any_spec = pl.BlockSpec(memory_space=pl.ANY)
    vmem = pl.BlockSpec(memory_space=pltpu.VMEM)
    share, cells = pl.pallas_call(
        main_kernel,
        out_shape=(
            jax.ShapeDtypeStruct((8, 8, 8, 128), F32),
            jax.ShapeDtypeStruct((rows * CP, cols), BF16),
        ),
        in_specs=[any_spec, any_spec, vmem, vmem, any_spec, any_spec, any_spec],
        out_specs=(any_spec, any_spec),
        scratch_shapes=[
            pltpu.VMEM((4096, 512), BF16),
            pltpu.VMEM((8 * CP, 17 * 256), BF16),
            pltpu.VMEM((8192, 256), BF16),
            pltpu.VMEM((512, 4096), BF16),
            pltpu.VMEM((18 * 1024, 256), BF16),
            pltpu.VMEM((512, 2048), BF16),
            pltpu.VMEM((2048, 512), F32),
            pltpu.VMEM((8, 4, 2, 2, 4, 8, 256), F32),
            pltpu.VMEM((512, 1536), BF16),
            pltpu.VMEM((384, 512), BF16),
            pltpu.VMEM((512, 512), BF16),
            pltpu.VMEM((512, 512), BF16),
            pltpu.VMEM((512, 512), BF16),
            pltpu.VMEM((512, 512), BF16),
            pltpu.VMEM((512, 512), BF16),
            pltpu.VMEM((CP, 512), F32),
            pltpu.VMEM((512, 256), BF16),
            pltpu.VMEM((512, 256), BF16),
            pltpu.VMEM((256, 256), BF16),
            pltpu.VMEM((512, 256), BF16),
            pltpu.VMEM((512, 256), BF16),
            pltpu.VMEM((CP, 128), BF16),
            pltpu.VMEM((CP, 128), BF16),
            pltpu.VMEM((CP, 128), BF16),
            pltpu.VMEM((512, 128), BF16),
            pltpu.VMEM((512, 128), BF16),
            pltpu.VMEM((512, 128), BF16),
            pltpu.VMEM((CP, 512), BF16),
            pltpu.VMEM((CP, 512), BF16),
            pltpu.VMEM((8, 4, 2, 4, 8, 256), F32),
            pltpu.VMEM((3, 3, 1, 2, 4, 8, 256), F32),
            pltpu.VMEM((3, 3, 4, 1, 4, 8, 128), F32),
            pltpu.VMEM((2, 3, 4, 2, 1, 8, 256), F32),
            pltpu.VMEM((3, 1, 2, 4, 8, 256), F32),
            pltpu.VMEM((3, 4, 1, 4, 8, 128), F32),
            pltpu.VMEM((2, 4, 2, 1, 8, 256), F32),
            pltpu.VMEM((3, 3, 1, 1, 4, 8, 128), F32),
            pltpu.VMEM((3, 3, 4, 1, 1, 8, 128), F32),
            pltpu.VMEM((3, 2, 1, 2, 1, 8, 256), F32),
            pltpu.VMEM((3, 1, 1, 4, 8, 128), F32),
            pltpu.VMEM((3, 4, 1, 1, 8, 128), F32),
            pltpu.VMEM((2, 1, 2, 1, 8, 256), F32),
            pltpu.VMEM((3, 3, 1, 1, 1, 8, 128), F32),
            pltpu.VMEM((3, 3, 1, 1, 1, 8, 128), F32),
            pltpu.VMEM((3, 2, 1, 1, 1, 8, 128), F32),
            pltpu.VMEM((8, 8, 128), F32),
            pltpu.VMEM((8, 8, 8, 128), F32),
            pltpu.SemaphoreType.DMA((10,)),
            pltpu.SemaphoreType.DMA((8,)),
            pltpu.SemaphoreType.DMA((10,)),
            pltpu.SemaphoreType.DMA((10,)),
            pltpu.SemaphoreType.DMA((8,)),
            pltpu.SemaphoreType.DMA((8,)),
            pltpu.SemaphoreType.DMA((8, 3)),
            pltpu.SemaphoreType.DMA((8, 3)),
            pltpu.SemaphoreType.DMA((3, 3)),
            pltpu.SemaphoreType.DMA((3, 3)),
            pltpu.SemaphoreType.DMA((3, 3)),
            pltpu.SemaphoreType.DMA((3, 3)),
            pltpu.SemaphoreType.DMA((7,)),
            pltpu.SemaphoreType.DMA((7,)),
        ],
        compiler_params=pltpu.CompilerParams(
            collective_id=0, has_side_effects=True, vmem_limit_bytes=62 * 1024 * 1024
        ),
        name="encoder_backward",
    )(
        state.reshape(sc * rows, cols), forcing.reshape(fc * rows, cols), land_mask, partner[None, :],
        cotangent.reshape(width * cotangent.shape[2], cotangent.shape[3]), weight_state.T, weight_force,
    )
    scale = 1.0 / math.sqrt(batch_n * (rows // 2) * lat_n * (cols // 2) * lon_n)
    own = width // (lat_n * batch_n)
    ks, kf, xs, xf = pl.pallas_call(
        functools.partial(last_kernel, scale),
        out_shape=(
            jax.ShapeDtypeStruct((own, sc * 16), F32),
            jax.ShapeDtypeStruct((own, fc * 16), F32),
            jax.ShapeDtypeStruct((sc * rows, cols), BF16),
            jax.ShapeDtypeStruct((fc * rows, cols), BF16),
        ),
        in_specs=[any_spec, any_spec, vmem],
        out_specs=(any_spec,) * 4,
        scratch_shapes=[
            pltpu.VMEM((512, 512), BF16),
            pltpu.VMEM((rows, CP, cols), BF16),
            pltpu.VMEM((rows * CP, cols), BF16),
            pltpu.VMEM((8, 8, 8, 128), F32),
            pltpu.VMEM((own, sc * 16), F32),
            pltpu.VMEM((own, fc * 16), F32),
            pltpu.SemaphoreType.DMA((9,)),
            pltpu.SemaphoreType.DMA((10,)),
        ],
        compiler_params=pltpu.CompilerParams(vmem_limit_bytes=62 * 1024 * 1024),
        name="encoder_finish",
    )(share, cells.reshape(rows, CP, cols), land_mask)
    return (
        xs.reshape(state.shape),
        xf.reshape(forcing.shape),
        ks,
        kf,
    )


def solution(mesh):
    in_specs = (
        P("batch", None, "lat", "lon"),
        P("batch", None, "lat", "lon"),
        P("lat", "lon"),
        P("lon"),
        P("batch", None, "lat", "lon"),
        P(),
        P(),
    )
    out_specs = (
        P("batch", None, "lat", "lon"),
        P("batch", None, "lat", "lon"),
        P(("lat", "batch"), None),
        P(("lat", "batch"), None),
    )
    return jax.shard_map(on_device, mesh=mesh, in_specs=in_specs, out_specs=out_specs, check_vma=False)
```

```python
import functools
import math

import jax
import jax.numpy as jnp
from jax import lax
from jax.experimental import pallas as pl
from jax.experimental.pallas import tpu as pltpu
from jax.sharding import PartitionSpec as P

SC = 21
FC = 96
CP = 128
F32 = jnp.float32
BF16 = jnp.bfloat16
JORD = (1, 2, 0, 3)
ROWS = ((1, 0, 0), (2, 1, 1), (0, 1, 0), (3, 0, 1))


def iota(shape, dim):
    return lax.broadcasted_iota(jnp.int32, shape, dim)


def dot(a, b):
    return lax.dot_general(a, b, (((1,), (0,)), ((), ())), preferred_element_type=F32)


def dot_nt(a, b):
    return lax.dot_general(a, b, (((1,), (1,)), ((), ())), preferred_element_type=F32)


def flag(where):
    return jnp.where(where, 1.0, 0.0).astype(BF16)


def main_kernel(
    state, force, mask, partner, cot, wst, wf,
    share_out, rows_out,
    raw, planes, craw, cot_a, cot_b, wcat, wscr, gbuf, wstage, wspad, perm, permt, perm2, permt2, fold_sel, top_row,
    rxs, rxn, rmir, rcs, rcn, sx, rxw, rxe, sc, rcw, rce, sfold, rfold,
    rcore, ra_z, ra_x, ra_y, s2_z, s2_x, s2_y, rb_z, rb_x, rb_y, s3_z, s3_x, s3_y, rc_z, rc_x, rc_y, s4, gathered,
    in_sem, out_sem, send, recv, core_s, core_r, a_s, a_r, b_s, b_r, c_s, c_r, g_s, g_r,
):
    lon_n = lax.axis_size("lon")
    lat_n = lax.axis_size("lat")
    lon = lax.axis_index("lon")
    lat = lax.axis_index("lat")
    at_top = lat == lat_n - 1
    at_bottom = lat == 0
    north = {"lat": lax.rem(lat + 1, lat_n)}
    south = {"lat": lax.rem(lat + lat_n - 1, lat_n)}
    east = {"lon": lax.rem(lon + 1, lon_n)}
    west = {"lon": lax.rem(lon + lon_n - 1, lon_n)}
    mirror = {"lon": lon_n - 1 - lon}
    at_y, at_z, core = lax.rem(lon, 4), lax.div(lat, 2), lax.rem(lat, 2)
    x_lo, x_hi = lax.axis_index("batch"), lax.div(lon, 4)
    spot = {"x": 2 * x_hi + x_lo, "y": at_y, "z": at_z}
    other_core = {"lat": 2 * at_z + 1 - core}

    def peer_on(axis, place):
        if axis == "z":
            return {"lat": 2 * place + core}
        if axis == "y":
            return {"lon": 4 * x_hi + place}
        return {"lon": 4 * lax.div(place, 2) + at_y, "batch": lax.rem(place, 2)}

    def lon_peer(d):
        return {"lon": lax.rem(lon + d, lon_n)}

    peers = [north, south, mirror, other_core] + [lon_peer(d) for d in range(1, 8)]
    for axis in "xyz":
        peers += [peer_on(axis, lax.rem(spot[axis] + d, 4)) for d in range(1, 4)]

    loads = []
    for k in range(6):
        loads.append(pltpu.make_async_copy(force.at[pl.ds(k * 512, 512)], raw.at[pl.ds(k * 512, 512)], in_sem.at[k]))
    loads.append(pltpu.make_async_copy(state, raw.at[pl.ds(FC * 32, SC * 32)], in_sem.at[6]))
    loads.append(pltpu.make_async_copy(cot, craw, in_sem.at[7]))
    loads.append(pltpu.make_async_copy(wst, wspad.at[pl.ds(0, 336)], in_sem.at[8]))
    loads.append(pltpu.make_async_copy(wf, wstage, in_sem.at[9]))
    for copy in loads[:7]:
        copy.start()

    barrier = pltpu.get_barrier_semaphore()
    for peer in peers:
        pl.semaphore_signal(barrier, inc=1, device_id=peer, device_id_type=pl.DeviceIdType.MESH)
    def remote(n, src, dst, peer):
        return pltpu.make_async_remote_copy(
            src_ref=src, dst_ref=dst, send_sem=send.at[n], recv_sem=recv.at[n],
            device_id=peer, device_id_type=pl.DeviceIdType.MESH,
        )

    down, across = iota((512, 1), 0), iota((1, 512), 1)

    def column(lane, late):
        half = lax.shift_right_logical(lane, 8)
        return (2 * lane + (-half if late else half)) & 511

    perm[...] = flag(down == column(across, False))
    permt[...] = flag(column(down, False) == across)
    perm2[...] = flag(down == column(across, True))
    permt2[...] = flag(column(down, True) == across)

    raw[pl.ds((FC + SC) * 32, (CP - FC - SC) * 32), :] = jnp.zeros(((CP - FC - SC) * 32, 512), BF16)
    mask_bf = mask[...].astype(F32).astype(BF16)
    zero16 = jnp.zeros((), BF16)
    lane128 = iota((CP, 128), 1)

    def put_row(parity, slot, channels, both):
        n = both.shape[0]
        lane256 = iota((n, 256), 1)
        even, odd = both[:, :256], both[:, 256:]
        left = jnp.where(lane256 == 0, zero16, pltpu.roll(odd, 1, 1))
        right = jnp.where(lane256 == 255, zero16, pltpu.roll(even, 255, 1))
        for j, part in enumerate((even, odd, left, right)):
            planes[pl.ds((parity * 4 + j) * CP + channels, n), pl.ds(slot * 256, 256)] = part

    lane16 = iota((16, 128), 1)
    for k in range(8):
        if k % 2 == 0:
            for copy in loads[k:min(k + 2, 7)]:
                copy.wait()
        if k == 4:
            for copy in loads[7:]:
                copy.start()
        x = raw[pl.ds(k * 512, 512), :].reshape(16, 32, 512) * mask_bf[None]
        y = dot(x.reshape(512, 512), perm[...]).astype(BF16)
        y = jnp.swapaxes(y.reshape(16, 32, 512), 0, 1)
        edge = jnp.zeros((16, 128), BF16)
        for r in range(32):
            put_row(r % 2, r // 2 + r % 2, k * 16, y[r])
            edge = jnp.where(lane16 == r + 1, y[r][:, 0:1], edge)
            edge = jnp.where(lane16 == 65 + r, y[r][:, 511:512], edge)
        sx[pl.ds(k * 16, 16), :] = edge

    pl.semaphore_wait(barrier, len(peers))
    x_north = remote(0, planes.at[pl.ds(512, 512), pl.ds(16 * 256, 256)], rxs, north)
    x_south = remote(1, planes.at[pl.ds(0, 512), pl.ds(0, 256)], rxn, south)
    x_mirror = remote(2, planes.at[pl.ds(512, 256), pl.ds(16 * 256, 256)], rmir, mirror)
    x_north.start()
    x_south.start()

    @pl.when(at_top)
    def _():
        x_mirror.start()

    loads[7].wait()
    clane = iota((512, 128), 1)
    lane32 = iota((32, 128), 1)

    def late(x):
        return jnp.where(iota(x.shape, 1) == 0, zero16, pltpu.roll(x, 1, 1))

    def split_tokens(k, _):
        x = craw[pl.ds(pl.multiple_of(k * 512, 512), 512), :].reshape(32, 16, 256)
        y = jnp.swapaxes(x, 0, 1)
        w = pl.multiple_of(k * 32, 32)
        edge = jnp.zeros((32, 128), BF16)
        for a in range(16):
            cot_a[pl.ds(w, 32), pl.ds(a * 256, 256)] = y[a]
            cot_b[pl.ds((a + 1) * 1024 + w, 32), :] = y[a]
            cot_b[pl.ds((a + 1) * 1024 + 512 + w, 32), :] = late(y[a])
            edge = jnp.where(lane32 == a + 1, y[a][:, 0:1], edge)
            edge = jnp.where(lane32 == 65 + a, y[a][:, 255:256], edge)
        sc[pl.ds(w, 32), :] = edge
        return 0

    lax.fori_loop(0, 16, split_tokens, 0)
    c_north = remote(3, cot_b.at[pl.ds(16 * 1024, 512)], rcs, north)
    c_south = remote(4, cot_b.at[pl.ds(1024, 512)], rcn, south)
    c_north.start()
    c_south.start()

    def tile(n, pair):
        _, parity, off = ROWS[n]
        rows = planes[pl.ds((parity * 4 + pair * 2) * CP, 2 * CP), pl.ds(off * 256, 4096)]
        return dot_nt(cot_a[...], rows)

    orders = ("zxy", "xyz", "yzx")
    recv_a, sum_2 = (ra_z, ra_x, ra_y), (s2_z, s2_x, s2_y)
    recv_b, sum_3 = (rb_z, rb_x, rb_y), (s3_z, s3_x, s3_y)
    recv_c = (rc_z, rc_x, rc_y)

    def part(axis, place):
        every = slice(None)
        if axis == "z":
            return (pl.ds(place, 1), every, every, every, every)
        if axis == "y":
            return (every, every, pl.ds(place, 1), every, every)
        lanes = pl.ds(pl.multiple_of(lax.div(place, 2) * 128, 128), 128)
        return (every, pl.ds(lax.rem(place, 2), 1), every, every, lanes)

    def exchange(axis, src, dst, ss, rs):
        copies = []
        for d in range(1, 4):
            place = lax.rem(spot[axis] + d, 4)
            copies.append(pltpu.make_async_remote_copy(
                src_ref=src(part(axis, place)), dst_ref=dst(d - 1), send_sem=ss(d - 1), recv_sem=rs(d - 1),
                device_id=peer_on(axis, place), device_id_type=pl.DeviceIdType.MESH,
            ))
        return copies

    def core_copy(p):
        return pltpu.make_async_remote_copy(
            src_ref=gbuf.at[p, :, 1 - core], dst_ref=rcore.at[p], send_sem=core_s.at[p], recv_sem=core_r.at[p],
            device_id=other_core, device_id_type=pl.DeviceIdType.MESH,
        )

    def a_copies(p):
        k, slot = p % 3, p // 3
        return exchange(
            orders[k][0], lambda at_part: rcore.at[(p,) + at_part], lambda d: recv_a[k].at[slot, d],
            lambda d: a_s.at[p, d], lambda d: a_r.at[p, d],
        )

    def b_copies(k):
        return exchange(
            orders[k][1], lambda at_part: sum_2[k].at[(slice(None),) + at_part], lambda d: recv_b[k].at[d],
            lambda d: b_s.at[k, d], lambda d: b_r.at[k, d],
        )

    def c_copies(k):
        return exchange(
            orders[k][2], lambda at_part: sum_3[k].at[(slice(None),) + at_part], lambda d: recv_c[k].at[d],
            lambda d: c_s.at[k, d], lambda d: c_r.at[k, d],
        )

    def g_copies():
        return [
            pltpu.make_async_remote_copy(
                src_ref=s4, dst_ref=gathered.at[lon], send_sem=g_s.at[d - 1], recv_sem=g_r.at[d - 1],
                device_id=lon_peer(d), device_id_type=pl.DeviceIdType.MESH,
            )
            for d in range(1, 8)
        ]

    def core_start(p, values):
        for n, value in enumerate(values):
            gbuf[p + n] = value.reshape(4, 2, 2, 4, 8, 256)
        for n in range(len(values)):
            core_copy(p + n).start()

    def a_start(p):
        core_copy(p).wait()
        rcore[p] = rcore[p] + gbuf[p, :, core]
        for copy in a_copies(p):
            copy.start()

    def b_start(k):
        for p in range(k, 8, 3):
            slot = p // 3
            for copy in a_copies(p):
                copy.wait()
            own = rcore[(p,) + part(orders[k][0], spot[orders[k][0]])]
            got = recv_a[k][slot]
            sum_2[k][slot] = own + got[0] + got[1] + got[2]
        for copy in b_copies(k):
            copy.start()

    def c_start(k):
        for copy in b_copies(k):
            copy.wait()
        own = sum_2[k][(slice(None),) + part(orders[k][1], spot[orders[k][1]])]
        got = recv_b[k][...]
        sum_3[k][...] = own + got[0] + got[1] + got[2]
        for copy in c_copies(k):
            copy.start()

    def g_start():
        for k in range(3):
            for copy in c_copies(k):
                copy.wait()
            own = sum_3[k][(slice(None),) + part(orders[k][2], spot[orders[k][2]])]
            got = recv_c[k][...]
            total = own + got[0] + got[1] + got[2]
            for slot in range(total.shape[0]):
                s4[slot * 3 + k] = total[slot, 0, 0, 0]
        for copy in g_copies():
            copy.start()

    fold_sel[...] = flag(down == partner[...] - (lon_n - 1 - lon) * 512)

    def folded(x, before, after):
        x = dot(x, before[...]).astype(BF16)
        x = dot(x, fold_sel[...]).astype(BF16)
        return dot(x, after[...])

    x_north.wait()
    x_south.wait()
    planes[pl.ds(512, 512), pl.ds(0, 256)] = jnp.where(at_bottom, zero16, rxs[...])
    planes[pl.ds(0, 512), pl.ds(16 * 256, 256)] = rxn[...]

    @pl.when(at_top)
    def _():
        x_mirror.wait()
        top = jnp.concatenate([rmir[pl.ds(0, CP), :], rmir[pl.ds(CP, CP), :]], axis=1)
        put_row(0, 16, 0, folded(top, permt, perm).astype(BF16))

    acc = sx[...]
    acc = jnp.where(lane128 == 0, planes[pl.ds(512, CP), pl.ds(0, 128)][:, 0:1], acc)
    acc = jnp.where(lane128 == 64, planes[pl.ds(512 + CP, CP), pl.ds(128, 128)][:, 127:128], acc)
    acc = jnp.where(lane128 == 33, planes[pl.ds(0, CP), pl.ds(16 * 256, 128)][:, 0:1], acc)
    acc = jnp.where(lane128 == 97, planes[pl.ds(CP, CP), pl.ds(16 * 256 + 128, 128)][:, 127:128], acc)
    sx[...] = acc
    x_east = remote(5, sx, rxw, east)
    x_west = remote(6, sx, rxe, west)
    x_east.start()
    x_west.start()

    core_start(0, [tile(0, 0), tile(1, 0)])

    c_north.wait()
    c_south.wait()
    low = jnp.where(at_bottom, zero16, rcs[...])
    high = jnp.where(at_top, zero16, rcn[...])
    for slot, x in ((0, low), (17, high)):
        cot_b[pl.ds(slot * 1024, 512), :] = x
        cot_b[pl.ds(slot * 1024 + 512, 512), :] = late(x)
    acc = sc[...]
    acc = jnp.where(clane == 0, low[:, 0:1], acc)
    acc = jnp.where(clane == 64, low[:, 255:256], acc)
    acc = jnp.where(clane == 17, high[:, 0:1], acc)
    acc = jnp.where(clane == 81, high[:, 255:256], acc)
    sc[...] = acc
    c_east = remote(7, sc, rcw, east)
    c_west = remote(8, sc, rce, west)
    c_east.start()
    c_west.start()

    core_start(2, [tile(2, 0), tile(3, 0)])
    a_start(0)
    a_start(1)
    x_east.wait()
    x_west.wait()
    side = jnp.concatenate(
        [jnp.where(lane128 >= 64, rxw[...], zero16), jnp.where(lane128 < 64, rxe[...], zero16)], axis=0
    )
    lrow, lcol = iota((128, 128), 0), iota((128, 128), 1)

    def side_tile(n):
        i = ROWS[n][0]
        first = (lrow >= 1) & (lrow <= 16) & (lcol == 62 + 2 * lrow + i)
        last = (lrow >= 65) & (lrow <= 80) & (lcol == 2 * lrow - 130 + i)
        moved = dot(sc[...], flag(first | last)).astype(BF16)
        return tile(n, 1) + dot_nt(moved, side)

    core_start(4, [side_tile(0), side_tile(1)])
    a_start(2)
    a_start(3)
    core_start(6, [side_tile(2), side_tile(3)])
    a_start(4)
    a_start(5)

    loads[8].wait()
    loads[9].wait()
    wspad[pl.ds(336, 48), :] = jnp.zeros((48, 512), BF16)
    pick = flag((lrow & 7) * 16 + lax.shift_right_logical(lrow, 3) == lcol)
    for o in range(16):
        wscr[pl.ds(o * CP + 120, 8), :] = jnp.zeros((8, 512), F32)
    for kb in range(15):
        if kb < 12:
            got = dot_nt(pick, wstage[:, pl.ds(kb * 128, 128)])
        else:
            got = dot(pick, wspad[pl.ds((kb - 12) * 128, 128), :])
        for o in range(16):
            wscr[pl.ds(o * CP + kb * 8, 8), :] = got[o * 8:o * 8 + 8, :]
    for parity in range(2):
        for q in range(2):
            for n, i in enumerate(((3, 1), (2, 0))[parity]):
                for m, j in enumerate(((1, 3), (0, 2))[q]):
                    wcat[pl.ds((parity * 2 + q) * CP, CP), pl.ds((n * 2 + m) * 512, 512)] = wscr[
                        pl.ds((i * 4 + j) * CP, CP), :
                    ].astype(BF16)
    a_start(6)
    a_start(7)

    c_east.wait()
    c_west.wait()
    for slot in range(18):
        at = (pl.ds(slot * 1024 + 512, 512), pl.ds(0, 128))
        cot_b[at] = jnp.where(clane == 0, rcw[...][:, 64 + slot:65 + slot], cot_b[at])
    last = []
    for parity in range(2):
        w_rows = wcat[pl.ds((parity * 2 + 1) * CP, CP), :]
        total = dot(w_rows[:, :512], rce[...]) + pltpu.roll(dot(w_rows[:, 512:1024], sc[...]), 64, 1)
        total = total + pltpu.roll(dot(w_rows[:, 1024:1536], rce[...]), 127, 1)
        last.append(total + pltpu.roll(dot(w_rows[:, 1536:], sc[...]), 63, 1))

    def token_row(s, parities):
        tokens = cot_b[pl.ds(pl.multiple_of(s * 1024, 1024), 2048), :]
        u = dot(wcat[pl.ds(0, 256 * parities), :], tokens)
        rows = []
        for parity in range(parities):
            even, odd = u[parity * 256:parity * 256 + 128], u[parity * 256 + 128:parity * 256 + 256]
            first = jnp.where(lane128 == 0, pltpu.roll(last[parity], lax.rem(128 - s, 128), 1), odd[:, :128])
            rows.append(jnp.concatenate([even, first, odd[:, 128:]], axis=1))
        return rows

    def keep(r, row):
        raw[pl.ds(r * CP if isinstance(r, int) else pl.multiple_of(r * CP, CP), CP), :] = row.astype(BF16)

    fold, top = token_row(16, 2)
    even, odd = token_row(15, 2)
    (bottom,) = token_row(0, 1)
    sfold[...] = fold.astype(BF16)
    top_row[...] = top
    keep(30, even)
    keep(29, odd)
    keep(0, bottom)
    g_mirror = remote(9, sfold, rfold, mirror)

    @pl.when(at_top)
    def _():
        g_mirror.start()

    def out_copy(n, first, count):
        return pltpu.make_async_copy(raw.at[pl.ds(first * CP, count * CP)], rows_out.at[pl.ds(first * CP, count * CP)], out_sem.at[n])

    def rows_of(t, _):
        s = 2 * t + 1
        even, odd = token_row(s, 2)
        even_2, odd_2 = token_row(s + 1, 2)
        keep(2 * s - 1, odd)
        keep(2 * s, even)
        keep(2 * s + 1, odd_2)
        keep(2 * s + 2, even_2)
        for k, b_at, c_at in ((2, 1, 3), (0, 1, 4), (1, 2, 4)):
            pl.when(t == b_at)(functools.partial(b_start, k))
            pl.when(t == c_at)(functools.partial(c_start, k))
        pl.when(t == 5)(lambda: out_copy(0, 0, 19).start())
        pl.when(t == 6)(g_start)
        return 0

    lax.fori_loop(0, 7, rows_of, 0)
    out_copy(1, 19, 12).start()

    @pl.when(at_top)
    def _():
        g_mirror.wait()
        top_row[...] = top_row[...] + folded(rfold[...], permt2, perm2)

    raw[pl.ds(31 * CP, CP), :] = top_row[...].astype(BF16)
    out_copy(2, 31, 1).start()
    for copy in g_copies():
        copy.wait()
    gathered[lon] = s4[...]
    out_share = pltpu.make_async_copy(gathered, share_out, out_sem.at[3])
    out_share.start()
    for n, first, count in ((0, 0, 19), (1, 19, 12), (2, 31, 1)):
        out_copy(n, first, count).wait()
    out_share.wait()


def last_kernel(scale, share, rows, mask, ks_out, kf_out, xs_out, xf_out, permt2, got, cells, own, ks, kf, in_sem, out_sem):
    loads = [pltpu.make_async_copy(share, own, in_sem.at[8])]
    for k in range(8):
        block = pl.ds(k * 16, 16)
        loads.append(pltpu.make_async_copy(rows.at[:, block], got.at[:, block], in_sem.at[k]))
    for copy in loads:
        copy.start()
    lane, across = iota((512, 1), 0), iota((1, 512), 1)
    permt2[...] = flag(((2 * lane - lax.shift_right_logical(lane, 8)) & 511) == across)
    mask_bf = mask[...].astype(F32).astype(BF16)

    loads[0].wait()
    turned = [None] * 16
    for p in range(8):
        for which in range(2):
            o = ROWS[p % 4][0] * 4 + JORD[p // 4 * 2 + which]
            mine = [own[4 * which + y, p] for y in range(4)] + [jnp.zeros((96, 128), F32)]
            turned[o] = jnp.transpose(jnp.concatenate(mine, axis=0)) * scale
    for n in range(15):
        block = jnp.stack([x[n * 8:n * 8 + 8] for x in turned], axis=0)
        block = jnp.transpose(jnp.swapaxes(block, 0, 1).reshape(128, 128))[:32]
        if n < 12:
            kf[:, pl.ds(n * 128, 128)] = block
        elif n < 14:
            ks[:, pl.ds((n - 12) * 128, 128)] = block
        else:
            ks[:, pl.ds(256, 80)] = block[:, :80]
    stores = [pltpu.make_async_copy(kf, kf_out, out_sem.at[8]), pltpu.make_async_copy(ks, ks_out, out_sem.at[9])]
    for copy in stores:
        copy.start()

    for pair in range(0, 8, 2):
        copies = []
        for copy in loads[pair + 1:pair + 3]:
            copy.wait()
        for k in (pair, pair + 1):
            x = jnp.swapaxes(got[:, pl.ds(k * 16, 16), :], 0, 1).reshape(512, 512)
            y = dot(x, permt2[...]).astype(BF16).reshape(16, 32, 512) * mask_bf[None]
            cells[pl.ds(k * 512, 512), :] = y.reshape(512, 512)
            if k < 6:
                dst, at, count = xf_out, k * 512, 512
            else:
                dst, at, count = xs_out, (k - 6) * 512, 512 if k == 6 else SC * 32 - 512
            copies.append(pltpu.make_async_copy(cells.at[pl.ds(k * 512, count)], dst.at[pl.ds(at, count)], out_sem.at[k]))
        for copy in copies:
            copy.start()
        stores += copies
    for copy in stores:
        copy.wait()


def on_device(state, forcing, land_mask, partner, cotangent, weight_state, weight_force):
    sc, fc = state.shape[1], forcing.shape[1]
    rows, cols = state.shape[2:]
    width = cotangent.shape[1]
    lon_n, lat_n, batch_n = (lax.axis_size(a) for a in ("lon", "lat", "batch"))
    any_spec = pl.BlockSpec(memory_space=pl.ANY)
    vmem = pl.BlockSpec(memory_space=pltpu.VMEM)
    share, cells = pl.pallas_call(
        main_kernel,
        out_shape=(
            jax.ShapeDtypeStruct((8, 8, 8, 128), F32),
            jax.ShapeDtypeStruct((rows * CP, cols), BF16),
        ),
        in_specs=[any_spec, any_spec, vmem, vmem, any_spec, any_spec, any_spec],
        out_specs=(any_spec, any_spec),
        scratch_shapes=[
            pltpu.VMEM((4096, 512), BF16),
            pltpu.VMEM((8 * CP, 17 * 256), BF16),
            pltpu.VMEM((8192, 256), BF16),
            pltpu.VMEM((512, 4096), BF16),
            pltpu.VMEM((18 * 1024, 256), BF16),
            pltpu.VMEM((512, 2048), BF16),
            pltpu.VMEM((2048, 512), F32),
            pltpu.VMEM((8, 4, 2, 2, 4, 8, 256), F32),
            pltpu.VMEM((512, 1536), BF16),
            pltpu.VMEM((384, 512), BF16),
            pltpu.VMEM((512, 512), BF16),
            pltpu.VMEM((512, 512), BF16),
            pltpu.VMEM((512, 512), BF16),
            pltpu.VMEM((512, 512), BF16),
            pltpu.VMEM((512, 512), BF16),
            pltpu.VMEM((CP, 512), F32),
            pltpu.VMEM((512, 256), BF16),
            pltpu.VMEM((512, 256), BF16),
            pltpu.VMEM((256, 256), BF16),
            pltpu.VMEM((512, 256), BF16),
            pltpu.VMEM((512, 256), BF16),
            pltpu.VMEM((CP, 128), BF16),
            pltpu.VMEM((CP, 128), BF16),
            pltpu.VMEM((CP, 128), BF16),
            pltpu.VMEM((512, 128), BF16),
            pltpu.VMEM((512, 128), BF16),
            pltpu.VMEM((512, 128), BF16),
            pltpu.VMEM((CP, 512), BF16),
            pltpu.VMEM((CP, 512), BF16),
            pltpu.VMEM((8, 4, 2, 4, 8, 256), F32),
            pltpu.VMEM((3, 3, 1, 2, 4, 8, 256), F32),
            pltpu.VMEM((3, 3, 4, 1, 4, 8, 128), F32),
            pltpu.VMEM((2, 3, 4, 2, 1, 8, 256), F32),
            pltpu.VMEM((3, 1, 2, 4, 8, 256), F32),
            pltpu.VMEM((3, 4, 1, 4, 8, 128), F32),
            pltpu.VMEM((2, 4, 2, 1, 8, 256), F32),
            pltpu.VMEM((3, 3, 1, 1, 4, 8, 128), F32),
            pltpu.VMEM((3, 3, 4, 1, 1, 8, 128), F32),
            pltpu.VMEM((3, 2, 1, 2, 1, 8, 256), F32),
            pltpu.VMEM((3, 1, 1, 4, 8, 128), F32),
            pltpu.VMEM((3, 4, 1, 1, 8, 128), F32),
            pltpu.VMEM((2, 1, 2, 1, 8, 256), F32),
            pltpu.VMEM((3, 3, 1, 1, 1, 8, 128), F32),
            pltpu.VMEM((3, 3, 1, 1, 1, 8, 128), F32),
            pltpu.VMEM((3, 2, 1, 1, 1, 8, 128), F32),
            pltpu.VMEM((8, 8, 128), F32),
            pltpu.VMEM((8, 8, 8, 128), F32),
            pltpu.SemaphoreType.DMA((10,)),
            pltpu.SemaphoreType.DMA((8,)),
            pltpu.SemaphoreType.DMA((10,)),
            pltpu.SemaphoreType.DMA((10,)),
            pltpu.SemaphoreType.DMA((8,)),
            pltpu.SemaphoreType.DMA((8,)),
            pltpu.SemaphoreType.DMA((8, 3)),
            pltpu.SemaphoreType.DMA((8, 3)),
            pltpu.SemaphoreType.DMA((3, 3)),
            pltpu.SemaphoreType.DMA((3, 3)),
            pltpu.SemaphoreType.DMA((3, 3)),
            pltpu.SemaphoreType.DMA((3, 3)),
            pltpu.SemaphoreType.DMA((7,)),
            pltpu.SemaphoreType.DMA((7,)),
        ],
        compiler_params=pltpu.CompilerParams(
            collective_id=0, has_side_effects=True, vmem_limit_bytes=62 * 1024 * 1024
        ),
        name="encoder_backward",
    )(
        state.reshape(sc * rows, cols), forcing.reshape(fc * rows, cols), land_mask, partner[None, :],
        cotangent.reshape(width * cotangent.shape[2], cotangent.shape[3]), weight_state.T, weight_force,
    )
    scale = 1.0 / math.sqrt(batch_n * (rows // 2) * lat_n * (cols // 2) * lon_n)
    own = width // (lat_n * batch_n)
    ks, kf, xs, xf = pl.pallas_call(
        functools.partial(last_kernel, scale),
        out_shape=(
            jax.ShapeDtypeStruct((own, sc * 16), F32),
            jax.ShapeDtypeStruct((own, fc * 16), F32),
            jax.ShapeDtypeStruct((sc * rows, cols), BF16),
            jax.ShapeDtypeStruct((fc * rows, cols), BF16),
        ),
        in_specs=[any_spec, any_spec, vmem],
        out_specs=(any_spec,) * 4,
        scratch_shapes=[
            pltpu.VMEM((512, 512), BF16),
            pltpu.VMEM((rows, CP, cols), BF16),
            pltpu.VMEM((rows * CP, cols), BF16),
            pltpu.VMEM((8, 8, 8, 128), F32),
            pltpu.VMEM((own, sc * 16), F32),
            pltpu.VMEM((own, fc * 16), F32),
            pltpu.SemaphoreType.DMA((9,)),
            pltpu.SemaphoreType.DMA((10,)),
        ],
        compiler_params=pltpu.CompilerParams(vmem_limit_bytes=62 * 1024 * 1024),
        name="encoder_finish",
    )(share, cells.reshape(rows, CP, cols), land_mask)
    return (
        xs.reshape(state.shape),
        xf.reshape(forcing.shape),
        ks,
        kf,
    )


def solution(mesh):
    in_specs = (
        P("batch", None, "lat", "lon"),
        P("batch", None, "lat", "lon"),
        P("lat", "lon"),
        P("lon"),
        P("batch", None, "lat", "lon"),
        P(),
        P(),
    )
    out_specs = (
        P("batch", None, "lat", "lon"),
        P("batch", None, "lat", "lon"),
        P(("lat", "batch"), None),
        P(("lat", "batch"), None),
    )
    return jax.shard_map(on_device, mesh=mesh, in_specs=in_specs, out_specs=out_specs, check_vma=False)
```

```python
import functools
import math

import jax
import jax.numpy as jnp
from jax import lax
from jax.experimental import pallas as pl
from jax.experimental.pallas import tpu as pltpu
from jax.sharding import PartitionSpec as P

SC = 21
FC = 96
CP = 128
F32 = jnp.float32
BF16 = jnp.bfloat16
JORD = (1, 2, 0, 3)
ROWS = ((1, 0, 0), (2, 1, 1), (0, 1, 0), (3, 0, 1))


def iota(shape, dim):
    return lax.broadcasted_iota(jnp.int32, shape, dim)


def dot(a, b):
    return lax.dot_general(a, b, (((1,), (0,)), ((), ())), preferred_element_type=F32)


def dot_nt(a, b):
    return lax.dot_general(a, b, (((1,), (1,)), ((), ())), preferred_element_type=F32)


def flag(where):
    return jnp.where(where, 1.0, 0.0).astype(BF16)


def main_kernel(
    state, force, mask, partner, cot, wst, wf,
    share_out, rows_out,
    raw, planes, craw, cot_a, cot_b, wcat, wscr, gbuf, wstage, wspad, perm, permt, perm2, permt2, fold_sel, top_row,
    rxs, rxn, rmir, rcs, rcn, sx, rxw, rxe, sc, rcw, rce, sfold, rfold,
    rcore, ra_z, ra_x, ra_y, s2_z, s2_x, s2_y, rb_z, rb_x, rb_y, s3_z, s3_x, s3_y, rc_z, rc_x, rc_y, s4, gathered,
    in_sem, out_sem, send, recv, core_s, core_r, a_s, a_r, b_s, b_r, c_s, c_r, g_s, g_r,
):
    lon_n = lax.axis_size("lon")
    lat_n = lax.axis_size("lat")
    lon = lax.axis_index("lon")
    lat = lax.axis_index("lat")
    at_top = lat == lat_n - 1
    at_bottom = lat == 0
    north = {"lat": lax.rem(lat + 1, lat_n)}
    south = {"lat": lax.rem(lat + lat_n - 1, lat_n)}
    east = {"lon": lax.rem(lon + 1, lon_n)}
    west = {"lon": lax.rem(lon + lon_n - 1, lon_n)}
    mirror = {"lon": lon_n - 1 - lon}
    at_y, at_z, core = lax.rem(lon, 4), lax.div(lat, 2), lax.rem(lat, 2)
    x_lo, x_hi = lax.axis_index("batch"), lax.div(lon, 4)
    spot = {"x": 2 * x_hi + x_lo, "y": at_y, "z": at_z}
    other_core = {"lat": 2 * at_z + 1 - core}

    def peer_on(axis, place):
        if axis == "z":
            return {"lat": 2 * place + core}
        if axis == "y":
            return {"lon": 4 * x_hi + place}
        return {"lon": 4 * lax.div(place, 2) + at_y, "batch": lax.rem(place, 2)}

    def lon_peer(d):
        return {"lon": lax.rem(lon + d, lon_n)}

    peers = [north, south, mirror, other_core] + [lon_peer(d) for d in range(1, 8)]
    for axis in "xyz":
        peers += [peer_on(axis, lax.rem(spot[axis] + d, 4)) for d in range(1, 4)]

    loads = []
    for k in range(6):
        loads.append(pltpu.make_async_copy(force.at[pl.ds(k * 512, 512)], raw.at[pl.ds(k * 512, 512)], in_sem.at[k]))
    loads.append(pltpu.make_async_copy(state, raw.at[pl.ds(FC * 32, SC * 32)], in_sem.at[6]))
    loads.append(pltpu.make_async_copy(cot, craw, in_sem.at[7]))
    loads.append(pltpu.make_async_copy(wst, wspad.at[pl.ds(0, 336)], in_sem.at[8]))
    loads.append(pltpu.make_async_copy(wf, wstage, in_sem.at[9]))
    for copy in loads[:7]:
        copy.start()

    barrier = pltpu.get_barrier_semaphore()
    for peer in peers:
        pl.semaphore_signal(barrier, inc=1, device_id=peer, device_id_type=pl.DeviceIdType.MESH)
    def remote(n, src, dst, peer):
        return pltpu.make_async_remote_copy(
            src_ref=src, dst_ref=dst, send_sem=send.at[n], recv_sem=recv.at[n],
            device_id=peer, device_id_type=pl.DeviceIdType.MESH,
        )

    down, across = iota((512, 1), 0), iota((1, 512), 1)

    def column(lane, late):
        half = lax.shift_right_logical(lane, 8)
        return (2 * lane + (-half if late else half)) & 511

    perm[...] = flag(down == column(across, False))
    permt[...] = flag(column(down, False) == across)
    perm2[...] = flag(down == column(across, True))
    permt2[...] = flag(column(down, True) == across)

    raw[pl.ds((FC + SC) * 32, (CP - FC - SC) * 32), :] = jnp.zeros(((CP - FC - SC) * 32, 512), BF16)
    mask_bf = mask[...].astype(F32).astype(BF16)
    zero16 = jnp.zeros((), BF16)
    lane128 = iota((CP, 128), 1)

    def put_row(parity, slot, channels, both):
        n = both.shape[0]
        lane256 = iota((n, 256), 1)
        even, odd = both[:, :256], both[:, 256:]
        left = jnp.where(lane256 == 0, zero16, pltpu.roll(odd, 1, 1))
        right = jnp.where(lane256 == 255, zero16, pltpu.roll(even, 255, 1))
        for j, part in enumerate((even, odd, left, right)):
            planes[pl.ds((parity * 4 + j) * CP + channels, n), pl.ds(slot * 256, 256)] = part

    lane16 = iota((16, 128), 1)
    for k in range(8):
        if k % 2 == 0:
            for copy in loads[k:min(k + 2, 7)]:
                copy.wait()
        if k == 4:
            for copy in loads[7:]:
                copy.start()
        x = raw[pl.ds(k * 512, 512), :].reshape(16, 32, 512) * mask_bf[None]
        y = dot(x.reshape(512, 512), perm[...]).astype(BF16)
        y = jnp.swapaxes(y.reshape(16, 32, 512), 0, 1)
        edge = jnp.zeros((16, 128), BF16)
        for r in range(32):
            put_row(r % 2, r // 2 + r % 2, k * 16, y[r])
            edge = jnp.where(lane16 == r + 1, y[r][:, 0:1], edge)
            edge = jnp.where(lane16 == 65 + r, y[r][:, 511:512], edge)
        sx[pl.ds(k * 16, 16), :] = edge

    pl.semaphore_wait(barrier, len(peers))
    x_north = remote(0, planes.at[pl.ds(512, 512), pl.ds(16 * 256, 256)], rxs, north)
    x_south = remote(1, planes.at[pl.ds(0, 512), pl.ds(0, 256)], rxn, south)
    x_mirror = remote(2, planes.at[pl.ds(512, 256), pl.ds(16 * 256, 256)], rmir, mirror)
    x_north.start()
    x_south.start()

    @pl.when(at_top)
    def _():
        x_mirror.start()

    loads[7].wait()
    clane = iota((512, 128), 1)
    lane32 = iota((32, 128), 1)

    def late(x):
        return jnp.where(iota(x.shape, 1) == 0, zero16, pltpu.roll(x, 1, 1))

    def split_tokens(k, _):
        x = craw[pl.ds(pl.multiple_of(k * 512, 512), 512), :].reshape(32, 16, 256)
        y = jnp.swapaxes(x, 0, 1)
        w = pl.multiple_of(k * 32, 32)
        edge = jnp.zeros((32, 128), BF16)
        for a in range(16):
            cot_a[pl.ds(w, 32), pl.ds(a * 256, 256)] = y[a]
            cot_b[pl.ds((a + 1) * 1024 + w, 32), :] = y[a]
            cot_b[pl.ds((a + 1) * 1024 + 512 + w, 32), :] = late(y[a])
            edge = jnp.where(lane32 == a + 1, y[a][:, 0:1], edge)
            edge = jnp.where(lane32 == 65 + a, y[a][:, 255:256], edge)
        sc[pl.ds(w, 32), :] = edge
        return 0

    lax.fori_loop(0, 16, split_tokens, 0)
    c_north = remote(3, cot_b.at[pl.ds(16 * 1024, 512)], rcs, north)
    c_south = remote(4, cot_b.at[pl.ds(1024, 512)], rcn, south)
    c_north.start()
    c_south.start()

    def tile(n, pair):
        _, parity, off = ROWS[n]
        rows = planes[pl.ds((parity * 4 + pair * 2) * CP, 2 * CP), pl.ds(off * 256, 4096)]
        return dot_nt(cot_a[...], rows)

    orders = ("zxy", "xyz", "yzx")
    recv_a, sum_2 = (ra_z, ra_x, ra_y), (s2_z, s2_x, s2_y)
    recv_b, sum_3 = (rb_z, rb_x, rb_y), (s3_z, s3_x, s3_y)
    recv_c = (rc_z, rc_x, rc_y)

    def part(axis, place):
        every = slice(None)
        if axis == "z":
            return (pl.ds(place, 1), every, every, every, every)
        if axis == "y":
            return (every, every, pl.ds(place, 1), every, every)
        lanes = pl.ds(pl.multiple_of(lax.div(place, 2) * 128, 128), 128)
        return (every, pl.ds(lax.rem(place, 2), 1), every, every, lanes)

    def exchange(axis, src, dst, ss, rs):
        copies = []
        for d in range(1, 4):
            place = lax.rem(spot[axis] + d, 4)
            copies.append(pltpu.make_async_remote_copy(
                src_ref=src(part(axis, place)), dst_ref=dst(d - 1), send_sem=ss(d - 1), recv_sem=rs(d - 1),
                device_id=peer_on(axis, place), device_id_type=pl.DeviceIdType.MESH,
            ))
        return copies

    def core_copy(p):
        return pltpu.make_async_remote_copy(
            src_ref=gbuf.at[p, :, 1 - core], dst_ref=rcore.at[p], send_sem=core_s.at[p], recv_sem=core_r.at[p],
            device_id=other_core, device_id_type=pl.DeviceIdType.MESH,
        )

    def a_copies(p):
        k, slot = p % 3, p // 3
        return exchange(
            orders[k][0], lambda at_part: rcore.at[(p,) + at_part], lambda d: recv_a[k].at[slot, d],
            lambda d: a_s.at[p, d], lambda d: a_r.at[p, d],
        )

    def b_copies(k):
        return exchange(
            orders[k][1], lambda at_part: sum_2[k].at[(slice(None),) + at_part], lambda d: recv_b[k].at[d],
            lambda d: b_s.at[k, d], lambda d: b_r.at[k, d],
        )

    def c_copies(k):
        return exchange(
            orders[k][2], lambda at_part: sum_3[k].at[(slice(None),) + at_part], lambda d: recv_c[k].at[d],
            lambda d: c_s.at[k, d], lambda d: c_r.at[k, d],
        )

    def g_copies():
        return [
            pltpu.make_async_remote_copy(
                src_ref=s4, dst_ref=gathered.at[lon], send_sem=g_s.at[d - 1], recv_sem=g_r.at[d - 1],
                device_id=lon_peer(d), device_id_type=pl.DeviceIdType.MESH,
            )
            for d in range(1, 8)
        ]

    def core_start(p, values):
        for n, value in enumerate(values):
            gbuf[p + n] = value.reshape(4, 2, 2, 4, 8, 256)
        for n in range(len(values)):
            core_copy(p + n).start()

    def a_start(p):
        core_copy(p).wait()
        rcore[p] = rcore[p] + gbuf[p, :, core]
        for copy in a_copies(p):
            copy.start()

    def b_start(k):
        for p in range(k, 8, 3):
            slot = p // 3
            for copy in a_copies(p):
                copy.wait()
            own = rcore[(p,) + part(orders[k][0], spot[orders[k][0]])]
            got = recv_a[k][slot]
            sum_2[k][slot] = own + got[0] + got[1] + got[2]
        for copy in b_copies(k):
            copy.start()

    def c_start(k):
        for copy in b_copies(k):
            copy.wait()
        own = sum_2[k][(slice(None),) + part(orders[k][1], spot[orders[k][1]])]
        got = recv_b[k][...]
        sum_3[k][...] = own + got[0] + got[1] + got[2]
        for copy in c_copies(k):
            copy.start()

    def g_start():
        for k in range(3):
            for copy in c_copies(k):
                copy.wait()
            own = sum_3[k][(slice(None),) + part(orders[k][2], spot[orders[k][2]])]
            got = recv_c[k][...]
            total = own + got[0] + got[1] + got[2]
            for slot in range(total.shape[0]):
                s4[slot * 3 + k] = total[slot, 0, 0, 0]
        for copy in g_copies():
            copy.start()

    fold_sel[...] = flag(down == partner[...] - (lon_n - 1 - lon) * 512)

    def folded(x, before, after):
        x = dot(x, before[...]).astype(BF16)
        x = dot(x, fold_sel[...]).astype(BF16)
        return dot(x, after[...])

    x_north.wait()
    x_south.wait()
    planes[pl.ds(512, 512), pl.ds(0, 256)] = jnp.where(at_bottom, zero16, rxs[...])
    planes[pl.ds(0, 512), pl.ds(16 * 256, 256)] = rxn[...]

    @pl.when(at_top)
    def _():
        x_mirror.wait()
        top = jnp.concatenate([rmir[pl.ds(0, CP), :], rmir[pl.ds(CP, CP), :]], axis=1)
        put_row(0, 16, 0, folded(top, permt, perm).astype(BF16))

    acc = sx[...]
    acc = jnp.where(lane128 == 0, planes[pl.ds(512, CP), pl.ds(0, 128)][:, 0:1], acc)
    acc = jnp.where(lane128 == 64, planes[pl.ds(512 + CP, CP), pl.ds(128, 128)][:, 127:128], acc)
    acc = jnp.where(lane128 == 33, planes[pl.ds(0, CP), pl.ds(16 * 256, 128)][:, 0:1], acc)
    acc = jnp.where(lane128 == 97, planes[pl.ds(CP, CP), pl.ds(16 * 256 + 128, 128)][:, 127:128], acc)
    sx[...] = acc
    x_east = remote(5, sx, rxw, east)
    x_west = remote(6, sx, rxe, west)
    x_east.start()
    x_west.start()


    c_north.wait()
    c_south.wait()
    low = jnp.where(at_bottom, zero16, rcs[...])
    high = jnp.where(at_top, zero16, rcn[...])
    for slot, x in ((0, low), (17, high)):
        cot_b[pl.ds(slot * 1024, 512), :] = x
        cot_b[pl.ds(slot * 1024 + 512, 512), :] = late(x)
    acc = sc[...]
    acc = jnp.where(clane == 0, low[:, 0:1], acc)
    acc = jnp.where(clane == 64, low[:, 255:256], acc)
    acc = jnp.where(clane == 17, high[:, 0:1], acc)
    acc = jnp.where(clane == 81, high[:, 255:256], acc)
    sc[...] = acc
    c_east = remote(7, sc, rcw, east)
    c_west = remote(8, sc, rce, west)
    c_east.start()
    c_west.start()

    core_start(0, [tile(0, 0), tile(1, 0), tile(2, 0), tile(3, 0)])
    a_start(0)
    a_start(1)
    x_east.wait()
    x_west.wait()
    side = jnp.concatenate(
        [jnp.where(lane128 >= 64, rxw[...], zero16), jnp.where(lane128 < 64, rxe[...], zero16)], axis=0
    )
    lrow, lcol = iota((128, 128), 0), iota((128, 128), 1)

    def side_tile(n):
        i = ROWS[n][0]
        first = (lrow >= 1) & (lrow <= 16) & (lcol == 62 + 2 * lrow + i)
        last = (lrow >= 65) & (lrow <= 80) & (lcol == 2 * lrow - 130 + i)
        moved = dot(sc[...], flag(first | last)).astype(BF16)
        return tile(n, 1) + dot_nt(moved, side)

    core_start(4, [side_tile(0), side_tile(1)])
    a_start(2)
    a_start(3)
    core_start(6, [side_tile(2), side_tile(3)])
    a_start(4)
    a_start(5)

    loads[8].wait()
    loads[9].wait()
    wspad[pl.ds(336, 48), :] = jnp.zeros((48, 512), BF16)
    pick = flag((lrow & 7) * 16 + lax.shift_right_logical(lrow, 3) == lcol)
    for o in range(16):
        wscr[pl.ds(o * CP + 120, 8), :] = jnp.zeros((8, 512), F32)
    for kb in range(15):
        if kb < 12:
            got = dot_nt(pick, wstage[:, pl.ds(kb * 128, 128)])
        else:
            got = dot(pick, wspad[pl.ds((kb - 12) * 128, 128), :])
        for o in range(16):
            wscr[pl.ds(o * CP + kb * 8, 8), :] = got[o * 8:o * 8 + 8, :]
    for parity in range(2):
        for q in range(2):
            for n, i in enumerate(((3, 1), (2, 0))[parity]):
                for m, j in enumerate(((1, 3), (0, 2))[q]):
                    wcat[pl.ds((parity * 2 + q) * CP, CP), pl.ds((n * 2 + m) * 512, 512)] = wscr[
                        pl.ds((i * 4 + j) * CP, CP), :
                    ].astype(BF16)
    a_start(6)
    a_start(7)

    c_east.wait()
    c_west.wait()
    for slot in range(18):
        at = (pl.ds(slot * 1024 + 512, 512), pl.ds(0, 128))
        cot_b[at] = jnp.where(clane == 0, rcw[...][:, 64 + slot:65 + slot], cot_b[at])
    last = []
    for parity in range(2):
        w_rows = wcat[pl.ds((parity * 2 + 1) * CP, CP), :]
        total = dot(w_rows[:, :512], rce[...]) + pltpu.roll(dot(w_rows[:, 512:1024], sc[...]), 64, 1)
        total = total + pltpu.roll(dot(w_rows[:, 1024:1536], rce[...]), 127, 1)
        last.append(total + pltpu.roll(dot(w_rows[:, 1536:], sc[...]), 63, 1))

    def token_row(s, parities):
        tokens = cot_b[pl.ds(pl.multiple_of(s * 1024, 1024), 2048), :]
        u = dot(wcat[pl.ds(0, 256 * parities), :], tokens)
        rows = []
        for parity in range(parities):
            even, odd = u[parity * 256:parity * 256 + 128], u[parity * 256 + 128:parity * 256 + 256]
            first = jnp.where(lane128 == 0, pltpu.roll(last[parity], lax.rem(128 - s, 128), 1), odd[:, :128])
            rows.append(jnp.concatenate([even, first, odd[:, 128:]], axis=1))
        return rows

    def keep(r, row):
        raw[pl.ds(r * CP if isinstance(r, int) else pl.multiple_of(r * CP, CP), CP), :] = row.astype(BF16)

    fold, top = token_row(16, 2)
    even, odd = token_row(15, 2)
    (bottom,) = token_row(0, 1)
    sfold[...] = fold.astype(BF16)
    top_row[...] = top
    keep(30, even)
    keep(29, odd)
    keep(0, bottom)
    g_mirror = remote(9, sfold, rfold, mirror)

    @pl.when(at_top)
    def _():
        g_mirror.start()

    def out_copy(n, first, count):
        return pltpu.make_async_copy(raw.at[pl.ds(first * CP, count * CP)], rows_out.at[pl.ds(first * CP, count * CP)], out_sem.at[n])

    def rows_of(t, _):
        s = 2 * t + 1
        even, odd = token_row(s, 2)
        even_2, odd_2 = token_row(s + 1, 2)
        keep(2 * s - 1, odd)
        keep(2 * s, even)
        keep(2 * s + 1, odd_2)
        keep(2 * s + 2, even_2)
        for k, b_at, c_at in ((2, 0, 2), (0, 0, 2), (1, 1, 3)):
            pl.when(t == b_at)(functools.partial(b_start, k))
            pl.when(t == c_at)(functools.partial(c_start, k))
        pl.when(t == 6)(lambda: out_copy(0, 0, 19).start())
        pl.when(t == 5)(g_start)
        return 0

    lax.fori_loop(0, 7, rows_of, 0)
    out_copy(1, 19, 12).start()

    @pl.when(at_top)
    def _():
        g_mirror.wait()
        top_row[...] = top_row[...] + folded(rfold[...], permt2, perm2)

    raw[pl.ds(31 * CP, CP), :] = top_row[...].astype(BF16)
    out_copy(2, 31, 1).start()
    for copy in g_copies():
        copy.wait()
    gathered[lon] = s4[...]
    out_share = pltpu.make_async_copy(gathered, share_out, out_sem.at[3])
    out_share.start()
    for n, first, count in ((0, 0, 19), (1, 19, 12), (2, 31, 1)):
        out_copy(n, first, count).wait()
    out_share.wait()


def last_kernel(scale, share, rows, mask, ks_out, kf_out, xs_out, xf_out, permt2, got, cells, own, ks, kf, in_sem, out_sem):
    loads = [pltpu.make_async_copy(share, own, in_sem.at[8])]
    for k in range(8):
        block = pl.ds(k * 16, 16)
        loads.append(pltpu.make_async_copy(rows.at[:, block], got.at[:, block], in_sem.at[k]))
    for copy in loads:
        copy.start()
    lane, across = iota((512, 1), 0), iota((1, 512), 1)
    permt2[...] = flag(((2 * lane - lax.shift_right_logical(lane, 8)) & 511) == across)
    mask_bf = mask[...].astype(F32).astype(BF16)

    loads[0].wait()
    turned = [None] * 16
    for p in range(8):
        for which in range(2):
            o = ROWS[p % 4][0] * 4 + JORD[p // 4 * 2 + which]
            mine = [own[4 * which + y, p] for y in range(4)] + [jnp.zeros((96, 128), F32)]
            turned[o] = jnp.transpose(jnp.concatenate(mine, axis=0)) * scale
    for n in range(15):
        block = jnp.stack([x[n * 8:n * 8 + 8] for x in turned], axis=0)
        block = jnp.transpose(jnp.swapaxes(block, 0, 1).reshape(128, 128))[:32]
        if n < 12:
            kf[:, pl.ds(n * 128, 128)] = block
        elif n < 14:
            ks[:, pl.ds((n - 12) * 128, 128)] = block
        else:
            ks[:, pl.ds(256, 80)] = block[:, :80]
    stores = [pltpu.make_async_copy(kf, kf_out, out_sem.at[8]), pltpu.make_async_copy(ks, ks_out, out_sem.at[9])]
    for copy in stores:
        copy.start()

    for pair in range(0, 8, 2):
        copies = []
        for copy in loads[pair + 1:pair + 3]:
            copy.wait()
        for k in (pair, pair + 1):
            x = jnp.swapaxes(got[:, pl.ds(k * 16, 16), :], 0, 1).reshape(512, 512)
            y = dot(x, permt2[...]).astype(BF16).reshape(16, 32, 512) * mask_bf[None]
            cells[pl.ds(k * 512, 512), :] = y.reshape(512, 512)
            if k < 6:
                dst, at, count = xf_out, k * 512, 512
            else:
                dst, at, count = xs_out, (k - 6) * 512, 512 if k == 6 else SC * 32 - 512
            copies.append(pltpu.make_async_copy(cells.at[pl.ds(k * 512, count)], dst.at[pl.ds(at, count)], out_sem.at[k]))
        for copy in copies:
            copy.start()
        stores += copies
    for copy in stores:
        copy.wait()


def on_device(state, forcing, land_mask, partner, cotangent, weight_state, weight_force):
    sc, fc = state.shape[1], forcing.shape[1]
    rows, cols = state.shape[2:]
    width = cotangent.shape[1]
    lon_n, lat_n, batch_n = (lax.axis_size(a) for a in ("lon", "lat", "batch"))
    any_spec = pl.BlockSpec(memory_space=pl.ANY)
    vmem = pl.BlockSpec(memory_space=pltpu.VMEM)
    share, cells = pl.pallas_call(
        main_kernel,
        out_shape=(
            jax.ShapeDtypeStruct((8, 8, 8, 128), F32),
            jax.ShapeDtypeStruct((rows * CP, cols), BF16),
        ),
        in_specs=[any_spec, any_spec, vmem, vmem, any_spec, any_spec, any_spec],
        out_specs=(any_spec, any_spec),
        scratch_shapes=[
            pltpu.VMEM((4096, 512), BF16),
            pltpu.VMEM((8 * CP, 17 * 256), BF16),
            pltpu.VMEM((8192, 256), BF16),
            pltpu.VMEM((512, 4096), BF16),
            pltpu.VMEM((18 * 1024, 256), BF16),
            pltpu.VMEM((512, 2048), BF16),
            pltpu.VMEM((2048, 512), F32),
            pltpu.VMEM((8, 4, 2, 2, 4, 8, 256), F32),
            pltpu.VMEM((512, 1536), BF16),
            pltpu.VMEM((384, 512), BF16),
            pltpu.VMEM((512, 512), BF16),
            pltpu.VMEM((512, 512), BF16),
            pltpu.VMEM((512, 512), BF16),
            pltpu.VMEM((512, 512), BF16),
            pltpu.VMEM((512, 512), BF16),
            pltpu.VMEM((CP, 512), F32),
            pltpu.VMEM((512, 256), BF16),
            pltpu.VMEM((512, 256), BF16),
            pltpu.VMEM((256, 256), BF16),
            pltpu.VMEM((512, 256), BF16),
            pltpu.VMEM((512, 256), BF16),
            pltpu.VMEM((CP, 128), BF16),
            pltpu.VMEM((CP, 128), BF16),
            pltpu.VMEM((CP, 128), BF16),
            pltpu.VMEM((512, 128), BF16),
            pltpu.VMEM((512, 128), BF16),
            pltpu.VMEM((512, 128), BF16),
            pltpu.VMEM((CP, 512), BF16),
            pltpu.VMEM((CP, 512), BF16),
            pltpu.VMEM((8, 4, 2, 4, 8, 256), F32),
            pltpu.VMEM((3, 3, 1, 2, 4, 8, 256), F32),
            pltpu.VMEM((3, 3, 4, 1, 4, 8, 128), F32),
            pltpu.VMEM((2, 3, 4, 2, 1, 8, 256), F32),
            pltpu.VMEM((3, 1, 2, 4, 8, 256), F32),
            pltpu.VMEM((3, 4, 1, 4, 8, 128), F32),
            pltpu.VMEM((2, 4, 2, 1, 8, 256), F32),
            pltpu.VMEM((3, 3, 1, 1, 4, 8, 128), F32),
            pltpu.VMEM((3, 3, 4, 1, 1, 8, 128), F32),
            pltpu.VMEM((3, 2, 1, 2, 1, 8, 256), F32),
            pltpu.VMEM((3, 1, 1, 4, 8, 128), F32),
            pltpu.VMEM((3, 4, 1, 1, 8, 128), F32),
            pltpu.VMEM((2, 1, 2, 1, 8, 256), F32),
            pltpu.VMEM((3, 3, 1, 1, 1, 8, 128), F32),
            pltpu.VMEM((3, 3, 1, 1, 1, 8, 128), F32),
            pltpu.VMEM((3, 2, 1, 1, 1, 8, 128), F32),
            pltpu.VMEM((8, 8, 128), F32),
            pltpu.VMEM((8, 8, 8, 128), F32),
            pltpu.SemaphoreType.DMA((10,)),
            pltpu.SemaphoreType.DMA((8,)),
            pltpu.SemaphoreType.DMA((10,)),
            pltpu.SemaphoreType.DMA((10,)),
            pltpu.SemaphoreType.DMA((8,)),
            pltpu.SemaphoreType.DMA((8,)),
            pltpu.SemaphoreType.DMA((8, 3)),
            pltpu.SemaphoreType.DMA((8, 3)),
            pltpu.SemaphoreType.DMA((3, 3)),
            pltpu.SemaphoreType.DMA((3, 3)),
            pltpu.SemaphoreType.DMA((3, 3)),
            pltpu.SemaphoreType.DMA((3, 3)),
            pltpu.SemaphoreType.DMA((7,)),
            pltpu.SemaphoreType.DMA((7,)),
        ],
        compiler_params=pltpu.CompilerParams(
            collective_id=0, has_side_effects=True, vmem_limit_bytes=62 * 1024 * 1024
        ),
        name="encoder_backward",
    )(
        state.reshape(sc * rows, cols), forcing.reshape(fc * rows, cols), land_mask, partner[None, :],
        cotangent.reshape(width * cotangent.shape[2], cotangent.shape[3]), weight_state.T, weight_force,
    )
    scale = 1.0 / math.sqrt(batch_n * (rows // 2) * lat_n * (cols // 2) * lon_n)
    own = width // (lat_n * batch_n)
    ks, kf, xs, xf = pl.pallas_call(
        functools.partial(last_kernel, scale),
        out_shape=(
            jax.ShapeDtypeStruct((own, sc * 16), F32),
            jax.ShapeDtypeStruct((own, fc * 16), F32),
            jax.ShapeDtypeStruct((sc * rows, cols), BF16),
            jax.ShapeDtypeStruct((fc * rows, cols), BF16),
        ),
        in_specs=[any_spec, any_spec, vmem],
        out_specs=(any_spec,) * 4,
        scratch_shapes=[
            pltpu.VMEM((512, 512), BF16),
            pltpu.VMEM((rows, CP, cols), BF16),
            pltpu.VMEM((rows * CP, cols), BF16),
            pltpu.VMEM((8, 8, 8, 128), F32),
            pltpu.VMEM((own, sc * 16), F32),
            pltpu.VMEM((own, fc * 16), F32),
            pltpu.SemaphoreType.DMA((9,)),
            pltpu.SemaphoreType.DMA((10,)),
        ],
        compiler_params=pltpu.CompilerParams(vmem_limit_bytes=62 * 1024 * 1024),
        name="encoder_finish",
    )(share, cells.reshape(rows, CP, cols), land_mask)
    return (
        xs.reshape(state.shape),
        xf.reshape(forcing.shape),
        ks,
        kf,
    )


def solution(mesh):
    in_specs = (
        P("batch", None, "lat", "lon"),
        P("batch", None, "lat", "lon"),
        P("lat", "lon"),
        P("lon"),
        P("batch", None, "lat", "lon"),
        P(),
        P(),
    )
    out_specs = (
        P("batch", None, "lat", "lon"),
        P("batch", None, "lat", "lon"),
        P(("lat", "batch"), None),
        P(("lat", "batch"), None),
    )
    return jax.shard_map(on_device, mesh=mesh, in_specs=in_specs, out_specs=out_specs, check_vma=False)
```
